32 devices in a mesh: sky: 16 (over z, y, x), band: 2 (over core).
Axes of the slice: x: 2, y: 2, z: 4, core: 2. Of those that a mesh axis runs over, the one named last changes fastest.
Arguments:
- stamps: bfloat16 [4096, 6, 2304], P('sky', 'band'), may hold values from 0 to 2
- stamp_gain: bfloat16 [4096], P('sky'), may hold values from 0.5 to 2
- stamp_invvar: bfloat16 [4096], P('sky'), may hold values from 1 to 10
- stamp_dest: int32 [4096, 1], P('sky'), may hold values from 0 to 15; in each aligned block of 256 rows (0 to 255, 256 to 511, ...) at most 32 rows name the same one
- stamp_obj: int32 [4096], P('sky'), may hold values from 0 to 63
- phi_tpl: bfloat16 [6, 16, 2304], P('band'), may hold values from 0 to 0.041503906
- psi_tpl: bfloat16 [6, 16, 2304], P('band'), may hold values from 0 to 0.041503906
- theta_init: float32 [16, 1024], P(None, 'sky'), may hold values from -3 to 3
- nb_id: int32 [1024, 4], P('sky'), may hold values from 0 to 1023, as said below
- nb_weight: float32 [1024, 4], P('sky'), may hold values from 0.2 to 0.8
Outputs:
- theta_fit: float32 [16, 1024], P(None, 'sky')
The draws below stay inside these ranges and needn't reach their ends.
Inputs may be any that keep to these rules, and one draw needn't show every extreme that they name: `stamp_dest`: among the stamps of one index of sky no destination is named more than 32 times, a bound that some block reaches. `nb_id`: each neighbour is owned by the object's own index of sky or by the index just before or after it, cyclically.
All inputs are finite; a program needn't handle non-finite values.
Results may differ from the reference program's by a relative error of at most 0.0007.
Values may be sent and summed in bfloat16 or wider, within the bound.
No kernel may reach another device: no remote copies, remote signals or barrier semaphores. Data moves between devices by JAX's collectives and lax.ppermute only.
A program may use at most 128 MiB of HBM per device.

```python
import math
import jax
import jax.numpy as jnp
import numpy as np
from jax import lax

BANDS = 6
K = 16
NEI = 4
ITERS = 3
STAMP_DEV = 256
OBJ_DEV = 64
PIX = 2304
CAP = 32
STAMPS = 4096
OBJECTS = 1024
N_SKY = 16


def draw_nb_id(key, part):
    first_key, second_key = jax.random.split(jax.random.fold_in(key, 7))
    home = jnp.arange(OBJECTS, dtype=jnp.int32)[:, None] // OBJ_DEV
    offset = jax.random.randint(first_key, (OBJECTS, NEI), -1, 2).astype(jnp.int32)
    local = jax.random.randint(second_key, (OBJECTS, NEI), 0, OBJ_DEV).astype(jnp.int32)
    return (jnp.mod(home + offset, N_SKY) * OBJ_DEV + local).astype(jnp.int32)


def touch_ends(result, own_key, smallest, largest):
    longest = result.shape.index(max(result.shape))
    spots = []
    for shift in (0, 1):
        where = [jax.random.randint(jax.random.fold_in(own_key, axis), (), 0, length) for axis, length in enumerate(result.shape)]
        where[longest] = (where[longest] + shift) % result.shape[longest]
        spots.append(tuple(where))
    return result.at[spots[0]].set(smallest).at[spots[1]].set(largest)


def block_scale(stream_key, shape, cuts, low, top_value):
    level = 1.0
    for dim, shards_of in cuts:
        steps = jax.random.uniform(jax.random.fold_in(jax.random.fold_in(stream_key, 6), dim), (shards_of,), jnp.float32, low / len(cuts), top_value / len(cuts))
        level = level * jnp.repeat(jnp.exp(steps), shape[dim] // shards_of).reshape((-1,) + (1,) * (len(shape) - 1 - dim))
    return level


def shared_out(key, own, number, rows, amount, top, bound, slope):
    order = jax.random.permutation(key, amount)
    packed, common = shares(amount, rows * top, bound, slope, True), shares(amount, rows * top, bound, slope, False)
    places = jnp.arange(amount)

    def named(lengths, rotation):
        used = int((lengths > 0).sum())
        fixed = max(1, used // 4)
        shifted = fixed + (places - fixed + rotation * (used - fixed)) % max(1, amount - fixed)
        return jnp.zeros((amount,), jnp.int32).at[order[jnp.where(places < fixed, places, shifted)]].set(jnp.asarray(lengths, jnp.int32))

    lengths = jnp.where(number % 4 == 0, named(packed, number // 4), named(common, number - number // 4 - 1))
    mixed = jax.random.permutation(jax.random.fold_in(own, 3), amount)
    donor, sink = mixed[0:amount // 2 * 2:2], mixed[1:amount // 2 * 2:2]
    margin = jnp.minimum(lengths[donor] - 1, bound - lengths[sink]) // 2
    margin = jnp.where((donor == order[0]) | (sink == order[0]) | (lengths[sink] == 0), 0, jnp.maximum(margin, 0))
    shifted = jax.random.randint(jax.random.fold_in(own, 4), (amount // 2,), 0, 1 << 20) % (margin + 1)
    lengths = lengths.at[donor].add(-shifted).at[sink].add(shifted)
    labels = jnp.searchsorted(jnp.cumsum(lengths), jnp.arange(rows * top), side="right").astype(jnp.int32)
    listing = labels.reshape(top, rows).T
    listing = listing[jax.random.permutation(jax.random.fold_in(own, 1), rows)]
    rotation = jax.random.randint(jax.random.fold_in(own, 2), (rows, 1), 0, top)
    return jnp.take_along_axis(listing, (jnp.arange(top)[None, :] + rotation) % top, axis=1)


def shares(count, total, most, lean, full):
    weights = [(1 << 20) // math.isqrt(rank ** lean) + 1 for rank in range(1, count + 1)]
    largest = most if full else min(most, max(-(-total // count), total * weights[0] // sum(weights)))
    least = 1 if total - largest >= count - 1 else 0
    given, surplus = [largest] + [least] * (count - 1), total - largest - least * (count - 1)
    while surplus > 0:
        candidates = [i for i in range(1, count) if given[i] < largest] or [i for i in range(1, count) if given[i] < most]
        mass, remaining = sum([weights[i] for i in candidates]), surplus
        for i in candidates:
            addition = min(most - given[i], max(1, remaining * weights[i] // mass), surplus)
            given[i] = given[i] + addition
            surplus = surplus - addition
    return np.array(given)


def normal_values(stream_key, shape, spread, limit, shards=(), kind=jnp.bfloat16):
    loudness = block_scale(stream_key, shape, shards, -0.22, 0.18) if shards else 1.0
    values = jax.random.normal(stream_key, shape, jnp.float32) * spread * loudness
    return jnp.minimum(jnp.maximum(values, -limit), limit).astype(kind)


def setup_inputs(seed: int = 0) -> dict:
    splits = jax.random.split(jax.random.key(seed), 11)
    stamps = jnp.clip(2.0 * jax.random.uniform(splits[0], (STAMPS, BANDS, PIX), jnp.float32) ** block_scale(splits[0], (STAMPS, BANDS, PIX), ((0, 16), (1, 2)), -0.2, 0.2), 0.0, 2.0).astype(jnp.bfloat16)
    stamp_gain = jnp.clip(jnp.exp(math.log(2.0) - 1.3862944 * jax.random.uniform(splits[1], (STAMPS,), jnp.float32) ** block_scale(splits[1], (STAMPS,), ((0, 16),), -0.2, 0.2)), 0.5, 2.0).astype(jnp.bfloat16)
    stamp_invvar = jnp.clip(jnp.exp(math.log(10.0) - 2.3025851 * jax.random.uniform(splits[2], (STAMPS,), jnp.float32) ** block_scale(splits[2], (STAMPS,), ((0, 16),), -0.2, 0.2)), 1.0, 10.0).astype(jnp.bfloat16)
    stamp_dest_keys = jax.random.split(jax.random.fold_in(splits[3], 1), STAMPS // STAMP_DEV)
    stamp_dest_turns = jax.random.permutation(jax.random.fold_in(splits[3], 3), STAMPS // STAMP_DEV)
    stamp_dest = jax.vmap(lambda own, number: shared_out(jax.random.fold_in(splits[3], 2), own, number, STAMP_DEV, N_SKY, 1, CAP, 2))(stamp_dest_keys, stamp_dest_turns).reshape((STAMPS, 1))
    stamp_obj = touch_ends(jax.random.randint(splits[4], (STAMPS,), 0, OBJ_DEV), jax.random.fold_in(splits[4], 1), 0, OBJ_DEV - 1).astype(jnp.int32)
    phi_tpl = jnp.clip(0.041503906 * jax.random.uniform(splits[5], (BANDS, K, PIX), jnp.float32) ** block_scale(splits[5], (BANDS, K, PIX), ((0, 2),), -0.2, 0.2), 0.0, 0.041503906).astype(jnp.bfloat16)
    psi_tpl = jnp.clip(0.041503906 * jax.random.uniform(splits[6], (BANDS, K, PIX), jnp.float32) ** block_scale(splits[6], (BANDS, K, PIX), ((0, 2),), -0.2, 0.2), 0.0, 0.041503906).astype(jnp.bfloat16)
    theta_init = normal_values(splits[7], (K, OBJECTS), 0.5, 3.0, ((1, 16),), jnp.float32)
    nb_id = draw_nb_id(jax.random.fold_in(splits[10], 71), 0)
    nb_weight = jnp.clip(0.2 + 0.6 * jax.random.uniform(splits[9], (OBJECTS, NEI), jnp.float32) ** block_scale(splits[9], (OBJECTS, NEI), ((0, 16),), -0.2, 0.2), 0.2, 0.8)
    return dict(stamps=stamps, stamp_gain=stamp_gain, stamp_invvar=stamp_invvar, stamp_dest=stamp_dest, stamp_obj=stamp_obj, phi_tpl=phi_tpl, psi_tpl=psi_tpl, theta_init=theta_init, nb_id=nb_id, nb_weight=nb_weight)


ROBUST = 9.0
DAMPING = 0.1
PRIOR = 1.0
STEP_LIMIT = 0.5


def batch_solve(matrix, target):
    size_k = matrix.shape[0]
    for pivot_row in range(size_k):
        pivot_value = matrix[pivot_row, pivot_row]
        scaled = matrix[pivot_row] / pivot_value[None, :]
        solved = target[pivot_row] / pivot_value
        factors = matrix[:, pivot_row].at[pivot_row].set(0.0)
        matrix = matrix - factors[:, None, :] * scaled[None, :, :]
        matrix = matrix.at[pivot_row].set(scaled)
        target = target - factors * solved[None, :]
        target = target.at[pivot_row].set(solved)
    return target


def reference(stamps, stamp_gain, stamp_invvar, stamp_dest, stamp_obj, phi_tpl, psi_tpl, theta_init, nb_id, nb_weight):
    owner = (stamp_dest[:, 0] * OBJ_DEV + stamp_obj).astype(jnp.int32)
    phi_wide = phi_tpl.astype(jnp.float32)
    psi_wide = psi_tpl.astype(jnp.float32)
    pair = (phi_wide[:, :, None, :] * phi_wide[:, None, :, :]).astype(jnp.bfloat16)
    pair_wide = pair.reshape(BANDS, K * K, PIX).astype(jnp.float32)
    blocks = STAMPS // STAMP_DEV
    stamp_blocks = stamps.reshape(blocks, STAMP_DEV, BANDS, PIX)
    gain_blocks = stamp_gain.reshape(blocks, STAMP_DEV)
    invvar_blocks = stamp_invvar.reshape(blocks, STAMP_DEV)
    owner_blocks = owner.reshape(blocks, STAMP_DEV)
    theta = theta_init
    for sweep in range(ITERS):
        amp = jnp.exp(theta)
        near = jnp.zeros_like(amp)
        for slot_j in range(NEI):
            near = near + nb_weight[:, slot_j][None, :] * jnp.take(amp, nb_id[:, slot_j], axis=1)

        def one_block(carry, inputs):
            normal_acc, grad_acc = carry
            pixels, gains, invvars, owners = inputs
            gain = gains.astype(jnp.float32)
            invvar = invvars.astype(jnp.float32)
            slot_f = jnp.take(amp, owners, axis=1).T
            slot_u = jnp.take(near, owners, axis=1).T
            lit = (gain[:, None] * slot_f).astype(jnp.bfloat16).astype(jnp.float32)
            nearlit = slot_u.astype(jnp.bfloat16).astype(jnp.float32)
            model = jnp.einsum('nk,bkp->nbp', lit, phi_wide) + jnp.einsum('nk,bkp->nbp', nearlit, psi_wide)
            resid = pixels.astype(jnp.float32) - model
            inv_b = invvar[:, None, None]
            weight = inv_b / (1.0 + inv_b * resid * resid / ROBUST)
            weight_low = weight.astype(jnp.bfloat16).astype(jnp.float32)
            wres = (weight * resid).astype(jnp.bfloat16).astype(jnp.float32)
            gram = jnp.einsum('nbp,bmp->nm', weight_low, pair_wide)
            proj = jnp.einsum('nbp,bkp->nk', wres, phi_wide)
            outer = (slot_f[:, :, None] * slot_f[:, None, :]).reshape(slot_f.shape[0], K * K)
            a_rows = (gain * gain)[:, None] * outer * gram
            r_rows = gain[:, None] * slot_f * proj
            normal_acc = normal_acc + jax.ops.segment_sum(a_rows, owners, num_segments=OBJECTS)
            grad_acc = grad_acc + jax.ops.segment_sum(r_rows, owners, num_segments=OBJECTS)
            return (normal_acc, grad_acc), None

        start = (jnp.zeros((OBJECTS, K * K), jnp.float32), jnp.zeros((OBJECTS, K), jnp.float32))
        (normal, grad), unused = lax.scan(one_block, start, (stamp_blocks, gain_blocks, invvar_blocks, owner_blocks))
        matrix = jnp.transpose(normal.reshape(OBJECTS, K, K), (1, 2, 0))
        eye_k = jnp.eye(K, dtype=jnp.float32)[:, :, None]
        matrix = matrix + DAMPING * (matrix * eye_k) + PRIOR * eye_k
        target = grad.T - PRIOR * (theta - theta_init)
        delta = batch_solve(matrix, target)
        theta = theta + STEP_LIMIT * jnp.tanh(delta / STEP_LIMIT)
    return theta
```

```python
import functools

import jax
import jax.numpy as jnp
import numpy as np
from jax import lax
from jax.experimental import pallas as pl
from jax.experimental.pallas import tpu as pltpu
from jax.sharding import PartitionSpec as P

ITERS = 3

ROBUST = 9.0
DAMPING = 0.1
PRIOR = 1.0
STEP_LIMIT = 0.5

LANES = 128
GROUP = 32
VMEM_LIMIT = 32 * 1024 * 1024

f32 = jnp.float32
bf16 = jnp.bfloat16
NT = (((1,), (1,)), ((), ()))
TN = (((0,), (0,)), ((), ()))
NN = (((1,), (0,)), ((), ()))


def dot(a, b, dims=NN, precision=None):
    return lax.dot_general(a, b, dims, precision=precision, preferred_element_type=f32)


def split3(x):
    first = x.astype(bf16)
    rest = x - first.astype(f32)
    second = rest.astype(bf16)
    third = (rest - second.astype(f32)).astype(bf16)
    return first, second, third


def iota(shape, dim):
    return lax.broadcasted_iota(jnp.int32, shape, dim)


@functools.lru_cache
def tables(size_k):
    pairs = [(k, l) for k in range(size_k) for l in range(k, size_k)]
    extra = len(pairs) - LANES
    assert 0 <= extra and extra + size_k <= GROUP
    left = np.zeros((size_k, 2 * LANES), np.float32)
    right = np.zeros((size_k, 2 * LANES), np.float32)
    grad = np.zeros((size_k, 2 * LANES), np.float32)
    full = np.zeros((size_k * size_k + size_k, 2 * LANES), np.float32)
    for m, (k, l) in enumerate(pairs):
        left[k, m] = 1.0
        right[l, m] = 1.0
        spots = [m] if m < LANES else [m + GROUP * g for g in range(LANES // GROUP)]
        full[k * size_k + l, spots] = 1.0
        full[l * size_k + k, spots] = 1.0
    for k in range(size_k):
        spot = LANES + extra + k
        grad[k, spot] = 1.0
        full[size_k * size_k + k, [spot + GROUP * g for g in range(LANES // GROUP)]] = 1.0
    return left, right, grad, full


def first_kernel(sizes, small_ref, theta_ref, nbi_ref, nbw_ref, pay_ref, sel_ref, inv_ref):
    n_sky, cap, obj_dev = sizes
    stamps = small_ref.shape[1]
    total = n_sky * cap
    dest = small_ref[0:1, :]
    obj = small_ref[1:2, :]
    along = jnp.broadcast_to(dest, (stamps, stamps))
    down = along.T
    before = iota((stamps, stamps), 0) < iota((stamps, stamps), 1)
    rank = jnp.sum(jnp.where(before & (along == down), 1.0, 0.0), axis=0, keepdims=True)
    place = dest.astype(jnp.int32) * cap + rank.astype(jnp.int32)
    sel = jnp.where(iota((total, stamps), 0) == place, 1.0, 0.0)
    sel_ref[...] = sel.astype(bf16)
    inv_ref[...] = jnp.broadcast_to(small_ref[3:4, :], (LANES, stamps)).T
    named = dot(jnp.broadcast_to(obj + 1.0, (8, stamps)), sel, NT, lax.Precision.HIGHEST)
    slot = iota((n_sky, total), 1)
    own = iota((n_sky, total), 0)
    spread = jnp.where((slot >= own * cap) & (slot < own * cap + cap), named[0:1, :], 0.0)
    turn = jnp.where(
        lax.rem(iota((total, LANES), 0), cap) == iota((total, LANES), 1), 1.0, 0.0
    )
    ids = dot(spread, turn, precision=lax.Precision.HIGHEST)
    size_k = theta_ref.shape[0]
    half = size_k // 2
    lane = iota((8, LANES), 1)
    row = iota((8, LANES), 0)
    theta = theta_ref[...]
    folded = jnp.concatenate([theta[:half], theta[half:]], axis=1)
    side = jnp.concatenate([nbi_ref[...].astype(f32), nbw_ref[...]], axis=1)
    side = jnp.concatenate([side, jnp.zeros((8 - side.shape[0], LANES), f32)], axis=0)
    del lane
    for d in range(n_sky):
        pay_ref[d, 0:8, :] = folded
        pay_ref[d, 8:16, :] = jnp.where(row == nbi_ref.shape[0], ids[d : d + 1, :], side)


def pair_kernel(phi_ref, psi_ref, left_ref, right_ref, grad_ref, tpl_ref, pair_ref, prow_ref):
    bands, size_k, pix = phi_ref.shape
    chunk = 256

    def step(c, carry):
        px = pl.ds(pl.multiple_of(c * chunk, chunk), chunk)
        for b in range(bands):
            phi = phi_ref[b, :, px]
            tpl_ref[b, 0:size_k, px] = phi
            tpl_ref[b, size_k : 2 * size_k, px] = psi_ref[b, :, px]
            pair_ref[b, :, px] = (dot(left_ref[...], phi) * dot(right_ref[...], phi)).astype(bf16)
            prow_ref[b, :, px] = dot(grad_ref[...], phi).astype(bf16)
        return carry

    lax.fori_loop(0, pix // chunk, step, 0)


def unfold(ref, rows, lane, i, left):
    x, y = ref[2 * i, rows, :], ref[2 * i + 1, rows, :]
    if left:
        return jnp.where(lane < LANES // 2, x, pltpu.roll(y, LANES // 2, 1))
    return jnp.where(lane < LANES // 2, pltpu.roll(x, LANES // 2, 1), y)


def index_kernel(sizes, got_ref, small_ref, pick_ref, member_ref, theta_ref, table_ref, hot_ref):
    n_sky, cap, obj_dev, nei = sizes
    stamps = small_ref.shape[1]
    total = n_sky * cap
    n_all = n_sky * obj_dev
    lane = iota((8, LANES), 1)
    for d in range(n_sky):
        theta_ref[d] = got_ref[d, 0:8, :]
    for i in range(n_sky // 2):
        span = slice(i * LANES, (i + 1) * LANES)
        table_ref[0:8, span] = unfold(got_ref, slice(8, 16), lane, i, True)
        table_ref[8:16, span] = unfold(got_ref, slice(8, 16), lane, i, False)
    owner = (small_ref[0:1, :] * obj_dev + small_ref[1:2, :]).astype(jnp.int32)
    block = 2 * obj_dev

    def hot(i, carry):
        rows = pl.ds(pl.multiple_of(i * block, block), block)
        hit = iota((block, stamps), 0) + i * block == owner
        hot_ref[rows, :] = jnp.where(hit, 1.0, 0.0).astype(bf16)
        return carry

    lax.fori_loop(0, n_all // block, hot, 0)
    parts = jnp.concatenate(split3(table_ref[...]), axis=0)
    found = dot(parts, hot_ref[...])
    found = found[0:16] + found[16:32] + found[32:48]
    near_id = found[0:nei].astype(jnp.int32)
    near_w = found[8 : 8 + nei]

    def blend(i, carry):
        rows = pl.ds(pl.multiple_of(i * block, block), block)
        here = iota((block, stamps), 0) + i * block
        mix = jnp.zeros((block, stamps), f32)
        for j in range(nei):
            mix = mix + jnp.where(here == near_id[j : j + 1], near_w[j : j + 1], 0.0)
        high = mix.astype(bf16)
        pick_ref[rows, 0:stamps] = hot_ref[rows, :]
        pick_ref[rows, stamps : 2 * stamps] = high
        pick_ref[rows, 2 * stamps : 3 * stamps] = (mix - high.astype(f32)).astype(bf16)
        return carry

    lax.fori_loop(0, n_all // block, blend, 0)
    ids = got_ref[:, 8 + nei, :]
    turn = jnp.where(
        iota((LANES, total), 0) == lax.rem(iota((LANES, total), 1), cap), 1.0, 0.0
    )
    spread = dot(ids, turn, precision=lax.Precision.HIGHEST)
    slot = iota((n_sky, total), 1)
    own = iota((n_sky, total), 0)
    mine = (slot >= own * cap) & (slot < own * cap + cap)
    row = jnp.sum(jnp.where(mine, spread, 0.0), axis=0, keepdims=True).astype(jnp.int32)
    member_ref[...] = jnp.where(iota((obj_dev, total), 0) + 1 == row, 1.0, 0.0).astype(bf16)


def terms_kernel(
    sizes,
    theta_ref,
    pick_ref,
    small_ref,
    inv_ref,
    pix_ref,
    tpl_ref,
    pair_ref,
    prow_ref,
    sel_ref,
    wide_ref,
    out_ref,
    amp_ref,
    acc_ref,
    lit_ref,
):
    n_sky, cap, fold, chunk, extra = sizes
    bands, stamps, pix = pix_ref.shape
    size_k = tpl_ref.shape[1] // 2
    lane = iota((8, LANES), 1)
    for i in range(n_sky // 2):
        span = slice(i * LANES, (i + 1) * LANES)
        amp_ref[0:8, span] = jnp.exp(unfold(theta_ref, slice(None), lane, i, True))
        amp_ref[8:16, span] = jnp.exp(unfold(theta_ref, slice(None), lane, i, False))
    parts = jnp.concatenate(split3(amp_ref[...]), axis=0)
    got = dot(parts, pick_ref[...])
    k1, k2, k3 = slice(0, size_k), slice(size_k, 2 * size_k), slice(2 * size_k, 3 * size_k)
    s1, s2, s3 = slice(0, stamps), slice(stamps, 2 * stamps), slice(2 * stamps, 3 * stamps)
    slot_f = got[k1, s1] + (got[k2, s1] + got[k3, s1])
    slot_u = got[k1, s2] + (got[k2, s2] + got[k1, s3] + (got[k3, s2] + got[k2, s3]))
    scaled = small_ref[2:3, :] * slot_f
    lit_ref[...] = jnp.concatenate([scaled, slot_u], axis=0).T.astype(bf16)
    acc_ref[...] = jnp.zeros_like(acc_ref)
    inv = jnp.concatenate([inv_ref[...]] * (chunk // LANES), axis=1)
    slope = inv * (1.0 / ROBUST)
    wide = pair_ref.shape[1]

    for b in range(bands):

        def step(c, carry):
            px = pl.ds(pl.multiple_of(c * chunk, chunk), chunk)
            model = dot(lit_ref[...], tpl_ref[b, :, px])
            resid = pix_ref[b, :, px].astype(f32) - model
            under = 1.0 + slope * (resid * resid)
            guess = pl.reciprocal(under, approx=True)
            weight = inv * (guess * (2.0 - under * guess))
            low = weight.astype(bf16)
            wres = (weight * resid).astype(bf16)
            acc_ref[:, 0:wide] += dot(low, pair_ref[b, :, px], NT)
            acc_ref[:, LANES : LANES + GROUP] += dot(wres, prow_ref[b, :, px], NT)
            return carry

        lax.fori_loop(0, pix // chunk, step, 0)

    scales = dot(jnp.concatenate(split3(scaled), axis=0), wide_ref[...], TN)
    col = iota((1, 2 * LANES), 1) - (LANES + extra)
    is_grad = jnp.where((col >= 0) & (col < size_k), 1.0, 0.0)
    terms = scales[:, : 2 * LANES] * (scales[:, 2 * LANES :] + is_grad) * acc_ref[...]
    t1, t2, t3 = split3(terms)
    sel = sel_ref[...]
    rows = dot(sel, t1) + (dot(sel, t2) + dot(sel, t3))
    per = cap // fold
    for d in range(n_sky):
        base = d * cap
        out_ref[d, 0:cap, :] = rows[base : base + cap, :LANES]
        tail = rows[base : base + per, LANES:]
        for g in range(1, fold):
            at = base + g * per
            tail = tail + pltpu.roll(rows[at : at + per, LANES:], g * GROUP, 1)
        out_ref[d, cap : cap + per, :] = tail


def solve_kernel(
    sizes,
    recv_ref,
    other_ref,
    member_ref,
    full_ref,
    theta_ref,
    init_ref,
    pay_ref,
    new_ref,
    rows_ref,
):
    n_sky, cap, fold = sizes
    per = cap // fold
    size_k, obj_dev = theta_ref.shape
    group = iota((per, LANES), 1) // GROUP
    for d in range(n_sky):
        both = recv_ref[d] + other_ref[d]
        rows_ref[d * cap : d * cap + cap, 0:LANES] = both[0:cap]
        tail = both[cap : cap + per]
        for g in range(fold):
            at = d * cap + g * per
            rows_ref[at : at + per, LANES:] = jnp.where(group == g, tail, 0.0)
    p1, p2, p3 = split3(rows_ref[...])
    member = member_ref[...]
    sums = dot(member, p1) + (dot(member, p2) + dot(member, p3))
    q1, q2, q3 = split3(sums)
    full = full_ref[...]
    wide = dot(full, q1, NT) + (dot(full, q2, NT) + dot(full, q3, NT))
    row = iota((size_k, obj_dev), 0)
    theta = theta_ref[...]
    target = wide[size_k * size_k :] - PRIOR * (theta - init_ref[...])
    matrix = []
    for k in range(size_k):
        line = wide[k * size_k : (k + 1) * size_k]
        matrix.append(jnp.where(row == k, line + (DAMPING * line + PRIOR), line))
    inverse = []
    for p in range(size_k):
        line = matrix[p]
        inv = 1.0 / line[p : p + 1]
        inverse.append(inv)
        if p + 1 < size_k:
            scaled = jnp.where(row > p, line * inv, 0.0)
            target = target - scaled * target[p : p + 1]
            for k in range(p + 1, size_k):
                matrix[k] = matrix[k] - scaled * line[k : k + 1]
    delta = jnp.zeros_like(target)
    for p in reversed(range(size_k)):
        value = target[p : p + 1] * inverse[p]
        delta = jnp.where(row == p, value, delta)
        if p:
            target = target - matrix[p] * value
    new = theta + STEP_LIMIT * jnp.tanh(delta / STEP_LIMIT)
    new_ref[...] = new
    half = size_k // 2
    folded = jnp.concatenate([new[:half], new[half:]], axis=1)
    for d in range(n_sky):
        pay_ref[d] = folded


def call(kernel, out_shape, scratch=()):
    return pl.pallas_call(
        kernel,
        out_shape=out_shape,
        scratch_shapes=list(scratch),
        compiler_params=pltpu.CompilerParams(vmem_limit_bytes=VMEM_LIMIT),
    )


def local(
    stamps,
    stamp_gain,
    stamp_invvar,
    stamp_dest,
    stamp_obj,
    phi_tpl,
    psi_tpl,
    theta_init,
    nb_id,
    nb_weight,
):
    n_sky = lax.axis_size("sky")
    n_band = lax.axis_size("band")
    stamp_dev, bands, pix = stamps.shape
    size_k, obj_dev = theta_init.shape
    nei = nb_id.shape[1]
    cap = 2 * stamp_dev // n_sky
    fold = max(1, min(LANES // GROUP, cap // 8))
    total = n_sky * cap
    n_all = n_sky * obj_dev
    rows = cap + cap // fold
    left, right, grad, full = tables(size_k)
    extra = size_k * (size_k + 1) // 2 - LANES
    wide = LANES + GROUP
    shape = jax.ShapeDtypeStruct

    pixels = jnp.transpose(stamps, (1, 0, 2))
    small = jnp.stack(
        [
            stamp_dest[:, 0].astype(f32),
            stamp_obj.astype(f32),
            stamp_gain.astype(f32),
            stamp_invvar.astype(f32),
        ]
    )
    payload, sel, inv = call(
        functools.partial(first_kernel, (n_sky, cap, obj_dev)),
        (
            shape((n_sky, 16, LANES), f32),
            shape((total, stamp_dev), bf16),
            shape((stamp_dev, LANES), f32),
        ),
    )(small, theta_init, nb_id.T, nb_weight.T)
    got = lax.all_to_all(payload, "sky", 0, 0, tiled=True)
    tpl, pair, prow = call(
        pair_kernel,
        (
            shape((bands, 2 * size_k, pix), bf16),
            shape((bands, wide, pix), bf16),
            shape((bands, GROUP, pix), bf16),
        ),
    )(
        phi_tpl,
        psi_tpl,
        jnp.asarray(left.T[:wide], bf16),
        jnp.asarray(right.T[:wide], bf16),
        jnp.asarray(grad.T[LANES:wide], bf16),
    )
    pick, member, everyone = call(
        functools.partial(index_kernel, (n_sky, cap, obj_dev, nei)),
        (
            shape((n_all, 3 * stamp_dev), bf16),
            shape((obj_dev, total), bf16),
            shape((n_sky, 8, LANES), f32),
        ),
        [pltpu.VMEM((16, n_all), f32), pltpu.VMEM((n_all, stamp_dev), bf16)],
    )(got, small)
    spread = np.concatenate([np.concatenate([left + grad, right], axis=1)] * 3, axis=0)
    terms = call(
        functools.partial(terms_kernel, (n_sky, cap, fold, 256, extra)),
        shape((n_sky, rows, LANES), f32),
        [
            pltpu.VMEM((size_k, n_all), f32),
            pltpu.VMEM((stamp_dev, 2 * LANES), f32),
            pltpu.VMEM((stamp_dev, 2 * size_k), bf16),
        ],
    )
    solve = call(
        functools.partial(solve_kernel, (n_sky, cap, fold)),
        (shape((n_sky, 8, LANES), f32), shape((size_k, obj_dev), f32)),
        [pltpu.VMEM((total, 2 * LANES), f32)],
    )
    spread = jnp.asarray(spread, bf16)
    full = jnp.asarray(full, bf16)
    theta = theta_init
    for sweep in range(ITERS):
        sent = terms(everyone, pick, small, inv, pixels, tpl, pair, prow, sel, spread)
        recv = lax.all_to_all(sent, "sky", 0, 0, tiled=True)
        if n_band == 2:
            other = lax.ppermute(recv, "band", [(0, 1), (1, 0)])
        else:
            other = lax.psum(recv, "band") - recv
        payload, theta = solve(recv, other, member, full, theta, theta_init)
        if sweep + 1 < ITERS:
            everyone = lax.all_to_all(payload, "sky", 0, 0, tiled=True)
    return theta


def solution(mesh):
    in_specs = (
        P("sky", "band", None),
        P("sky"),
        P("sky"),
        P("sky", None),
        P("sky"),
        P("band", None, None),
        P("band", None, None),
        P(None, "sky"),
        P("sky", None),
        P("sky", None),
    )
    out_specs = P(None, "sky")
    return jax.shard_map(local, mesh=mesh, in_specs=in_specs, out_specs=out_specs, check_vma=False)
```

```python
import functools

import jax
import jax.numpy as jnp
from jax import lax
from jax.experimental import pallas as pl
from jax.experimental.pallas import tpu as pltpu
from jax.sharding import PartitionSpec as P

ITERS = 3

ROBUST = 9.0
DAMPING = 0.1
PRIOR = 1.0
STEP_LIMIT = 0.5

LANES = 128
GROUP = 32
VMEM_LIMIT = 24 * 1024 * 1024

f32 = jnp.float32
bf16 = jnp.bfloat16
NT = (((1,), (1,)), ((), ()))
TN = (((0,), (0,)), ((), ()))
NN = (((1,), (0,)), ((), ()))


def dot(a, b, dims=NN, precision=None):
    return lax.dot_general(a, b, dims, precision=precision, preferred_element_type=f32)


def split3(x):
    first = x.astype(bf16)
    rest = x - first.astype(f32)
    second = rest.astype(bf16)
    third = (rest - second.astype(f32)).astype(bf16)
    return first, second, third


def iota(shape, dim):
    return lax.broadcasted_iota(jnp.int32, shape, dim)


def dma(copies):
    for copy in copies:
        copy.start()
    return copies


def wait(copies):
    for copy in copies:
        copy.wait()


def offset(k, size_k):
    return lax.div(k * (2 * size_k + 1 - k), 2)


def column(shape, m):
    lane = iota(shape, 1)
    folded = jnp.where(lane < LANES, lane, LANES + lax.rem(lane, GROUP))
    return folded == m


def pack_kernel(theta_hbm, nbi_hbm, nbw_hbm, pay_ref, theta_ref, nbi_ref, nbw_ref, sem):
    n_sky = pay_ref.shape[0]
    wait(
        dma(
            [
                pltpu.make_async_copy(theta_hbm, theta_ref, sem.at[0]),
                pltpu.make_async_copy(nbi_hbm, nbi_ref, sem.at[1]),
                pltpu.make_async_copy(nbw_hbm, nbw_ref, sem.at[2]),
            ]
        )
    )
    half = theta_ref.shape[0] // 2
    theta = theta_ref[...]
    folded = jnp.concatenate([theta[:half], theta[half:]], axis=1)
    side = jnp.concatenate([nbi_ref[...].astype(f32), nbw_ref[...]], axis=1)
    side = jnp.concatenate([side, jnp.zeros((8 - side.shape[0], LANES), f32)], axis=0)
    for d in range(n_sky):
        pay_ref[d, 0:8, :] = folded
        pay_ref[d, 8:16, :] = side


def ready_kernel(
    sizes,
    dest_hbm,
    obj_hbm,
    gain_hbm,
    invvar_hbm,
    phi_hbm,
    psi_hbm,
    tpl_ref,
    pair_ref,
    sel_ref,
    wide_ref,
    full_ref,
    base_ref,
    tag_ref,
    gain_ref,
    owner_ref,
    dest_ref,
    obj_ref,
    gain_low_ref,
    invvar_ref,
    sem,
):
    n_sky, cap, obj_dev, extra = sizes
    bands, size_k, pix = phi_hbm.shape
    stamps = dest_ref.shape[1]
    total = n_sky * cap
    first = [
        pltpu.make_async_copy(phi_hbm, tpl_ref.at[:, 0:size_k, :], sem.at[0]),
        pltpu.make_async_copy(psi_hbm, tpl_ref.at[:, size_k : 2 * size_k, :], sem.at[1]),
        pltpu.make_async_copy(dest_hbm, dest_ref, sem.at[2]),
        pltpu.make_async_copy(obj_hbm, obj_ref, sem.at[3]),
        pltpu.make_async_copy(gain_hbm, gain_low_ref, sem.at[4]),
        pltpu.make_async_copy(invvar_hbm, invvar_ref, sem.at[5]),
    ]
    dma(first)

    pairs = LANES + extra
    shape = (pair_ref.shape[1], size_k)
    m = iota(shape, 0)
    k = iota(shape, 1)
    lows = jnp.where((m >= offset(k, size_k)) & (m < offset(k + 1, size_k)), 1.0, 0.0)
    of_m = jnp.sum(lows * k.astype(f32), axis=1, keepdims=True).astype(jnp.int32)
    highs = jnp.where((m < pairs) & (m - offset(of_m, size_k) + of_m == k), 1.0, 0.0)
    lows, highs = lows.astype(bf16), highs.astype(bf16)

    shape = (size_k, 2 * LANES)
    k = iota(shape, 0)
    lane = iota(shape, 1)
    spot = pairs + k
    left = (lane >= offset(k, size_k)) & (lane < offset(k + 1, size_k))
    left = jnp.where(left | (lane == spot), 1.0, 0.0)
    lane_k = jnp.sum(jnp.where(lane >= offset(k + 1, size_k), 1, 0), axis=0, keepdims=True)
    right = (lane[0:1] - offset(lane_k, size_k) + lane_k == k) & (lane < pairs)
    both = jnp.concatenate([left, jnp.where(right, 1.0, 0.0)], axis=1).astype(bf16)
    for part in range(3):
        wide_ref[part * size_k : (part + 1) * size_k, :] = both

    shape = full_ref.shape
    r = iota((shape[0], 1), 0)
    a, b = lax.div(r, size_k), lax.rem(r, size_k)
    low, high = jnp.minimum(a, b), jnp.maximum(a, b)
    m = jnp.where(r < size_k * size_k, offset(low, size_k) + high - low, pairs + b)
    full_ref[...] = jnp.where(column(shape, m), 1.0, 0.0).astype(bf16)

    wait(first)
    dest = dest_ref[...]
    obj = obj_ref[...]
    gain_ref[...] = jnp.broadcast_to(gain_low_ref[...].astype(f32), gain_ref.shape)
    base_ref[...] = jnp.broadcast_to(1.0 / invvar_ref[...].astype(f32), (LANES, stamps)).T
    named = jnp.broadcast_to((obj + 1).astype(f32), (LANES, stamps)).T
    tag_ref[...] = jnp.where(
        iota((stamps, LANES), 1) == extra + size_k, named, 0.0
    )
    along = jnp.broadcast_to(dest.astype(f32), (stamps, stamps))
    before = iota((stamps, stamps), 0) < iota((stamps, stamps), 1)
    rank = jnp.sum(jnp.where(before & (along == along.T), 1.0, 0.0), axis=0, keepdims=True)
    owner_ref[...] = jnp.broadcast_to(dest * obj_dev + obj, owner_ref.shape)
    place = dest * cap + rank.astype(jnp.int32)
    sel_ref[...] = jnp.where(iota((total, stamps), 0) == place, 1.0, 0.0).astype(bf16)
    chunk = 256

    def step(c, carry):
        px = pl.ds(pl.multiple_of(c * chunk, chunk), chunk)
        for b in range(bands):
            phi = tpl_ref[b, 0:size_k, px]
            pair_ref[b, :, px] = (dot(lows, phi) * dot(highs, phi)).astype(bf16)
        return carry

    lax.fori_loop(0, pix // chunk, step, 0)


def unfold(ref, rows, lane, i, left):
    x, y = ref[2 * i, rows, :], ref[2 * i + 1, rows, :]
    if left:
        return jnp.where(lane < LANES // 2, x, pltpu.roll(y, LANES // 2, 1))
    return jnp.where(lane < LANES // 2, pltpu.roll(x, LANES // 2, 1), y)


def index_kernel(nei, got_ref, owner_ref, theta_ref, hot_ref, blend_ref, table_ref):
    n_sky = got_ref.shape[0]
    n_all, stamps = hot_ref.shape
    block = LANES
    owner = owner_ref[0:1, :]

    def hot(i, carry):
        rows = pl.ds(pl.multiple_of(i * block, block), block)
        hit = iota((block, stamps), 0) + i * block == owner
        hot_ref[rows, :] = jnp.where(hit, 1.0, 0.0).astype(bf16)
        return carry

    lax.fori_loop(0, n_all // block, hot, 0)
    lane = iota((8, LANES), 1)
    for d in range(n_sky):
        theta_ref[d] = got_ref[d, 0:8, :]
    for i in range(n_sky // 2):
        span = slice(i * LANES, (i + 1) * LANES)
        table_ref[0:8, span] = unfold(got_ref, slice(8, 16), lane, i, True)
        table_ref[8:16, span] = unfold(got_ref, slice(8, 16), lane, i, False)
    parts = jnp.concatenate(split3(table_ref[...]), axis=0)
    found = dot(parts, hot_ref[...])
    found = found[0:16] + found[16:32] + found[32:48]
    near_id = found[0:nei].astype(jnp.int32)
    near_w = found[8 : 8 + nei]

    def blend(i, carry):
        rows = pl.ds(pl.multiple_of(i * block, block), block)
        here = iota((block, stamps), 0) + i * block
        mix = jnp.zeros((block, stamps), f32)
        for j in range(nei):
            mix = mix + jnp.where(here == near_id[j : j + 1], near_w[j : j + 1], 0.0)
        high = mix.astype(bf16)
        blend_ref[rows, 0:stamps] = high
        blend_ref[rows, stamps : 2 * stamps] = (mix - high.astype(f32)).astype(bf16)
        return carry

    lax.fori_loop(0, n_all // block, blend, 0)


def terms_kernel(
    sizes,
    theta_ref,
    hot_ref,
    blend_ref,
    gain_ref,
    base_ref,
    tag_ref,
    pix_hbm,
    tpl_ref,
    pair_ref,
    sel_ref,
    wide_ref,
    out_ref,
    amp_ref,
    acc_ref,
    proj_ref,
    lit_ref,
    pix_ref,
    sem,
):
    n_sky, cap, fold, chunk, extra = sizes
    bands, stamps, pix = pix_ref.shape
    size_k = tpl_ref.shape[1] // 2
    steps = [
        (b, slice(c * chunk, (c + 1) * chunk)) for b in range(bands) for c in range(pix // chunk)
    ]
    loads = dma(
        [
            pltpu.make_async_copy(pix_hbm.at[b, :, px], pix_ref.at[b, :, px], sem.at[i])
            for i, (b, px) in enumerate(steps)
        ]
    )
    lane = iota((8, LANES), 1)
    for i in range(n_sky // 2):
        span = slice(i * LANES, (i + 1) * LANES)
        amp_ref[0:8, span] = jnp.exp(unfold(theta_ref, slice(None), lane, i, True))
        amp_ref[8:16, span] = jnp.exp(unfold(theta_ref, slice(None), lane, i, False))
    parts = jnp.concatenate(split3(amp_ref[...]), axis=0)
    got = dot(parts, hot_ref[...])
    mix = dot(parts, blend_ref[...])
    k1, k2, k3 = slice(0, size_k), slice(size_k, 2 * size_k), slice(2 * size_k, 3 * size_k)
    slot_f = got[k1] + (got[k2] + got[k3])
    high, low = mix[:, :stamps], mix[:, stamps:]
    slot_u = high[k1] + (high[k2] + low[k1] + (high[k3] + low[k2]))
    scaled = gain_ref[0:1, :] * slot_f
    lit_ref[...] = jnp.concatenate([scaled, slot_u], axis=0).T.astype(bf16)
    acc_ref[...] = jnp.zeros_like(acc_ref)
    proj_ref[...] = jnp.zeros_like(proj_ref)
    lit = lit_ref[...]
    base = jnp.concatenate([base_ref[...]] * (chunk // LANES), axis=1)
    wide = pair_ref.shape[1]

    def model(b, px):
        return dot(lit, tpl_ref[b, :, px])

    def weigh(b, px, light):
        resid = pix_ref[b, :, px].astype(f32) - light
        under = base + (resid * resid) * (1.0 / ROBUST)
        guess = pltpu.reciprocal(under, approx=True)
        weight = guess * (2.0 - under * guess)
        return weight.astype(bf16), (weight * resid).astype(bf16)

    def gather(b, px, weight, wres):
        acc_ref[:, 0:wide] += dot(weight, pair_ref[b, :, px], NT)
        proj_ref[:, 0:size_k] += dot(wres, tpl_ref[b, 0:size_k, px], NT)

    light = model(*steps[0])
    held = None
    for i, here in enumerate(steps):
        ahead = model(*steps[i + 1]) if i + 1 < len(steps) else None
        loads[i].wait()
        now = weigh(*here, light)
        if held is not None:
            gather(*steps[i - 1], *held)
        light, held = ahead, now
    gather(*steps[-1], *held)

    scales = dot(jnp.concatenate(split3(scaled), axis=0), wide_ref[...], TN)
    col = iota((1, 2 * LANES), 1) - (LANES + extra)
    is_grad = jnp.where((col >= 0) & (col < size_k), 1.0, 0.0)
    factor = scales[:, : 2 * LANES] * (scales[:, 2 * LANES :] + is_grad)
    tail = acc_ref[:, LANES:] + pltpu.roll(proj_ref[...], extra, 1)
    terms = jnp.concatenate(
        [
            factor[:, :LANES] * acc_ref[:, :LANES],
            factor[:, LANES:] * tail + tag_ref[...],
        ],
        axis=1,
    )
    t1, t2, t3 = split3(terms)
    sel = sel_ref[...]
    rows = dot(sel, t1) + (dot(sel, t2) + dot(sel, t3))
    per = cap // fold
    for d in range(n_sky):
        base_row = d * cap
        out_ref[d, 0:cap, :] = rows[base_row : base_row + cap, :LANES]
        tail = rows[base_row : base_row + per, LANES:]
        for g in range(1, fold):
            at = base_row + g * per
            tail = tail + pltpu.roll(rows[at : at + per, LANES:], g * GROUP, 1)
        out_ref[d, cap : cap + per, :] = tail


def solve_kernel(
    sizes,
    recv_ref,
    other_ref,
    member_in_ref,
    full_ref,
    theta_ref,
    init_ref,
    pay_ref,
    new_ref,
    member_ref,
    rows_ref,
):
    n_sky, cap, fold, n_band, tag, learn = sizes
    per = cap // fold
    size_k, obj_dev = theta_ref.shape
    total = n_sky * cap
    group = iota((per, LANES), 1) // GROUP
    for d in range(n_sky):
        both = recv_ref[d] + other_ref[d]
        rows_ref[d * cap : d * cap + cap, 0:LANES] = both[0:cap]
        tail = both[cap : cap + per]
        for g in range(fold):
            at = d * cap + g * per
            rows_ref[at : at + per, LANES:] = jnp.where(group == g, tail, 0.0)
    p1, p2, p3 = split3(rows_ref[...])
    if learn:
        where_tag = jnp.where(column((8, 2 * LANES), LANES + tag), 1.0, 0.0).astype(bf16)
        ids = dot(where_tag, p1, NT) + (dot(where_tag, p2, NT) + dot(where_tag, p3, NT))
        named = (iota((obj_dev, total), 0) + 1) * n_band
        hit = named == ids[0:1, :].astype(jnp.int32)
        member_ref[...] = jnp.where(hit, 1.0, 0.0).astype(bf16)
        member = member_ref[...]
    else:
        member = member_in_ref[...]
    sums = dot(member, p1) + (dot(member, p2) + dot(member, p3))
    q1, q2, q3 = split3(sums)
    full = full_ref[...]
    wide = dot(full, q1, NT) + (dot(full, q2, NT) + dot(full, q3, NT))
    row = iota((size_k, obj_dev), 0)
    theta = theta_ref[...]
    target = wide[size_k * size_k :] - PRIOR * (theta - init_ref[...])
    matrix = []
    for k in range(size_k):
        line = wide[k * size_k : (k + 1) * size_k]
        matrix.append(jnp.where(row == k, line + (DAMPING * line + PRIOR), line))
    inverse = []
    for p in range(size_k):
        line = matrix[p]
        inv = 1.0 / line[p : p + 1]
        inverse.append(inv)
        if p + 1 < size_k:
            scaled = jnp.where(row > p, line * inv, 0.0)
            target = target - scaled * target[p : p + 1]
            for k in range(p + 1, size_k):
                matrix[k] = matrix[k] - scaled * line[k : k + 1]
    delta = jnp.zeros_like(target)
    for p in reversed(range(size_k)):
        value = target[p : p + 1] * inverse[p]
        delta = jnp.where(row == p, value, delta)
        if p:
            target = target - matrix[p] * value
    new = theta + STEP_LIMIT * jnp.tanh(delta / STEP_LIMIT)
    new_ref[...] = new
    if pay_ref is not None:
        half = size_k // 2
        folded = jnp.concatenate([new[:half], new[half:]], axis=1)
        for d in range(n_sky):
            pay_ref[d] = folded


def hbm(x):
    return pltpu.with_memory_space_constraint(x, pltpu.HBM)


def call(kernel, out_shape, scratch=(), spaces=None):
    specs = {}
    if spaces:
        specs["in_specs"] = [
            pl.BlockSpec(memory_space=pltpu.HBM if s == "h" else pltpu.VMEM) for s in spaces
        ]
    return pl.pallas_call(
        kernel,
        out_shape=out_shape,
        scratch_shapes=list(scratch),
        compiler_params=pltpu.CompilerParams(vmem_limit_bytes=VMEM_LIMIT),
        **specs,
    )


def local(
    stamps,
    stamp_gain,
    stamp_invvar,
    stamp_dest,
    stamp_obj,
    phi_tpl,
    psi_tpl,
    theta_init,
    nb_id,
    nb_weight,
):
    n_sky = lax.axis_size("sky")
    n_band = lax.axis_size("band")
    stamp_dev, bands, pix = stamps.shape
    size_k, obj_dev = theta_init.shape
    nei = nb_id.shape[1]
    cap = 2 * stamp_dev // n_sky
    fold = max(1, min(LANES // GROUP, cap // 8))
    total = n_sky * cap
    n_all = n_sky * obj_dev
    rows = cap + cap // fold
    extra = size_k * (size_k + 1) // 2 - LANES
    wide = LANES + -(-extra // 16) * 16
    assert n_band == 2 and 2 * obj_dev == LANES and 0 <= extra and extra + size_k < GROUP
    shape = jax.ShapeDtypeStruct
    chunk = max(c for c in range(LANES, 1024, LANES) if pix % c == 0)

    pixels = jnp.transpose(stamps, (1, 0, 2))
    payload = call(
        pack_kernel,
        shape((n_sky, 16, LANES), f32),
        [
            pltpu.VMEM((size_k, obj_dev), f32),
            pltpu.VMEM((nei, obj_dev), jnp.int32),
            pltpu.VMEM((nei, obj_dev), f32),
            pltpu.SemaphoreType.DMA((3,)),
        ],
        "hhh",
    )(hbm(theta_init), hbm(nb_id.T), hbm(nb_weight.T))
    got = lax.all_to_all(payload, "sky", 0, 0, tiled=True)
    tpl, pair, sel, spread, full, base, tag, gain, owner = call(
        functools.partial(ready_kernel, (n_sky, cap, obj_dev, extra)),
        (
            shape((bands, 2 * size_k, pix), bf16),
            shape((bands, wide, pix), bf16),
            shape((total, stamp_dev), bf16),
            shape((3 * size_k, 4 * LANES), bf16),
            shape((size_k * size_k + size_k, 2 * LANES), bf16),
            shape((stamp_dev, LANES), f32),
            shape((stamp_dev, LANES), f32),
            shape((8, stamp_dev), f32),
            shape((8, stamp_dev), jnp.int32),
        ),
        [
            pltpu.VMEM((1, stamp_dev), jnp.int32),
            pltpu.VMEM((1, stamp_dev), jnp.int32),
            pltpu.VMEM((1, stamp_dev), bf16),
            pltpu.VMEM((1, stamp_dev), bf16),
            pltpu.SemaphoreType.DMA((6,)),
        ],
        "hhhhhh",
    )(
        hbm(stamp_dest.T),
        hbm(stamp_obj[None, :]),
        hbm(stamp_gain[None, :]),
        hbm(stamp_invvar[None, :]),
        hbm(phi_tpl),
        hbm(psi_tpl),
    )
    everyone, hot, blend = call(
        functools.partial(index_kernel, nei),
        (
            shape((n_sky, 8, LANES), f32),
            shape((n_all, stamp_dev), bf16),
            shape((n_all, 2 * stamp_dev), bf16),
        ),
        [pltpu.VMEM((16, n_all), f32)],
    )(got, owner)
    terms = call(
        functools.partial(terms_kernel, (n_sky, cap, fold, chunk, extra)),
        shape((n_sky, rows, LANES), f32),
        [
            pltpu.VMEM((size_k, n_all), f32),
            pltpu.VMEM((stamp_dev, 2 * LANES), f32),
            pltpu.VMEM((stamp_dev, LANES), f32),
            pltpu.VMEM((stamp_dev, 2 * size_k), bf16),
            pltpu.VMEM((bands, stamp_dev, pix), bf16),
            pltpu.SemaphoreType.DMA((bands * (pix // chunk),)),
        ],
        "vvvvvvhvvvv",
    )
    theta = theta_init
    member = None
    for sweep in range(ITERS):
        sent = terms(
            everyone, hot, blend, gain, base, tag, hbm(pixels), tpl, pair, sel, spread
        )
        recv = lax.all_to_all(sent, "sky", 0, 0, tiled=True)
        other = lax.ppermute(recv, "band", [(0, 1), (1, 0)])
        learn, last = sweep == 0, sweep + 1 == ITERS
        sizes = (n_sky, cap, fold, n_band, extra + size_k, learn)

        def solve(*refs, learn=learn, last=last, sizes=sizes):
            refs = list(refs)
            if learn:
                refs.insert(2, None)
            if last:
                refs.insert(6, None)
            if not learn:
                refs.insert(8, None)
            solve_kernel(sizes, *refs)

        outs = [shape((n_sky, 8, LANES), f32)] * (not last)
        outs += [shape((size_k, obj_dev), f32)]
        outs += [shape((obj_dev, total), bf16)] * learn
        given = [recv, other] + [member] * (not learn) + [full, theta, theta_init]
        outs = call(solve, outs, [pltpu.VMEM((total, 2 * LANES), f32)])(*given)
        theta = outs[0 if last else 1]
        if learn:
            member = outs[-1]
        if not last:
            everyone = lax.all_to_all(outs[0], "sky", 0, 0, tiled=True)
    return theta


def solution(mesh):
    in_specs = (
        P("sky", "band", None),
        P("sky"),
        P("sky"),
        P("sky", None),
        P("sky"),
        P("band", None, None),
        P("band", None, None),
        P(None, "sky"),
        P("sky", None),
        P("sky", None),
    )
    out_specs = P(None, "sky")
    return jax.shard_map(local, mesh=mesh, in_specs=in_specs, out_specs=out_specs, check_vma=False)
```

```python
import functools

import jax
import jax.numpy as jnp
from jax import lax
from jax.experimental import pallas as pl
from jax.experimental.pallas import tpu as pltpu
from jax.sharding import PartitionSpec as P

ITERS = 3

ROBUST = 9.0
DAMPING = 0.1
PRIOR = 1.0
STEP_LIMIT = 0.5

LANES = 128
GROUP = 32
VMEM_LIMIT = 24 * 1024 * 1024

f32 = jnp.float32
bf16 = jnp.bfloat16
NT = (((1,), (1,)), ((), ()))
TN = (((0,), (0,)), ((), ()))
NN = (((1,), (0,)), ((), ()))


def dot(a, b, dims=NN, precision=None):
    return lax.dot_general(a, b, dims, precision=precision, preferred_element_type=f32)


def split3(x):
    first = x.astype(bf16)
    rest = x - first.astype(f32)
    second = rest.astype(bf16)
    third = (rest - second.astype(f32)).astype(bf16)
    return first, second, third


def iota(shape, dim):
    return lax.broadcasted_iota(jnp.int32, shape, dim)


def dma(copies):
    for copy in copies:
        copy.start()
    return copies


def wait(copies):
    for copy in copies:
        copy.wait()


def offset(k, size_k):
    return lax.div(k * (2 * size_k + 1 - k), 2)


def column(shape, m):
    lane = iota(shape, 1)
    folded = jnp.where(lane < LANES, lane, LANES + lax.rem(lane, GROUP))
    return folded == m


def pack_kernel(theta_hbm, nbi_hbm, nbw_hbm, pay_ref, theta_ref, nbi_ref, nbw_ref, sem):
    n_sky = pay_ref.shape[0]
    wait(
        dma(
            [
                pltpu.make_async_copy(theta_hbm, theta_ref, sem.at[0]),
                pltpu.make_async_copy(nbi_hbm, nbi_ref, sem.at[1]),
                pltpu.make_async_copy(nbw_hbm, nbw_ref, sem.at[2]),
            ]
        )
    )
    half = theta_ref.shape[0] // 2
    theta = theta_ref[...]
    folded = jnp.concatenate([theta[:half], theta[half:]], axis=1)
    side = jnp.concatenate([nbi_ref[...].astype(f32), nbw_ref[...]], axis=1)
    side = jnp.concatenate([side, jnp.zeros((8 - side.shape[0], LANES), f32)], axis=0)
    for d in range(n_sky):
        pay_ref[d, 0:8, :] = folded
        pay_ref[d, 8:16, :] = side


def ready_kernel(
    sizes,
    dest_hbm,
    obj_hbm,
    gain_hbm,
    invvar_hbm,
    phi_hbm,
    psi_hbm,
    tpl_ref,
    pair_ref,
    sel_ref,
    wide_ref,
    full_ref,
    base_ref,
    tag_ref,
    gain_ref,
    owner_ref,
    dest_ref,
    obj_ref,
    gain_low_ref,
    invvar_ref,
    sem,
):
    n_sky, cap, obj_dev, extra = sizes
    bands, size_k, pix = phi_hbm.shape
    stamps = dest_ref.shape[1]
    total = n_sky * cap
    first = [
        pltpu.make_async_copy(phi_hbm, tpl_ref.at[:, 0:size_k, :], sem.at[0]),
        pltpu.make_async_copy(psi_hbm, tpl_ref.at[:, size_k : 2 * size_k, :], sem.at[1]),
        pltpu.make_async_copy(dest_hbm, dest_ref, sem.at[2]),
        pltpu.make_async_copy(obj_hbm, obj_ref, sem.at[3]),
        pltpu.make_async_copy(gain_hbm, gain_low_ref, sem.at[4]),
        pltpu.make_async_copy(invvar_hbm, invvar_ref, sem.at[5]),
    ]
    dma(first)

    pairs = LANES + extra
    shape = (pair_ref.shape[1], size_k)
    m = iota(shape, 0)
    k = iota(shape, 1)
    lows = jnp.where((m >= offset(k, size_k)) & (m < offset(k + 1, size_k)), 1.0, 0.0)
    of_m = jnp.sum(lows * k.astype(f32), axis=1, keepdims=True).astype(jnp.int32)
    highs = jnp.where((m < pairs) & (m - offset(of_m, size_k) + of_m == k), 1.0, 0.0)
    lows, highs = lows.astype(bf16), highs.astype(bf16)

    shape = (size_k, 2 * LANES)
    k = iota(shape, 0)
    lane = iota(shape, 1)
    spot = pairs + k
    left = (lane >= offset(k, size_k)) & (lane < offset(k + 1, size_k))
    left = jnp.where(left | (lane == spot), 1.0, 0.0)
    lane_k = jnp.sum(jnp.where(lane >= offset(k + 1, size_k), 1, 0), axis=0, keepdims=True)
    right = (lane[0:1] - offset(lane_k, size_k) + lane_k == k) & (lane < pairs)
    both = jnp.concatenate([left, jnp.where(right, 1.0, 0.0)], axis=1).astype(bf16)
    for part in range(3):
        wide_ref[part * size_k : (part + 1) * size_k, :] = both

    shape = full_ref.shape
    r = iota((shape[0], 1), 0)
    a, b = lax.div(r, size_k), lax.rem(r, size_k)
    low, high = jnp.minimum(a, b), jnp.maximum(a, b)
    m = jnp.where(r < size_k * size_k, offset(low, size_k) + high - low, pairs + b)
    full_ref[...] = jnp.where(column(shape, m), 1.0, 0.0).astype(bf16)

    wait(first)
    dest = dest_ref[...]
    obj = obj_ref[...]
    gain_ref[...] = jnp.broadcast_to(gain_low_ref[...].astype(f32), gain_ref.shape)
    base_ref[...] = jnp.broadcast_to(1.0 / invvar_ref[...].astype(f32), (LANES, stamps)).T
    named = jnp.broadcast_to((obj + 1).astype(f32), (LANES, stamps)).T
    tag_ref[...] = jnp.where(
        iota((stamps, LANES), 1) == extra + size_k, named, 0.0
    )
    along = jnp.broadcast_to(dest.astype(f32), (stamps, stamps))
    before = iota((stamps, stamps), 0) < iota((stamps, stamps), 1)
    rank = jnp.sum(jnp.where(before & (along == along.T), 1.0, 0.0), axis=0, keepdims=True)
    owner_ref[...] = jnp.broadcast_to(dest * obj_dev + obj, owner_ref.shape)
    place = dest * cap + rank.astype(jnp.int32)
    sel_ref[...] = jnp.where(iota((total, stamps), 0) == place, 1.0, 0.0).astype(bf16)
    chunk = 256

    def step(c, carry):
        px = pl.ds(pl.multiple_of(c * chunk, chunk), chunk)
        for b in range(bands):
            phi = tpl_ref[b, 0:size_k, px]
            pair_ref[b, :, px] = (dot(lows, phi) * dot(highs, phi)).astype(bf16)
        return carry

    lax.fori_loop(0, pix // chunk, step, 0)


def unfold(ref, rows, lane, i, left):
    x, y = ref[2 * i, rows, :], ref[2 * i + 1, rows, :]
    if left:
        return jnp.where(lane < LANES // 2, x, pltpu.roll(y, LANES // 2, 1))
    return jnp.where(lane < LANES // 2, pltpu.roll(x, LANES // 2, 1), y)


def index_kernel(
    nei, got_ref, owner_ref, pix_hbm, theta_ref, hot_ref, blend_ref, pix_ref, table_ref, sem
):
    load = dma([pltpu.make_async_copy(pix_hbm, pix_ref, sem)])
    n_sky = got_ref.shape[0]
    n_all, stamps = hot_ref.shape
    block = LANES
    owner = owner_ref[0:1, :]

    def hot(i, carry):
        rows = pl.ds(pl.multiple_of(i * block, block), block)
        hit = iota((block, stamps), 0) + i * block == owner
        hot_ref[rows, :] = jnp.where(hit, 1.0, 0.0).astype(bf16)
        return carry

    lax.fori_loop(0, n_all // block, hot, 0)
    lane = iota((8, LANES), 1)
    for d in range(n_sky):
        theta_ref[d] = got_ref[d, 0:8, :]
    for i in range(n_sky // 2):
        span = slice(i * LANES, (i + 1) * LANES)
        table_ref[0:8, span] = unfold(got_ref, slice(8, 16), lane, i, True)
        table_ref[8:16, span] = unfold(got_ref, slice(8, 16), lane, i, False)
    parts = jnp.concatenate(split3(table_ref[...]), axis=0)
    found = dot(parts, hot_ref[...])
    found = found[0:16] + found[16:32] + found[32:48]
    near_id = found[0:nei].astype(jnp.int32)
    near_w = found[8 : 8 + nei]

    def blend(i, carry):
        rows = pl.ds(pl.multiple_of(i * block, block), block)
        here = iota((block, stamps), 0) + i * block
        mix = jnp.zeros((block, stamps), f32)
        for j in range(nei):
            mix = mix + jnp.where(here == near_id[j : j + 1], near_w[j : j + 1], 0.0)
        high = mix.astype(bf16)
        blend_ref[rows, 0:stamps] = high
        blend_ref[rows, stamps : 2 * stamps] = (mix - high.astype(f32)).astype(bf16)
        return carry

    lax.fori_loop(0, n_all // block, blend, 0)
    wait(load)


def terms_kernel(
    sizes,
    theta_ref,
    hot_ref,
    blend_ref,
    gain_ref,
    base_ref,
    tag_ref,
    pix_ref,
    tpl_ref,
    pair_ref,
    sel_ref,
    wide_ref,
    out_ref,
    amp_ref,
    acc_ref,
    proj_ref,
    lit_ref,
):
    n_sky, cap, fold, chunk, extra = sizes
    bands, stamps, pix = pix_ref.shape
    size_k = tpl_ref.shape[1] // 2
    steps = [
        (b, slice(c * chunk, (c + 1) * chunk)) for b in range(bands) for c in range(pix // chunk)
    ]
    lane = iota((8, LANES), 1)
    for i in range(n_sky // 2):
        span = slice(i * LANES, (i + 1) * LANES)
        amp_ref[0:8, span] = jnp.exp(unfold(theta_ref, slice(None), lane, i, True))
        amp_ref[8:16, span] = jnp.exp(unfold(theta_ref, slice(None), lane, i, False))
    parts = jnp.concatenate(split3(amp_ref[...]), axis=0)
    got = dot(parts, hot_ref[...])
    mix = dot(parts, blend_ref[...])
    k1, k2, k3 = slice(0, size_k), slice(size_k, 2 * size_k), slice(2 * size_k, 3 * size_k)
    slot_f = got[k1] + (got[k2] + got[k3])
    high, low = mix[:, :stamps], mix[:, stamps:]
    slot_u = high[k1] + (high[k2] + low[k1] + (high[k3] + low[k2]))
    scaled = gain_ref[0:1, :] * slot_f
    lit_ref[...] = jnp.concatenate([scaled, slot_u], axis=0).T.astype(bf16)
    acc_ref[...] = jnp.zeros_like(acc_ref)
    proj_ref[...] = jnp.zeros_like(proj_ref)
    lit = lit_ref[...]
    base = jnp.concatenate([base_ref[...]] * (chunk // LANES), axis=1)
    wide = pair_ref.shape[1]

    def model(b, px):
        return dot(lit, tpl_ref[b, :, px])

    def weigh(b, px, light):
        resid = pix_ref[b, :, px].astype(f32) - light
        under = base + (resid * resid) * (1.0 / ROBUST)
        guess = pltpu.reciprocal(under, approx=True)
        weight = guess * (2.0 - under * guess)
        return weight.astype(bf16), (weight * resid).astype(bf16)

    def gather(b, px, weight, wres):
        acc_ref[:, 0:wide] += dot(weight, pair_ref[b, :, px], NT)
        proj_ref[:, 0:size_k] += dot(wres, tpl_ref[b, 0:size_k, px], NT)

    light = model(*steps[0])
    held = None
    for i, here in enumerate(steps):
        ahead = model(*steps[i + 1]) if i + 1 < len(steps) else None
        now = weigh(*here, light)
        if held is not None:
            gather(*steps[i - 1], *held)
        light, held = ahead, now
    gather(*steps[-1], *held)

    scales = dot(jnp.concatenate(split3(scaled), axis=0), wide_ref[...], TN)
    col = iota((1, 2 * LANES), 1) - (LANES + extra)
    is_grad = jnp.where((col >= 0) & (col < size_k), 1.0, 0.0)
    factor = scales[:, : 2 * LANES] * (scales[:, 2 * LANES :] + is_grad)
    tail = acc_ref[:, LANES:] + pltpu.roll(proj_ref[...], extra, 1)
    terms = jnp.concatenate(
        [
            factor[:, :LANES] * acc_ref[:, :LANES],
            factor[:, LANES:] * tail + tag_ref[...],
        ],
        axis=1,
    )
    t1, t2, t3 = split3(terms)
    sel = sel_ref[...]
    rows = dot(sel, t1) + (dot(sel, t2) + dot(sel, t3))
    per = cap // fold
    for d in range(n_sky):
        base_row = d * cap
        out_ref[d, 0:cap, :] = rows[base_row : base_row + cap, :LANES]
        tail = rows[base_row : base_row + per, LANES:]
        for g in range(1, fold):
            at = base_row + g * per
            tail = tail + pltpu.roll(rows[at : at + per, LANES:], g * GROUP, 1)
        out_ref[d, cap : cap + per, :] = tail


def solve_kernel(
    sizes,
    recv_ref,
    other_ref,
    member_in_ref,
    full_ref,
    theta_ref,
    init_ref,
    pay_ref,
    new_ref,
    member_ref,
    rows_ref,
):
    n_sky, cap, fold, n_band, tag, learn = sizes
    per = cap // fold
    size_k, obj_dev = theta_ref.shape
    total = n_sky * cap
    group = iota((per, LANES), 1) // GROUP
    for d in range(n_sky):
        both = recv_ref[d] + other_ref[d]
        rows_ref[d * cap : d * cap + cap, 0:LANES] = both[0:cap]
        tail = both[cap : cap + per]
        for g in range(fold):
            at = d * cap + g * per
            rows_ref[at : at + per, LANES:] = jnp.where(group == g, tail, 0.0)
    p1, p2, p3 = split3(rows_ref[...])
    if learn:
        where_tag = jnp.where(column((8, 2 * LANES), LANES + tag), 1.0, 0.0).astype(bf16)
        ids = dot(where_tag, p1, NT) + (dot(where_tag, p2, NT) + dot(where_tag, p3, NT))
        named = (iota((obj_dev, total), 0) + 1) * n_band
        hit = named == ids[0:1, :].astype(jnp.int32)
        member_ref[...] = jnp.where(hit, 1.0, 0.0).astype(bf16)
        member = member_ref[...]
    else:
        member = member_in_ref[...]
    sums = dot(member, p1) + (dot(member, p2) + dot(member, p3))
    q1, q2, q3 = split3(sums)
    full = full_ref[...]
    wide = dot(full, q1, NT) + (dot(full, q2, NT) + dot(full, q3, NT))
    row = iota((size_k, obj_dev), 0)
    theta = theta_ref[...]
    target = wide[size_k * size_k :] - PRIOR * (theta - init_ref[...])
    matrix = []
    for k in range(size_k):
        line = wide[k * size_k : (k + 1) * size_k]
        matrix.append(jnp.where(row == k, line + (DAMPING * line + PRIOR), line))
    inverse = []
    for p in range(size_k):
        line = matrix[p]
        inv = 1.0 / line[p : p + 1]
        inverse.append(inv)
        if p + 1 < size_k:
            scaled = jnp.where(row > p, line * inv, 0.0)
            target = target - scaled * target[p : p + 1]
            for k in range(p + 1, size_k):
                matrix[k] = matrix[k] - scaled * line[k : k + 1]
    delta = jnp.zeros_like(target)
    for p in reversed(range(size_k)):
        value = target[p : p + 1] * inverse[p]
        delta = jnp.where(row == p, value, delta)
        if p:
            target = target - matrix[p] * value
    new = theta + STEP_LIMIT * jnp.tanh(delta / STEP_LIMIT)
    new_ref[...] = new
    if pay_ref is not None:
        half = size_k // 2
        folded = jnp.concatenate([new[:half], new[half:]], axis=1)
        for d in range(n_sky):
            pay_ref[d] = folded


def hbm(x):
    return pltpu.with_memory_space_constraint(x, pltpu.HBM)


def call(kernel, out_shape, scratch=(), spaces=None):
    specs = {}
    if spaces:
        specs["in_specs"] = [
            pl.BlockSpec(memory_space=pltpu.HBM if s == "h" else pltpu.VMEM) for s in spaces
        ]
    return pl.pallas_call(
        kernel,
        out_shape=out_shape,
        scratch_shapes=list(scratch),
        compiler_params=pltpu.CompilerParams(vmem_limit_bytes=VMEM_LIMIT),
        **specs,
    )


def local(
    stamps,
    stamp_gain,
    stamp_invvar,
    stamp_dest,
    stamp_obj,
    phi_tpl,
    psi_tpl,
    theta_init,
    nb_id,
    nb_weight,
):
    n_sky = lax.axis_size("sky")
    n_band = lax.axis_size("band")
    stamp_dev, bands, pix = stamps.shape
    size_k, obj_dev = theta_init.shape
    nei = nb_id.shape[1]
    cap = 2 * stamp_dev // n_sky
    fold = max(1, min(LANES // GROUP, cap // 8))
    total = n_sky * cap
    n_all = n_sky * obj_dev
    rows = cap + cap // fold
    extra = size_k * (size_k + 1) // 2 - LANES
    wide = LANES + -(-extra // 16) * 16
    assert n_band == 2 and 2 * obj_dev == LANES and 0 <= extra and extra + size_k < GROUP
    shape = jax.ShapeDtypeStruct
    chunk = max(c for c in range(LANES, 1024, LANES) if pix % c == 0)

    pixels = jnp.transpose(stamps, (1, 0, 2))
    payload = call(
        pack_kernel,
        shape((n_sky, 16, LANES), f32),
        [
            pltpu.VMEM((size_k, obj_dev), f32),
            pltpu.VMEM((nei, obj_dev), jnp.int32),
            pltpu.VMEM((nei, obj_dev), f32),
            pltpu.SemaphoreType.DMA((3,)),
        ],
        "hhh",
    )(hbm(theta_init), hbm(nb_id.T), hbm(nb_weight.T))
    got = lax.all_to_all(payload, "sky", 0, 0, tiled=True)
    tpl, pair, sel, spread, full, base, tag, gain, owner = call(
        functools.partial(ready_kernel, (n_sky, cap, obj_dev, extra)),
        (
            shape((bands, 2 * size_k, pix), bf16),
            shape((bands, wide, pix), bf16),
            shape((total, stamp_dev), bf16),
            shape((3 * size_k, 4 * LANES), bf16),
            shape((size_k * size_k + size_k, 2 * LANES), bf16),
            shape((stamp_dev, LANES), f32),
            shape((stamp_dev, LANES), f32),
            shape((8, stamp_dev), f32),
            shape((8, stamp_dev), jnp.int32),
        ),
        [
            pltpu.VMEM((1, stamp_dev), jnp.int32),
            pltpu.VMEM((1, stamp_dev), jnp.int32),
            pltpu.VMEM((1, stamp_dev), bf16),
            pltpu.VMEM((1, stamp_dev), bf16),
            pltpu.SemaphoreType.DMA((6,)),
        ],
        "hhhhhh",
    )(
        hbm(stamp_dest.T),
        hbm(stamp_obj[None, :]),
        hbm(stamp_gain[None, :]),
        hbm(stamp_invvar[None, :]),
        hbm(phi_tpl),
        hbm(psi_tpl),
    )
    everyone, hot, blend, pixels = call(
        functools.partial(index_kernel, nei),
        (
            shape((n_sky, 8, LANES), f32),
            shape((n_all, stamp_dev), bf16),
            shape((n_all, 2 * stamp_dev), bf16),
            shape((bands, stamp_dev, pix), bf16),
        ),
        [pltpu.VMEM((16, n_all), f32), pltpu.SemaphoreType.DMA(())],
        "vvh",
    )(got, owner, hbm(pixels))
    terms = call(
        functools.partial(terms_kernel, (n_sky, cap, fold, chunk, extra)),
        shape((n_sky, rows, LANES), f32),
        [
            pltpu.VMEM((size_k, n_all), f32),
            pltpu.VMEM((stamp_dev, 2 * LANES), f32),
            pltpu.VMEM((stamp_dev, LANES), f32),
            pltpu.VMEM((stamp_dev, 2 * size_k), bf16),
        ],
    )
    theta = theta_init
    member = None
    for sweep in range(ITERS):
        sent = terms(
            everyone, hot, blend, gain, base, tag, pixels, tpl, pair, sel, spread
        )
        recv = lax.all_to_all(sent, "sky", 0, 0, tiled=True)
        other = lax.ppermute(recv, "band", [(0, 1), (1, 0)])
        learn, last = sweep == 0, sweep + 1 == ITERS
        sizes = (n_sky, cap, fold, n_band, extra + size_k, learn)

        def solve(*refs, learn=learn, last=last, sizes=sizes):
            refs = list(refs)
            if learn:
                refs.insert(2, None)
            if last:
                refs.insert(6, None)
            if not learn:
                refs.insert(8, None)
            solve_kernel(sizes, *refs)

        outs = [shape((n_sky, 8, LANES), f32)] * (not last)
        outs += [shape((size_k, obj_dev), f32)]
        outs += [shape((obj_dev, total), bf16)] * learn
        given = [recv, other] + [member] * (not learn) + [full, theta, theta_init]
        outs = call(solve, outs, [pltpu.VMEM((total, 2 * LANES), f32)])(*given)
        theta = outs[0 if last else 1]
        if learn:
            member = outs[-1]
        if not last:
            everyone = lax.all_to_all(outs[0], "sky", 0, 0, tiled=True)
    return theta


def solution(mesh):
    in_specs = (
        P("sky", "band", None),
        P("sky"),
        P("sky"),
        P("sky", None),
        P("sky"),
        P("band", None, None),
        P("band", None, None),
        P(None, "sky"),
        P("sky", None),
        P("sky", None),
    )
    out_specs = P(None, "sky")
    return jax.shard_map(local, mesh=mesh, in_specs=in_specs, out_specs=out_specs, check_vma=False)
```

```python
import functools

import jax
import jax.numpy as jnp
from jax import lax
from jax.experimental import pallas as pl
from jax.experimental.pallas import tpu as pltpu
from jax.sharding import PartitionSpec as P

ITERS = 3

ROBUST = 9.0
DAMPING = 0.1
PRIOR = 1.0
STEP_LIMIT = 0.5

LANES = 128
GROUP = 32
VMEM_LIMIT = 24 * 1024 * 1024

f32 = jnp.float32
bf16 = jnp.bfloat16
NT = (((1,), (1,)), ((), ()))
TN = (((0,), (0,)), ((), ()))
NN = (((1,), (0,)), ((), ()))


def dot(a, b, dims=NN, precision=None):
    return lax.dot_general(a, b, dims, precision=precision, preferred_element_type=f32)


def split3(x):
    first = x.astype(bf16)
    rest = x - first.astype(f32)
    second = rest.astype(bf16)
    third = (rest - second.astype(f32)).astype(bf16)
    return first, second, third


def iota(shape, dim):
    return lax.broadcasted_iota(jnp.int32, shape, dim)


def dma(copies):
    for copy in copies:
        copy.start()
    return copies


def wait(copies):
    for copy in copies:
        copy.wait()


def offset(k, size_k):
    return lax.div(k * (2 * size_k + 1 - k), 2)


def column(shape, m):
    lane = iota(shape, 1)
    folded = jnp.where(lane < LANES, lane, LANES + lax.rem(lane, GROUP))
    return folded == m


def pack_kernel(theta_hbm, nbi_hbm, nbw_hbm, pay_ref, theta_ref, nbi_ref, nbw_ref, sem):
    n_sky = pay_ref.shape[0]
    wait(
        dma(
            [
                pltpu.make_async_copy(theta_hbm, theta_ref, sem.at[0]),
                pltpu.make_async_copy(nbi_hbm, nbi_ref, sem.at[1]),
                pltpu.make_async_copy(nbw_hbm, nbw_ref, sem.at[2]),
            ]
        )
    )
    half = theta_ref.shape[0] // 2
    theta = theta_ref[...]
    folded = jnp.concatenate([theta[:half], theta[half:]], axis=1)
    side = jnp.concatenate([nbi_ref[...].astype(f32), nbw_ref[...]], axis=1)
    side = jnp.concatenate([side, jnp.zeros((8 - side.shape[0], LANES), f32)], axis=0)
    for d in range(n_sky):
        pay_ref[d, 0:8, :] = folded
        pay_ref[d, 8:16, :] = side


def ready_kernel(
    sizes,
    dest_hbm,
    obj_hbm,
    gain_hbm,
    invvar_hbm,
    phi_hbm,
    psi_hbm,
    tpl_ref,
    pair_ref,
    sel_ref,
    wide_ref,
    full_ref,
    base_ref,
    tag_ref,
    gain_ref,
    owner_ref,
    dest_ref,
    obj_ref,
    gain_low_ref,
    invvar_ref,
    sem,
):
    n_sky, cap, obj_dev, extra = sizes
    bands, size_k, pix = phi_hbm.shape
    stamps = dest_ref.shape[1]
    total = n_sky * cap
    first = [
        pltpu.make_async_copy(phi_hbm, tpl_ref.at[:, 0:size_k, :], sem.at[0]),
        pltpu.make_async_copy(psi_hbm, tpl_ref.at[:, size_k : 2 * size_k, :], sem.at[1]),
        pltpu.make_async_copy(dest_hbm, dest_ref, sem.at[2]),
        pltpu.make_async_copy(obj_hbm, obj_ref, sem.at[3]),
        pltpu.make_async_copy(gain_hbm, gain_low_ref, sem.at[4]),
        pltpu.make_async_copy(invvar_hbm, invvar_ref, sem.at[5]),
    ]
    dma(first)

    pairs = LANES + extra
    shape = (pair_ref.shape[1], size_k)
    m = iota(shape, 0)
    k = iota(shape, 1)
    lows = jnp.where((m >= offset(k, size_k)) & (m < offset(k + 1, size_k)), 1.0, 0.0)
    of_m = jnp.sum(lows * k.astype(f32), axis=1, keepdims=True).astype(jnp.int32)
    highs = jnp.where((m < pairs) & (m - offset(of_m, size_k) + of_m == k), 1.0, 0.0)
    lows, highs = lows.astype(bf16), highs.astype(bf16)

    shape = (size_k, 2 * LANES)
    k = iota(shape, 0)
    lane = iota(shape, 1)
    spot = pairs + k
    left = (lane >= offset(k, size_k)) & (lane < offset(k + 1, size_k))
    left = jnp.where(left | (lane == spot), 1.0, 0.0)
    lane_k = jnp.sum(jnp.where(lane >= offset(k + 1, size_k), 1, 0), axis=0, keepdims=True)
    right = (lane[0:1] - offset(lane_k, size_k) + lane_k == k) & (lane < pairs)
    both = jnp.concatenate([left, jnp.where(right, 1.0, 0.0)], axis=1).astype(bf16)
    for part in range(3):
        wide_ref[part * size_k : (part + 1) * size_k, :] = both

    shape = full_ref.shape
    r = iota((shape[0], 1), 0)
    a, b = lax.div(r, size_k), lax.rem(r, size_k)
    low, high = jnp.minimum(a, b), jnp.maximum(a, b)
    m = jnp.where(r < size_k * size_k, offset(low, size_k) + high - low, pairs + b)
    full_ref[...] = jnp.where(column(shape, m), 1.0, 0.0).astype(bf16)

    wait(first)
    dest = dest_ref[...]
    obj = obj_ref[...]
    gain = gain_low_ref[...].astype(f32).reshape(1, stamps)
    gain_ref[...] = jnp.broadcast_to(gain, gain_ref.shape)
    variance = 1.0 / invvar_ref[...].astype(f32).reshape(1, stamps)
    base_ref[...] = jnp.broadcast_to(variance, (LANES, stamps)).T
    named = jnp.broadcast_to((obj + 1).astype(f32), (LANES, stamps)).T
    tag_ref[...] = jnp.where(
        iota((stamps, LANES), 1) == extra + size_k, named, 0.0
    )
    along = jnp.broadcast_to(dest.astype(f32), (stamps, stamps))
    before = iota((stamps, stamps), 0) < iota((stamps, stamps), 1)
    rank = jnp.sum(jnp.where(before & (along == along.T), 1.0, 0.0), axis=0, keepdims=True)
    owner_ref[...] = jnp.broadcast_to(dest * obj_dev + obj, owner_ref.shape)
    place = dest * cap + rank.astype(jnp.int32)
    sel_ref[...] = jnp.where(iota((total, stamps), 0) == place, 1.0, 0.0).astype(bf16)
    chunk = 256

    def step(c, carry):
        px = pl.ds(pl.multiple_of(c * chunk, chunk), chunk)
        for b in range(bands):
            phi = tpl_ref[b, 0:size_k, px]
            pair_ref[b, :, px] = (dot(lows, phi) * dot(highs, phi)).astype(bf16)
        return carry

    lax.fori_loop(0, pix // chunk, step, 0)


def unfold(ref, rows, lane, i, left):
    x, y = ref[2 * i, rows, :], ref[2 * i + 1, rows, :]
    if left:
        return jnp.where(lane < LANES // 2, x, pltpu.roll(y, LANES // 2, 1))
    return jnp.where(lane < LANES // 2, pltpu.roll(x, LANES // 2, 1), y)


def index_kernel(
    nei, got_ref, owner_ref, pix_hbm, theta_ref, hot_ref, blend_ref, pix_ref, table_ref, sem
):
    bands, stamps = pix_ref.shape[:2]
    half = stamps // 2
    parts = [(b, slice(h * half, (h + 1) * half)) for b in range(bands) for h in range(2)]
    load = dma(
        [
            pltpu.make_async_copy(pix_hbm.at[b, rows], pix_ref.at[b, rows], sem.at[i])
            for i, (b, rows) in enumerate(parts)
        ]
    )
    n_sky = got_ref.shape[0]
    n_all = hot_ref.shape[0]
    block = LANES
    owner = owner_ref[0:1, :]

    def hot(i, carry):
        rows = pl.ds(pl.multiple_of(i * block, block), block)
        hit = iota((block, stamps), 0) + i * block == owner
        hot_ref[rows, :] = jnp.where(hit, 1.0, 0.0).astype(bf16)
        return carry

    lax.fori_loop(0, n_all // block, hot, 0)
    lane = iota((8, LANES), 1)
    for d in range(n_sky):
        theta_ref[d] = got_ref[d, 0:8, :]
    for i in range(n_sky // 2):
        span = slice(i * LANES, (i + 1) * LANES)
        table_ref[0:8, span] = unfold(got_ref, slice(8, 16), lane, i, True)
        table_ref[8:16, span] = unfold(got_ref, slice(8, 16), lane, i, False)
    parts = jnp.concatenate(split3(table_ref[...]), axis=0)
    found = dot(parts, hot_ref[...])
    found = found[0:16] + found[16:32] + found[32:48]
    near_id = found[0:nei].astype(jnp.int32)
    near_w = found[8 : 8 + nei]

    def blend(i, carry):
        rows = pl.ds(pl.multiple_of(i * block, block), block)
        here = iota((block, stamps), 0) + i * block
        mix = jnp.zeros((block, stamps), f32)
        for j in range(nei):
            mix = mix + jnp.where(here == near_id[j : j + 1], near_w[j : j + 1], 0.0)
        high = mix.astype(bf16)
        blend_ref[rows, 0:stamps] = high
        blend_ref[rows, stamps : 2 * stamps] = (mix - high.astype(f32)).astype(bf16)
        return carry

    lax.fori_loop(0, n_all // block, blend, 0)
    wait(load)


def terms_kernel(
    sizes,
    theta_ref,
    hot_ref,
    blend_ref,
    gain_ref,
    base_ref,
    tag_ref,
    pix_ref,
    tpl_ref,
    pair_ref,
    sel_ref,
    wide_ref,
    out_ref,
    amp_ref,
    acc_ref,
    proj_ref,
    lit_ref,
):
    n_sky, cap, fold, chunk, extra = sizes
    bands, stamps, pix = pix_ref.shape
    size_k = tpl_ref.shape[1] // 2
    steps = [
        (b, slice(c * chunk, (c + 1) * chunk)) for b in range(bands) for c in range(pix // chunk)
    ]
    lane = iota((8, LANES), 1)
    for i in range(n_sky // 2):
        span = slice(i * LANES, (i + 1) * LANES)
        amp_ref[0:8, span] = jnp.exp(unfold(theta_ref, slice(None), lane, i, True))
        amp_ref[8:16, span] = jnp.exp(unfold(theta_ref, slice(None), lane, i, False))
    parts = jnp.concatenate(split3(amp_ref[...]), axis=0)
    got = dot(parts, hot_ref[...])
    mix = dot(parts, blend_ref[...])
    k1, k2, k3 = slice(0, size_k), slice(size_k, 2 * size_k), slice(2 * size_k, 3 * size_k)
    slot_f = got[k1] + (got[k2] + got[k3])
    high, low = mix[:, :stamps], mix[:, stamps:]
    slot_u = high[k1] + (high[k2] + low[k1] + (high[k3] + low[k2]))
    scaled = gain_ref[0:1, :] * slot_f
    lit_ref[...] = jnp.concatenate([scaled, slot_u], axis=0).T.astype(bf16)
    acc_ref[...] = jnp.zeros_like(acc_ref)
    proj_ref[...] = jnp.zeros_like(proj_ref)
    lit = lit_ref[...]
    base = jnp.concatenate([base_ref[...]] * (chunk // LANES), axis=1)
    wide = pair_ref.shape[1]

    def model(b, px):
        return dot(lit, tpl_ref[b, :, px])

    def weigh(b, px, light):
        resid = pix_ref[b, :, px].astype(f32) - light
        under = base + (resid * resid) * (1.0 / ROBUST)
        guess = pltpu.reciprocal(under, approx=True)
        weight = guess * (2.0 - under * guess)
        return weight.astype(bf16), (weight * resid).astype(bf16)

    def gather(b, px, weight, wres):
        acc_ref[:, 0:wide] += dot(weight, pair_ref[b, :, px], NT)
        proj_ref[:, 0:size_k] += dot(wres, tpl_ref[b, 0:size_k, px], NT)

    light = model(*steps[0])
    held = None
    for i, here in enumerate(steps):
        ahead = model(*steps[i + 1]) if i + 1 < len(steps) else None
        now = weigh(*here, light)
        if held is not None:
            gather(*steps[i - 1], *held)
        light, held = ahead, now
    gather(*steps[-1], *held)

    scales = dot(jnp.concatenate(split3(scaled), axis=0), wide_ref[...], TN)
    col = iota((1, 2 * LANES), 1) - (LANES + extra)
    is_grad = jnp.where((col >= 0) & (col < size_k), 1.0, 0.0)
    factor = scales[:, : 2 * LANES] * (scales[:, 2 * LANES :] + is_grad)
    tail = acc_ref[:, LANES:] + pltpu.roll(proj_ref[...], extra, 1)
    terms = jnp.concatenate(
        [
            factor[:, :LANES] * acc_ref[:, :LANES],
            factor[:, LANES:] * tail + tag_ref[...],
        ],
        axis=1,
    )
    t1, t2, t3 = split3(terms)
    sel = sel_ref[...]
    rows = dot(sel, t1) + (dot(sel, t2) + dot(sel, t3))
    per = cap // fold
    for d in range(n_sky):
        base_row = d * cap
        out_ref[d, 0:cap, :] = rows[base_row : base_row + cap, :LANES]
        tail = rows[base_row : base_row + per, LANES:]
        for g in range(1, fold):
            at = base_row + g * per
            tail = tail + pltpu.roll(rows[at : at + per, LANES:], g * GROUP, 1)
        out_ref[d, cap : cap + per, :] = tail


def solve_kernel(
    sizes,
    recv_ref,
    other_ref,
    member_in_ref,
    full_ref,
    theta_ref,
    init_ref,
    pay_ref,
    new_ref,
    member_ref,
    rows_ref,
):
    n_sky, cap, fold, n_band, tag, learn = sizes
    per = cap // fold
    size_k, obj_dev = theta_ref.shape
    total = n_sky * cap
    group = iota((per, LANES), 1) // GROUP
    for d in range(n_sky):
        both = recv_ref[d] + other_ref[d]
        rows_ref[d * cap : d * cap + cap, 0:LANES] = both[0:cap]
        tail = both[cap : cap + per]
        for g in range(fold):
            at = d * cap + g * per
            rows_ref[at : at + per, LANES:] = jnp.where(group == g, tail, 0.0)
    p1, p2, p3 = split3(rows_ref[...])
    if learn:
        where_tag = jnp.where(column((8, 2 * LANES), LANES + tag), 1.0, 0.0).astype(bf16)
        ids = dot(where_tag, p1, NT) + (dot(where_tag, p2, NT) + dot(where_tag, p3, NT))
        named = (iota((obj_dev, total), 0) + 1) * n_band
        hit = named == ids[0:1, :].astype(jnp.int32)
        member_ref[...] = jnp.where(hit, 1.0, 0.0).astype(bf16)
        member = member_ref[...]
    else:
        member = member_in_ref[...]
    sums = dot(member, p1) + (dot(member, p2) + dot(member, p3))
    q1, q2, q3 = split3(sums)
    full = full_ref[...]
    wide = dot(full, q1, NT) + (dot(full, q2, NT) + dot(full, q3, NT))
    row = iota((size_k, obj_dev), 0)
    theta = theta_ref[...]
    target = wide[size_k * size_k :] - PRIOR * (theta - init_ref[...])
    matrix = []
    for k in range(size_k):
        line = wide[k * size_k : (k + 1) * size_k]
        matrix.append(jnp.where(row == k, line + (DAMPING * line + PRIOR), line))
    inverse = []
    for p in range(size_k):
        line = matrix[p]
        inv = 1.0 / line[p : p + 1]
        inverse.append(inv)
        if p + 1 < size_k:
            scaled = jnp.where(row > p, line * inv, 0.0)
            target = target - scaled * target[p : p + 1]
            for k in range(p + 1, size_k):
                matrix[k] = matrix[k] - scaled * line[k : k + 1]
    delta = jnp.zeros_like(target)
    for p in reversed(range(size_k)):
        value = target[p : p + 1] * inverse[p]
        delta = jnp.where(row == p, value, delta)
        if p:
            target = target - matrix[p] * value
    new = theta + STEP_LIMIT * jnp.tanh(delta / STEP_LIMIT)
    new_ref[...] = new
    if pay_ref is not None:
        half = size_k // 2
        folded = jnp.concatenate([new[:half], new[half:]], axis=1)
        for d in range(n_sky):
            pay_ref[d] = folded


def hbm(x):
    return pltpu.with_memory_space_constraint(x, pltpu.HBM)


def call(kernel, out_shape, scratch=(), spaces=None):
    specs = {}
    if spaces:
        specs["in_specs"] = [
            pl.BlockSpec(memory_space=pltpu.HBM if s == "h" else pltpu.VMEM) for s in spaces
        ]
    return pl.pallas_call(
        kernel,
        out_shape=out_shape,
        scratch_shapes=list(scratch),
        compiler_params=pltpu.CompilerParams(vmem_limit_bytes=VMEM_LIMIT),
        **specs,
    )


def local(
    stamps,
    stamp_gain,
    stamp_invvar,
    stamp_dest,
    stamp_obj,
    phi_tpl,
    psi_tpl,
    theta_init,
    nb_id,
    nb_weight,
):
    n_sky = lax.axis_size("sky")
    n_band = lax.axis_size("band")
    stamp_dev, bands, pix = stamps.shape
    size_k, obj_dev = theta_init.shape
    nei = nb_id.shape[1]
    cap = 2 * stamp_dev // n_sky
    fold = max(1, min(LANES // GROUP, cap // 8))
    total = n_sky * cap
    n_all = n_sky * obj_dev
    rows = cap + cap // fold
    extra = size_k * (size_k + 1) // 2 - LANES
    wide = LANES + -(-extra // 16) * 16
    assert n_band == 2 and 2 * obj_dev == LANES and 0 <= extra and extra + size_k < GROUP
    shape = jax.ShapeDtypeStruct
    chunk = max(c for c in range(LANES, 1024, LANES) if pix % c == 0)

    pixels = jnp.transpose(stamps, (1, 0, 2))
    payload = call(
        pack_kernel,
        shape((n_sky, 16, LANES), f32),
        [
            pltpu.VMEM((size_k, obj_dev), f32),
            pltpu.VMEM((nei, obj_dev), jnp.int32),
            pltpu.VMEM((nei, obj_dev), f32),
            pltpu.SemaphoreType.DMA((3,)),
        ],
        "hhh",
    )(hbm(theta_init), hbm(nb_id.T), hbm(nb_weight.T))
    got = lax.all_to_all(payload, "sky", 0, 0, tiled=True)
    tpl, pair, sel, spread, full, base, tag, gain, owner = call(
        functools.partial(ready_kernel, (n_sky, cap, obj_dev, extra)),
        (
            shape((bands, 2 * size_k, pix), bf16),
            shape((bands, wide, pix), bf16),
            shape((total, stamp_dev), bf16),
            shape((3 * size_k, 4 * LANES), bf16),
            shape((size_k * size_k + size_k, 2 * LANES), bf16),
            shape((stamp_dev, LANES), f32),
            shape((stamp_dev, LANES), f32),
            shape((8, stamp_dev), f32),
            shape((8, stamp_dev), jnp.int32),
        ),
        [
            pltpu.VMEM((1, stamp_dev), jnp.int32),
            pltpu.VMEM((1, stamp_dev), jnp.int32),
            pltpu.VMEM((stamp_dev,), bf16),
            pltpu.VMEM((stamp_dev,), bf16),
            pltpu.SemaphoreType.DMA((6,)),
        ],
        "hhhhhh",
    )(
        hbm(stamp_dest.T),
        hbm(stamp_obj[None, :]),
        hbm(stamp_gain),
        hbm(stamp_invvar),
        hbm(phi_tpl),
        hbm(psi_tpl),
    )
    everyone, hot, blend, pixels = call(
        functools.partial(index_kernel, nei),
        (
            shape((n_sky, 8, LANES), f32),
            shape((n_all, stamp_dev), bf16),
            shape((n_all, 2 * stamp_dev), bf16),
            shape((bands, stamp_dev, pix), bf16),
        ),
        [pltpu.VMEM((16, n_all), f32), pltpu.SemaphoreType.DMA((2 * bands,))],
        "vvh",
    )(got, owner, hbm(pixels))
    terms = call(
        functools.partial(terms_kernel, (n_sky, cap, fold, chunk, extra)),
        shape((n_sky, rows, LANES), f32),
        [
            pltpu.VMEM((size_k, n_all), f32),
            pltpu.VMEM((stamp_dev, 2 * LANES), f32),
            pltpu.VMEM((stamp_dev, LANES), f32),
            pltpu.VMEM((stamp_dev, 2 * size_k), bf16),
        ],
    )
    theta = theta_init
    member = None
    for sweep in range(ITERS):
        sent = terms(
            everyone, hot, blend, gain, base, tag, pixels, tpl, pair, sel, spread
        )
        recv = lax.all_to_all(sent, "sky", 0, 0, tiled=True)
        other = lax.ppermute(recv, "band", [(0, 1), (1, 0)])
        learn, last = sweep == 0, sweep + 1 == ITERS
        sizes = (n_sky, cap, fold, n_band, extra + size_k, learn)

        def solve(*refs, learn=learn, last=last, sizes=sizes):
            refs = list(refs)
            if learn:
                refs.insert(2, None)
            if last:
                refs.insert(6, None)
            if not learn:
                refs.insert(8, None)
            solve_kernel(sizes, *refs)

        outs = [shape((n_sky, 8, LANES), f32)] * (not last)
        outs += [shape((size_k, obj_dev), f32)]
        outs += [shape((obj_dev, total), bf16)] * learn
        given = [recv, other] + [member] * (not learn) + [full, theta, theta_init]
        outs = call(solve, outs, [pltpu.VMEM((total, 2 * LANES), f32)])(*given)
        theta = outs[0 if last else 1]
        if learn:
            member = outs[-1]
        if not last:
            everyone = lax.all_to_all(outs[0], "sky", 0, 0, tiled=True)
    return theta


def solution(mesh):
    in_specs = (
        P("sky", "band", None),
        P("sky"),
        P("sky"),
        P("sky", None),
        P("sky"),
        P("band", None, None),
        P("band", None, None),
        P(None, "sky"),
        P("sky", None),
        P("sky", None),
    )
    out_specs = P(None, "sky")
    return jax.shard_map(local, mesh=mesh, in_specs=in_specs, out_specs=out_specs, check_vma=False)
```

```python
import functools

import jax
import jax.numpy as jnp
from jax import lax
from jax.experimental import pallas as pl
from jax.experimental.pallas import tpu as pltpu
from jax.sharding import PartitionSpec as P

ITERS = 3

ROBUST = 9.0
DAMPING = 0.1
PRIOR = 1.0
STEP_LIMIT = 0.5

LANES = 128
GROUP = 32
SUB = 4
VMEM_LIMIT = 24 * 1024 * 1024

f32 = jnp.float32
bf16 = jnp.bfloat16
NT = (((1,), (1,)), ((), ()))
TN = (((0,), (0,)), ((), ()))
NN = (((1,), (0,)), ((), ()))


def dot(a, b, dims=NN, precision=None):
    return lax.dot_general(a, b, dims, precision=precision, preferred_element_type=f32)


def split3(x):
    first = x.astype(bf16)
    rest = x - first.astype(f32)
    second = rest.astype(bf16)
    third = (rest - second.astype(f32)).astype(bf16)
    return first, second, third


def iota(shape, dim):
    return lax.broadcasted_iota(jnp.int32, shape, dim)


def dma(copies):
    for copy in copies:
        copy.start()
    return copies


def wait(copies):
    for copy in copies:
        copy.wait()


def offset(k, size_k):
    return lax.div(k * (2 * size_k + 1 - k), 2)


def column(shape, m):
    lane = iota(shape, 1)
    folded = jnp.where(lane < LANES, lane, LANES + lax.rem(lane, GROUP))
    return folded == m


def pack_kernel(theta_hbm, nbi_hbm, nbw_hbm, pay_ref, theta_ref, nbi_ref, nbw_ref, sem):
    n_sky = pay_ref.shape[0]
    wait(
        dma(
            [
                pltpu.make_async_copy(theta_hbm, theta_ref, sem.at[0]),
                pltpu.make_async_copy(nbi_hbm, nbi_ref, sem.at[1]),
                pltpu.make_async_copy(nbw_hbm, nbw_ref, sem.at[2]),
            ]
        )
    )
    half = theta_ref.shape[0] // 2
    theta = theta_ref[...]
    folded = jnp.concatenate([theta[:half], theta[half:]], axis=1)
    side = jnp.concatenate([nbi_ref[...].astype(f32), nbw_ref[...]], axis=1)
    side = jnp.concatenate([side, jnp.zeros((8 - side.shape[0], LANES), f32)], axis=0)
    for d in range(n_sky):
        pay_ref[d, 0:8, :] = folded
        pay_ref[d, 8:16, :] = side


def ready_kernel(
    sizes,
    dest_hbm,
    obj_hbm,
    gain_hbm,
    invvar_hbm,
    phi_hbm,
    psi_hbm,
    tpl_ref,
    pair_ref,
    sel_ref,
    wide_ref,
    full_ref,
    base_ref,
    tag_ref,
    gain_ref,
    owner_ref,
    dest_ref,
    obj_ref,
    gain_low_ref,
    invvar_ref,
    sem,
):
    n_sky, cap, obj_dev, extra = sizes
    bands, size_k, pix = phi_hbm.shape
    stamps = dest_ref.shape[1]
    total = n_sky * cap
    first = [
        pltpu.make_async_copy(phi_hbm, tpl_ref.at[:, 0:size_k, :], sem.at[0]),
        pltpu.make_async_copy(psi_hbm, tpl_ref.at[:, size_k : 2 * size_k, :], sem.at[1]),
        pltpu.make_async_copy(dest_hbm, dest_ref, sem.at[2]),
        pltpu.make_async_copy(obj_hbm, obj_ref, sem.at[3]),
        pltpu.make_async_copy(gain_hbm, gain_low_ref, sem.at[4]),
        pltpu.make_async_copy(invvar_hbm, invvar_ref, sem.at[5]),
    ]
    dma(first)

    pairs = LANES + extra
    shape = (pair_ref.shape[1], size_k)
    m = iota(shape, 0)
    k = iota(shape, 1)
    lows = jnp.where((m >= offset(k, size_k)) & (m < offset(k + 1, size_k)), 1.0, 0.0)
    of_m = jnp.sum(lows * k.astype(f32), axis=1, keepdims=True).astype(jnp.int32)
    highs = jnp.where((m < pairs) & (m - offset(of_m, size_k) + of_m == k), 1.0, 0.0)
    lows, highs = lows.astype(bf16), highs.astype(bf16)

    shape = (size_k, 2 * LANES)
    k = iota(shape, 0)
    lane = iota(shape, 1)
    spot = pairs + k
    left = (lane >= offset(k, size_k)) & (lane < offset(k + 1, size_k))
    left = jnp.where(left | (lane == spot), 1.0, 0.0)
    lane_k = jnp.sum(jnp.where(lane >= offset(k + 1, size_k), 1, 0), axis=0, keepdims=True)
    right = (lane[0:1] - offset(lane_k, size_k) + lane_k == k) & (lane < pairs)
    both = jnp.concatenate([left, jnp.where(right, 1.0, 0.0)], axis=1).astype(bf16)
    for part in range(3):
        wide_ref[part * size_k : (part + 1) * size_k, :] = both

    shape = full_ref.shape
    r = iota((shape[0], 1), 0)
    a, b = lax.div(r, size_k), lax.rem(r, size_k)
    low, high = jnp.minimum(a, b), jnp.maximum(a, b)
    m = jnp.where(r < size_k * size_k, offset(low, size_k) + high - low, pairs + b)
    full_ref[...] = jnp.where(column(shape, m), 1.0, 0.0).astype(bf16)

    wait(first)
    dest = dest_ref[...]
    obj = obj_ref[...]
    gain = gain_low_ref[...].astype(f32).reshape(1, stamps)
    gain_ref[...] = jnp.broadcast_to(gain, gain_ref.shape)
    variance = 1.0 / invvar_ref[...].astype(f32).reshape(1, stamps)
    base_ref[...] = jnp.broadcast_to(variance, (LANES, stamps)).T
    named = jnp.broadcast_to((obj + 1).astype(f32), (LANES, stamps)).T
    tag_ref[...] = jnp.where(
        iota((stamps, LANES), 1) == extra + size_k, named, 0.0
    )
    along = jnp.broadcast_to(dest.astype(f32), (stamps, stamps))
    before = iota((stamps, stamps), 0) < iota((stamps, stamps), 1)
    rank = jnp.sum(jnp.where(before & (along == along.T), 1.0, 0.0), axis=0, keepdims=True)
    owner_ref[...] = jnp.broadcast_to(dest * obj_dev + obj, owner_ref.shape)
    half = cap // 2
    rank = rank.astype(jnp.int32)
    given = jnp.where(rank >= half, 1, 0) != lax.axis_index("band")
    place = (dest + jnp.where(given, n_sky, 0)) * half + lax.rem(rank, half)
    sel_ref[...] = jnp.where(iota((total, stamps), 0) == place, 1.0, 0.0).astype(bf16)
    chunk = 256

    def step(c, carry):
        px = pl.ds(pl.multiple_of(c * chunk, chunk), chunk)
        for b in range(bands):
            phi = tpl_ref[b, 0:size_k, px]
            pair_ref[b, :, px] = (dot(lows, phi) * dot(highs, phi)).astype(bf16)
        return carry

    lax.fori_loop(0, pix // chunk, step, 0)


def unfold(ref, rows, lane, i, left):
    x, y = ref[2 * i, rows, :], ref[2 * i + 1, rows, :]
    if left:
        return jnp.where(lane < LANES // 2, x, pltpu.roll(y, LANES // 2, 1))
    return jnp.where(lane < LANES // 2, pltpu.roll(x, LANES // 2, 1), y)


def index_kernel(
    nei, got_ref, owner_ref, pix_hbm, theta_ref, hot_ref, blend_ref, pix_ref, table_ref, sem
):
    bands, stamps = pix_ref.shape[:2]
    half = stamps // 2
    parts = [(b, slice(h * half, (h + 1) * half)) for b in range(bands) for h in range(2)]
    load = dma(
        [
            pltpu.make_async_copy(pix_hbm.at[b, rows], pix_ref.at[b, rows], sem.at[i])
            for i, (b, rows) in enumerate(parts)
        ]
    )
    n_sky = got_ref.shape[0]
    n_all = hot_ref.shape[0]
    block = LANES
    owner = owner_ref[0:1, :]

    def hot(i, carry):
        rows = pl.ds(pl.multiple_of(i * block, block), block)
        hit = iota((block, stamps), 0) + i * block == owner
        hot_ref[rows, :] = jnp.where(hit, 1.0, 0.0).astype(bf16)
        return carry

    lax.fori_loop(0, n_all // block, hot, 0)
    lane = iota((8, LANES), 1)
    for d in range(n_sky):
        theta_ref[d] = got_ref[d, 0:8, :]
    for i in range(n_sky // 2):
        span = slice(i * LANES, (i + 1) * LANES)
        table_ref[0:8, span] = unfold(got_ref, slice(8, 16), lane, i, True)
        table_ref[8:16, span] = unfold(got_ref, slice(8, 16), lane, i, False)
    parts = jnp.concatenate(split3(table_ref[...]), axis=0)
    found = dot(parts, hot_ref[...])
    found = found[0:16] + found[16:32] + found[32:48]
    near_id = found[0:nei].astype(jnp.int32)
    near_w = found[8 : 8 + nei]

    def blend(i, carry):
        rows = pl.ds(pl.multiple_of(i * block, block), block)
        here = iota((block, stamps), 0) + i * block
        mix = jnp.zeros((block, stamps), f32)
        for j in range(nei):
            mix = mix + jnp.where(here == near_id[j : j + 1], near_w[j : j + 1], 0.0)
        high = mix.astype(bf16)
        blend_ref[rows, 0:stamps] = high
        blend_ref[rows, stamps : 2 * stamps] = (mix - high.astype(f32)).astype(bf16)
        return carry

    lax.fori_loop(0, n_all // block, blend, 0)
    wait(load)


def terms_kernel(
    sizes,
    theta_ref,
    hot_ref,
    blend_ref,
    gain_ref,
    base_ref,
    tag_ref,
    pix_ref,
    tpl_ref,
    pair_ref,
    sel_ref,
    wide_ref,
    keep_ref,
    give_ref,
    amp_ref,
    acc_ref,
    proj_ref,
    lit_ref,
    rows_ref,
):
    n_sky, half, chunk, extra = sizes
    bands, stamps, pix = pix_ref.shape
    size_k = tpl_ref.shape[1] // 2
    steps = [
        (b, slice(c * chunk, (c + 1) * chunk)) for b in range(bands) for c in range(pix // chunk)
    ]
    lane = iota((8, LANES), 1)
    for i in range(n_sky // 2):
        span = slice(i * LANES, (i + 1) * LANES)
        amp_ref[0:8, span] = jnp.exp(unfold(theta_ref, slice(None), lane, i, True))
        amp_ref[8:16, span] = jnp.exp(unfold(theta_ref, slice(None), lane, i, False))
    parts = jnp.concatenate(split3(amp_ref[...]), axis=0)
    got = dot(parts, hot_ref[...])
    mix = dot(parts, blend_ref[...])
    k1, k2, k3 = slice(0, size_k), slice(size_k, 2 * size_k), slice(2 * size_k, 3 * size_k)
    slot_f = got[k1] + (got[k2] + got[k3])
    high, low = mix[:, :stamps], mix[:, stamps:]
    slot_u = high[k1] + (high[k2] + low[k1] + (high[k3] + low[k2]))
    scaled = gain_ref[0:1, :] * slot_f
    lit_ref[...] = jnp.concatenate([scaled, slot_u], axis=0).T.astype(bf16)
    acc_ref[...] = jnp.zeros_like(acc_ref)
    proj_ref[...] = jnp.zeros_like(proj_ref)
    lit = lit_ref[...]
    base = jnp.concatenate([base_ref[...]] * (chunk // LANES), axis=1)
    wide = pair_ref.shape[1]

    def model(b, px):
        return dot(lit, tpl_ref[b, :, px])

    def weigh(b, px, light):
        resid = pix_ref[b, :, px].astype(f32) - light
        under = base + (resid * resid) * (1.0 / ROBUST)
        guess = pltpu.reciprocal(under, approx=True)
        weight = guess * (2.0 - under * guess)
        return weight.astype(bf16), (weight * resid).astype(bf16)

    def gather(b, px, weight, wres):
        acc_ref[:, 0:wide] += dot(weight, pair_ref[b, :, px], NT)
        proj_ref[:, 0:size_k] += dot(wres, tpl_ref[b, 0:size_k, px], NT)

    light = model(*steps[0])
    held = None
    for i, here in enumerate(steps):
        ahead = model(*steps[i + 1]) if i + 1 < len(steps) else None
        now = weigh(*here, light)
        if held is not None:
            gather(*steps[i - 1], *held)
        light, held = ahead, now
    gather(*steps[-1], *held)

    scales = dot(jnp.concatenate(split3(scaled), axis=0), wide_ref[...], TN)
    col = iota((1, 2 * LANES), 1) - (LANES + extra)
    is_grad = jnp.where((col >= 0) & (col < size_k), 1.0, 0.0)
    factor = scales[:, : 2 * LANES] * (scales[:, 2 * LANES :] + is_grad)
    tail = acc_ref[:, LANES:] + pltpu.roll(proj_ref[...], extra, 1)
    terms = jnp.concatenate(
        [
            factor[:, :LANES] * acc_ref[:, :LANES],
            factor[:, LANES:] * tail + tag_ref[...],
        ],
        axis=1,
    )
    t1, t2, t3 = split3(terms)
    sel = sel_ref[...]
    rows_ref[...] = dot(sel, t1) + (dot(sel, t2) + dot(sel, t3))
    groups = half // SUB
    for part, out_ref in enumerate((keep_ref, give_ref)):
        for d in range(n_sky):
            at = (part * n_sky + d) * half
            for g in range(groups):
                line = rows_ref[at + g * SUB : at + (g + 1) * SUB, :]
                out_ref[d, :, g * LANES : (g + 1) * LANES] = line[:, :LANES]
                more = pltpu.roll(line[:, LANES:], g * GROUP, 1) if g else line[:, LANES:]
                tail = tail + more if g else more
            out_ref[d, :, groups * LANES :] = tail


def solve_kernel(
    sizes,
    recv_ref,
    other_ref,
    member_in_ref,
    full_ref,
    theta_ref,
    init_ref,
    pay_ref,
    new_ref,
    member_ref,
    rows_ref,
):
    n_sky, half, n_band, tag, learn = sizes
    size_k, obj_dev = theta_ref.shape
    total = 2 * n_sky * half
    groups = half // SUB
    group = iota((SUB, LANES), 1) // GROUP
    first = jnp.full((SUB, LANES), lax.axis_index("band")) == 0
    for d in range(n_sky):
        for g in range(groups + 1):
            span = slice(g * LANES, (g + 1) * LANES)
            mine, others = recv_ref[d, :, span], other_ref[d, :, span]
            pair = (jnp.where(first, mine, others), jnp.where(first, others, mine))
            for part, line in enumerate(pair):
                at = (part * n_sky + d) * half
                if g < groups:
                    rows_ref[at + g * SUB : at + (g + 1) * SUB, 0:LANES] = line
                else:
                    for h in range(groups):
                        rows_ref[at + h * SUB : at + (h + 1) * SUB, LANES:] = jnp.where(
                            group == h, line, 0.0
                        )
    p1, p2, p3 = split3(rows_ref[...])
    if learn:
        where_tag = jnp.where(column((8, 2 * LANES), LANES + tag), 1.0, 0.0).astype(bf16)
        ids = dot(where_tag, p1, NT) + (dot(where_tag, p2, NT) + dot(where_tag, p3, NT))
        named = (iota((obj_dev, total), 0) + 1) * n_band
        hit = named == ids[0:1, :].astype(jnp.int32)
        member_ref[...] = jnp.where(hit, 1.0, 0.0).astype(bf16)
        member = member_ref[...]
    else:
        member = member_in_ref[...]
    sums = dot(member, p1) + (dot(member, p2) + dot(member, p3))
    q1, q2, q3 = split3(sums)
    full = full_ref[...]
    wide = dot(full, q1, NT) + (dot(full, q2, NT) + dot(full, q3, NT))
    row = iota((size_k, obj_dev), 0)
    theta = theta_ref[...]
    target = wide[size_k * size_k :] - PRIOR * (theta - init_ref[...])
    matrix = []
    for k in range(size_k):
        line = wide[k * size_k : (k + 1) * size_k]
        matrix.append(jnp.where(row == k, line + (DAMPING * line + PRIOR), line))
    inverse = []
    for p in range(size_k):
        line = matrix[p]
        inv = 1.0 / line[p : p + 1]
        inverse.append(inv)
        if p + 1 < size_k:
            scaled = jnp.where(row > p, line * inv, 0.0)
            target = target - scaled * target[p : p + 1]
            for k in range(p + 1, size_k):
                matrix[k] = matrix[k] - scaled * line[k : k + 1]
    delta = jnp.zeros_like(target)
    for p in reversed(range(size_k)):
        value = target[p : p + 1] * inverse[p]
        delta = jnp.where(row == p, value, delta)
        if p:
            target = target - matrix[p] * value
    new = theta + STEP_LIMIT * jnp.tanh(delta / STEP_LIMIT)
    new_ref[...] = new
    if pay_ref is not None:
        half = size_k // 2
        folded = jnp.concatenate([new[:half], new[half:]], axis=1)
        for d in range(n_sky):
            pay_ref[d] = folded


def hbm(x):
    return pltpu.with_memory_space_constraint(x, pltpu.HBM)


def call(kernel, out_shape, scratch=(), spaces=None):
    specs = {}
    if spaces:
        specs["in_specs"] = [
            pl.BlockSpec(memory_space=pltpu.HBM if s == "h" else pltpu.VMEM) for s in spaces
        ]
    return pl.pallas_call(
        kernel,
        out_shape=out_shape,
        scratch_shapes=list(scratch),
        compiler_params=pltpu.CompilerParams(vmem_limit_bytes=VMEM_LIMIT),
        **specs,
    )


def local(
    stamps,
    stamp_gain,
    stamp_invvar,
    stamp_dest,
    stamp_obj,
    phi_tpl,
    psi_tpl,
    theta_init,
    nb_id,
    nb_weight,
):
    n_sky = lax.axis_size("sky")
    n_band = lax.axis_size("band")
    stamp_dev, bands, pix = stamps.shape
    size_k, obj_dev = theta_init.shape
    nei = nb_id.shape[1]
    cap = 2 * stamp_dev // n_sky
    half = cap // 2
    total = n_sky * cap
    n_all = n_sky * obj_dev
    extra = size_k * (size_k + 1) // 2 - LANES
    wide = LANES + -(-extra // 16) * 16
    assert n_band == 2 and half % SUB == 0 and half // SUB <= LANES // GROUP
    assert 2 * obj_dev == LANES and 0 <= extra and extra + size_k < GROUP
    shape = jax.ShapeDtypeStruct
    chunk = max(c for c in range(LANES, 1024, LANES) if pix % c == 0)

    pixels = jnp.transpose(stamps, (1, 0, 2))
    payload = call(
        pack_kernel,
        shape((n_sky, 16, LANES), f32),
        [
            pltpu.VMEM((size_k, obj_dev), f32),
            pltpu.VMEM((nei, obj_dev), jnp.int32),
            pltpu.VMEM((nei, obj_dev), f32),
            pltpu.SemaphoreType.DMA((3,)),
        ],
        "hhh",
    )(hbm(theta_init), hbm(nb_id.T), hbm(nb_weight.T))
    got = lax.all_to_all(payload, "sky", 0, 0, tiled=True)
    tpl, pair, sel, spread, full, base, tag, gain, owner = call(
        functools.partial(ready_kernel, (n_sky, cap, obj_dev, extra)),
        (
            shape((bands, 2 * size_k, pix), bf16),
            shape((bands, wide, pix), bf16),
            shape((total, stamp_dev), bf16),
            shape((3 * size_k, 4 * LANES), bf16),
            shape((size_k * size_k + size_k, 2 * LANES), bf16),
            shape((stamp_dev, LANES), f32),
            shape((stamp_dev, LANES), f32),
            shape((8, stamp_dev), f32),
            shape((8, stamp_dev), jnp.int32),
        ),
        [
            pltpu.VMEM((1, stamp_dev), jnp.int32),
            pltpu.VMEM((1, stamp_dev), jnp.int32),
            pltpu.VMEM((stamp_dev,), bf16),
            pltpu.VMEM((stamp_dev,), bf16),
            pltpu.SemaphoreType.DMA((6,)),
        ],
        "hhhhhh",
    )(
        hbm(stamp_dest.T),
        hbm(stamp_obj[None, :]),
        hbm(stamp_gain),
        hbm(stamp_invvar),
        hbm(phi_tpl),
        hbm(psi_tpl),
    )
    everyone, hot, blend, pixels = call(
        functools.partial(index_kernel, nei),
        (
            shape((n_sky, 8, LANES), f32),
            shape((n_all, stamp_dev), bf16),
            shape((n_all, 2 * stamp_dev), bf16),
            shape((bands, stamp_dev, pix), bf16),
        ),
        [pltpu.VMEM((16, n_all), f32), pltpu.SemaphoreType.DMA((2 * bands,))],
        "vvh",
    )(got, owner, hbm(pixels))
    terms = call(
        functools.partial(terms_kernel, (n_sky, half, chunk, extra)),
        [shape((n_sky, SUB, (half // SUB + 1) * LANES), f32)] * 2,
        [
            pltpu.VMEM((size_k, n_all), f32),
            pltpu.VMEM((stamp_dev, 2 * LANES), f32),
            pltpu.VMEM((stamp_dev, LANES), f32),
            pltpu.VMEM((stamp_dev, 2 * size_k), bf16),
            pltpu.VMEM((total, 2 * LANES), f32),
        ],
    )
    swap = [(0, 1), (1, 0)]
    theta = theta_init
    member = None
    for sweep in range(ITERS):
        keep, give = terms(
            everyone, hot, blend, gain, base, tag, pixels, tpl, pair, sel, spread
        )
        sent = keep + lax.ppermute(give, "band", swap)
        recv = lax.all_to_all(sent, "sky", 0, 0, tiled=True)
        other = lax.ppermute(recv, "band", swap)
        learn, last = sweep == 0, sweep + 1 == ITERS
        sizes = (n_sky, half, n_band, extra + size_k, learn)

        def solve(*refs, learn=learn, last=last, sizes=sizes):
            refs = list(refs)
            if learn:
                refs.insert(2, None)
            if last:
                refs.insert(6, None)
            if not learn:
                refs.insert(8, None)
            solve_kernel(sizes, *refs)

        outs = [shape((n_sky, 8, LANES), f32)] * (not last)
        outs += [shape((size_k, obj_dev), f32)]
        outs += [shape((obj_dev, total), bf16)] * learn
        given = [recv, other] + [member] * (not learn) + [full, theta, theta_init]
        outs = call(solve, outs, [pltpu.VMEM((total, 2 * LANES), f32)])(*given)
        theta = outs[0 if last else 1]
        if learn:
            member = outs[-1]
        if not last:
            everyone = lax.all_to_all(outs[0], "sky", 0, 0, tiled=True)
    return theta


def solution(mesh):
    in_specs = (
        P("sky", "band", None),
        P("sky"),
        P("sky"),
        P("sky", None),
        P("sky"),
        P("band", None, None),
        P("band", None, None),
        P(None, "sky"),
        P("sky", None),
        P("sky", None),
    )
    out_specs = P(None, "sky")
    return jax.shard_map(local, mesh=mesh, in_specs=in_specs, out_specs=out_specs, check_vma=False)
```

```python
import functools

import jax
import jax.numpy as jnp
from jax import lax
from jax.experimental import pallas as pl
from jax.experimental.pallas import tpu as pltpu
from jax.sharding import PartitionSpec as P

ITERS = 3

ROBUST = 9.0
DAMPING = 0.1
PRIOR = 1.0
STEP_LIMIT = 0.5

LANES = 128
GROUP = 32
SUB = 4
VMEM_LIMIT = 24 * 1024 * 1024

f32 = jnp.float32
bf16 = jnp.bfloat16
NT = (((1,), (1,)), ((), ()))
TN = (((0,), (0,)), ((), ()))
NN = (((1,), (0,)), ((), ()))


def dot(a, b, dims=NN, precision=None):
    return lax.dot_general(a, b, dims, precision=precision, preferred_element_type=f32)


def split3(x):
    first = x.astype(bf16)
    rest = x - first.astype(f32)
    second = rest.astype(bf16)
    third = (rest - second.astype(f32)).astype(bf16)
    return first, second, third


def iota(shape, dim):
    return lax.broadcasted_iota(jnp.int32, shape, dim)


def dma(copies):
    for copy in copies:
        copy.start()
    return copies


def wait(copies):
    for copy in copies:
        copy.wait()


def offset(k, size_k):
    return lax.div(k * (2 * size_k + 1 - k), 2)


def column(shape, m):
    lane = iota(shape, 1)
    folded = jnp.where(lane < LANES, lane, LANES + lax.rem(lane, GROUP))
    return folded == m


def ready_kernel(
    sizes,
    dest_hbm,
    obj_hbm,
    gain_hbm,
    invvar_hbm,
    phi_hbm,
    psi_hbm,
    theta_hbm,
    nbi_hbm,
    nbw_hbm,
    pix_hbm,
    pay_ref,
    pix_ref,
    tpl_ref,
    pair_ref,
    sel_ref,
    wide_ref,
    full_ref,
    base_ref,
    tag_ref,
    gain_ref,
    owner_ref,
    dest_ref,
    obj_ref,
    gain_low_ref,
    invvar_ref,
    theta_ref,
    nbi_ref,
    nbw_ref,
    sem,
):
    n_sky, cap, obj_dev, extra, chunk = sizes
    bands, size_k, pix = phi_hbm.shape
    stamps = dest_ref.shape[1]
    total = n_sky * cap
    first = [
        pltpu.make_async_copy(phi_hbm, tpl_ref.at[:, 0:size_k, :], sem.at[0]),
        pltpu.make_async_copy(psi_hbm, tpl_ref.at[:, size_k : 2 * size_k, :], sem.at[1]),
        pltpu.make_async_copy(dest_hbm, dest_ref, sem.at[2]),
        pltpu.make_async_copy(obj_hbm, obj_ref, sem.at[3]),
        pltpu.make_async_copy(gain_hbm, gain_low_ref, sem.at[4]),
        pltpu.make_async_copy(invvar_hbm, invvar_ref, sem.at[5]),
        pltpu.make_async_copy(theta_hbm, theta_ref, sem.at[6]),
        pltpu.make_async_copy(nbi_hbm, nbi_ref, sem.at[7]),
        pltpu.make_async_copy(nbw_hbm, nbw_ref, sem.at[8]),
    ]
    last = [pltpu.make_async_copy(pix_hbm, pix_ref, sem.at[9])]
    dma(first)
    dma(last)

    pairs = LANES + extra
    shape = (pair_ref.shape[1], size_k)
    m = iota(shape, 0)
    k = iota(shape, 1)
    lows = jnp.where((m >= offset(k, size_k)) & (m < offset(k + 1, size_k)), 1.0, 0.0)
    of_m = jnp.sum(lows * k.astype(f32), axis=1, keepdims=True).astype(jnp.int32)
    highs = jnp.where((m < pairs) & (m - offset(of_m, size_k) + of_m == k), 1.0, 0.0)
    lows, highs = lows.astype(bf16), highs.astype(bf16)

    shape = (size_k, 2 * LANES)
    k = iota(shape, 0)
    lane = iota(shape, 1)
    spot = pairs + k
    left = (lane >= offset(k, size_k)) & (lane < offset(k + 1, size_k))
    left = jnp.where(left | (lane == spot), 1.0, 0.0)
    lane_k = jnp.sum(jnp.where(lane >= offset(k + 1, size_k), 1, 0), axis=0, keepdims=True)
    right = (lane[0:1] - offset(lane_k, size_k) + lane_k == k) & (lane < pairs)
    both = jnp.concatenate([left, jnp.where(right, 1.0, 0.0)], axis=1).astype(bf16)
    for part in range(3):
        wide_ref[part * size_k : (part + 1) * size_k, :] = both

    shape = full_ref.shape
    r = iota((shape[0], 1), 0)
    a, b = lax.div(r, size_k), lax.rem(r, size_k)
    low, high = jnp.minimum(a, b), jnp.maximum(a, b)
    m = jnp.where(r < size_k * size_k, offset(low, size_k) + high - low, pairs + b)
    full_ref[...] = jnp.where(column(shape, m), 1.0, 0.0).astype(bf16)

    wait(first)
    theta = theta_ref[...]
    folded = jnp.concatenate([theta[: size_k // 2], theta[size_k // 2 :]], axis=1)
    side = jnp.concatenate([nbi_ref[...].astype(f32), nbw_ref[...]], axis=1)
    side = jnp.concatenate([side, jnp.zeros((8 - side.shape[0], LANES), f32)], axis=0)
    for d in range(n_sky):
        pay_ref[d, 0:8, :] = folded
        pay_ref[d, 8:16, :] = side
    dest = dest_ref[...]
    obj = obj_ref[...]
    gain = gain_low_ref[...].astype(f32).reshape(1, stamps)
    gain_ref[...] = jnp.broadcast_to(gain, gain_ref.shape)
    variance = 1.0 / invvar_ref[...].astype(f32).reshape(1, stamps)
    base_ref[...] = jnp.broadcast_to(variance, (LANES, stamps)).T
    named = jnp.broadcast_to((obj + 1).astype(f32), (LANES, stamps)).T
    tag_ref[...] = jnp.where(
        iota((stamps, LANES), 1) == extra + size_k, named, 0.0
    )
    along = jnp.broadcast_to(dest.astype(f32), (stamps, stamps))
    before = iota((stamps, stamps), 0) < iota((stamps, stamps), 1)
    rank = jnp.sum(jnp.where(before & (along == along.T), 1.0, 0.0), axis=0, keepdims=True)
    owner_ref[...] = jnp.broadcast_to(dest * obj_dev + obj, owner_ref.shape)
    half = cap // 2
    rank = rank.astype(jnp.int32)
    given = jnp.where(rank >= half, 1, 0) != lax.axis_index("band")
    place = (dest + jnp.where(given, n_sky, 0)) * half + lax.rem(rank, half)
    sel_ref[...] = jnp.where(iota((total, stamps), 0) == place, 1.0, 0.0).astype(bf16)
    for b in range(bands):
        for c in range(pix // chunk):
            px = slice(c * chunk, (c + 1) * chunk)
            phi = tpl_ref[b, 0:size_k, px]
            pair_ref[b, :, px] = (dot(lows, phi) * dot(highs, phi)).astype(bf16)
    wait(last)


def unfold(ref, rows, lane, i, left):
    x, y = ref[2 * i, rows, :], ref[2 * i + 1, rows, :]
    if left:
        return jnp.where(lane < LANES // 2, x, pltpu.roll(y, LANES // 2, 1))
    return jnp.where(lane < LANES // 2, pltpu.roll(x, LANES // 2, 1), y)


def index_kernel(nei, got_ref, owner_ref, theta_ref, hot_ref, blend_ref, table_ref):
    n_sky = got_ref.shape[0]
    n_all, stamps = hot_ref.shape
    block = LANES
    owner = owner_ref[0:1, :]

    def hot(i, carry):
        rows = pl.ds(pl.multiple_of(i * block, block), block)
        hit = iota((block, stamps), 0) + i * block == owner
        hot_ref[rows, :] = jnp.where(hit, 1.0, 0.0).astype(bf16)
        return carry

    lax.fori_loop(0, n_all // block, hot, 0)
    lane = iota((8, LANES), 1)
    for d in range(n_sky):
        theta_ref[d] = got_ref[d, 0:8, :]
    for i in range(n_sky // 2):
        span = slice(i * LANES, (i + 1) * LANES)
        table_ref[0:8, span] = unfold(got_ref, slice(8, 16), lane, i, True)
        table_ref[8:16, span] = unfold(got_ref, slice(8, 16), lane, i, False)
    parts = jnp.concatenate(split3(table_ref[...]), axis=0)
    found = dot(parts, hot_ref[...])
    found = found[0:16] + found[16:32] + found[32:48]
    near_id = found[0:nei].astype(jnp.int32)
    near_w = found[8 : 8 + nei]

    def blend(i, carry):
        rows = pl.ds(pl.multiple_of(i * block, block), block)
        here = iota((block, stamps), 0) + i * block
        mix = jnp.zeros((block, stamps), f32)
        for j in range(nei):
            mix = mix + jnp.where(here == near_id[j : j + 1], near_w[j : j + 1], 0.0)
        high = mix.astype(bf16)
        blend_ref[rows, 0:stamps] = high
        blend_ref[rows, stamps : 2 * stamps] = (mix - high.astype(f32)).astype(bf16)
        return carry

    lax.fori_loop(0, n_all // block, blend, 0)


def terms_kernel(
    sizes,
    theta_ref,
    hot_ref,
    blend_ref,
    gain_ref,
    base_ref,
    tag_ref,
    pix_ref,
    tpl_ref,
    pair_ref,
    sel_ref,
    wide_ref,
    keep_ref,
    give_ref,
    amp_ref,
    acc_ref,
    proj_ref,
    lit_ref,
    rows_ref,
):
    n_sky, half, chunk, extra = sizes
    bands, stamps, pix = pix_ref.shape
    size_k = tpl_ref.shape[1] // 2
    steps = [
        (b, slice(c * chunk, (c + 1) * chunk)) for b in range(bands) for c in range(pix // chunk)
    ]
    lane = iota((8, LANES), 1)
    for i in range(n_sky // 2):
        span = slice(i * LANES, (i + 1) * LANES)
        amp_ref[0:8, span] = jnp.exp(unfold(theta_ref, slice(None), lane, i, True))
        amp_ref[8:16, span] = jnp.exp(unfold(theta_ref, slice(None), lane, i, False))
    parts = jnp.concatenate(split3(amp_ref[...]), axis=0)
    got = dot(parts, hot_ref[...])
    mix = dot(parts, blend_ref[...])
    k1, k2, k3 = slice(0, size_k), slice(size_k, 2 * size_k), slice(2 * size_k, 3 * size_k)
    slot_f = got[k1] + (got[k2] + got[k3])
    high, low = mix[:, :stamps], mix[:, stamps:]
    slot_u = high[k1] + (high[k2] + low[k1] + (high[k3] + low[k2]))
    scaled = gain_ref[0:1, :] * slot_f
    lit_ref[...] = jnp.concatenate([scaled, slot_u], axis=0).T.astype(bf16)
    acc_ref[...] = jnp.zeros_like(acc_ref)
    proj_ref[...] = jnp.zeros_like(proj_ref)
    lit = lit_ref[...]
    base = jnp.concatenate([base_ref[...]] * (chunk // LANES), axis=1)
    wide = pair_ref.shape[1]

    def model(b, px):
        return dot(lit, tpl_ref[b, :, px])

    def weigh(b, px, light):
        resid = pix_ref[b, :, px].astype(f32) - light
        under = base + (resid * resid) * (1.0 / ROBUST)
        guess = pltpu.reciprocal(under, approx=True)
        weight = guess * (2.0 - under * guess)
        return weight.astype(bf16), (weight * resid).astype(bf16)

    def gather(b, px, weight, wres):
        acc_ref[:, 0:wide] += dot(weight, pair_ref[b, :, px], NT)
        proj_ref[:, 0:size_k] += dot(wres, tpl_ref[b, 0:size_k, px], NT)

    light = model(*steps[0])
    held = None
    for i, here in enumerate(steps):
        ahead = model(*steps[i + 1]) if i + 1 < len(steps) else None
        now = weigh(*here, light)
        if held is not None:
            gather(*steps[i - 1], *held)
        light, held = ahead, now
    gather(*steps[-1], *held)

    scales = dot(jnp.concatenate(split3(scaled), axis=0), wide_ref[...], TN)
    col = iota((1, 2 * LANES), 1) - (LANES + extra)
    is_grad = jnp.where((col >= 0) & (col < size_k), 1.0, 0.0)
    factor = scales[:, : 2 * LANES] * (scales[:, 2 * LANES :] + is_grad)
    tail = acc_ref[:, LANES:] + pltpu.roll(proj_ref[...], extra, 1)
    terms = jnp.concatenate(
        [
            factor[:, :LANES] * acc_ref[:, :LANES],
            factor[:, LANES:] * tail + tag_ref[...],
        ],
        axis=1,
    )
    t1, t2, t3 = split3(terms)
    sel = sel_ref[...]
    rows_ref[...] = dot(sel, t1) + (dot(sel, t2) + dot(sel, t3))
    groups = half // SUB
    for part, out_ref in enumerate((keep_ref, give_ref)):
        for d in range(n_sky):
            at = (part * n_sky + d) * half
            for g in range(groups):
                line = rows_ref[at + g * SUB : at + (g + 1) * SUB, :]
                out_ref[d, :, g * LANES : (g + 1) * LANES] = line[:, :LANES]
                more = pltpu.roll(line[:, LANES:], g * GROUP, 1) if g else line[:, LANES:]
                tail = tail + more if g else more
            out_ref[d, :, groups * LANES :] = tail


def solve_kernel(
    sizes,
    recv_ref,
    other_ref,
    member_in_ref,
    full_ref,
    theta_ref,
    init_ref,
    pay_ref,
    new_ref,
    member_ref,
    rows_ref,
):
    n_sky, half, n_band, tag, learn = sizes
    size_k, obj_dev = theta_ref.shape
    total = 2 * n_sky * half
    groups = half // SUB
    group = iota((SUB, LANES), 1) // GROUP
    first = jnp.full((SUB, LANES), lax.axis_index("band")) == 0
    for d in range(n_sky):
        for g in range(groups + 1):
            span = slice(g * LANES, (g + 1) * LANES)
            mine, others = recv_ref[d, :, span], other_ref[d, :, span]
            pair = (jnp.where(first, mine, others), jnp.where(first, others, mine))
            for part, line in enumerate(pair):
                at = (part * n_sky + d) * half
                if g < groups:
                    rows_ref[at + g * SUB : at + (g + 1) * SUB, 0:LANES] = line
                else:
                    for h in range(groups):
                        rows_ref[at + h * SUB : at + (h + 1) * SUB, LANES:] = jnp.where(
                            group == h, line, 0.0
                        )
    p1, p2, p3 = split3(rows_ref[...])
    if learn:
        where_tag = jnp.where(column((8, 2 * LANES), LANES + tag), 1.0, 0.0).astype(bf16)
        ids = dot(where_tag, p1, NT) + (dot(where_tag, p2, NT) + dot(where_tag, p3, NT))
        named = (iota((obj_dev, total), 0) + 1) * n_band
        hit = named == ids[0:1, :].astype(jnp.int32)
        member_ref[...] = jnp.where(hit, 1.0, 0.0).astype(bf16)
        member = member_ref[...]
    else:
        member = member_in_ref[...]
    sums = dot(member, p1) + (dot(member, p2) + dot(member, p3))
    q1, q2, q3 = split3(sums)
    full = full_ref[...]
    wide = dot(full, q1, NT) + (dot(full, q2, NT) + dot(full, q3, NT))
    row = iota((size_k, obj_dev), 0)
    theta = theta_ref[...]
    target = wide[size_k * size_k :] - PRIOR * (theta - init_ref[...])
    matrix = []
    for k in range(size_k):
        line = wide[k * size_k : (k + 1) * size_k]
        matrix.append(jnp.where(row == k, line + (DAMPING * line + PRIOR), line))
    inverse = []
    for p in range(size_k):
        line = matrix[p]
        inv = 1.0 / line[p : p + 1]
        inverse.append(inv)
        if p + 1 < size_k:
            scaled = jnp.where(row > p, line * inv, 0.0)
            target = target - scaled * target[p : p + 1]
            for k in range(p + 1, size_k):
                matrix[k] = matrix[k] - scaled * line[k : k + 1]
    delta = jnp.zeros_like(target)
    for p in reversed(range(size_k)):
        value = target[p : p + 1] * inverse[p]
        delta = jnp.where(row == p, value, delta)
        if p:
            target = target - matrix[p] * value
    new = theta + STEP_LIMIT * jnp.tanh(delta / STEP_LIMIT)
    new_ref[...] = new
    if pay_ref is not None:
        half = size_k // 2
        folded = jnp.concatenate([new[:half], new[half:]], axis=1)
        for d in range(n_sky):
            pay_ref[d] = folded


def hbm(x):
    return pltpu.with_memory_space_constraint(x, pltpu.HBM)


def call(kernel, out_shape, scratch=(), spaces=None):
    specs = {}
    if spaces:
        specs["in_specs"] = [
            pl.BlockSpec(memory_space=pltpu.HBM if s == "h" else pltpu.VMEM) for s in spaces
        ]
    return pl.pallas_call(
        kernel,
        out_shape=out_shape,
        scratch_shapes=list(scratch),
        compiler_params=pltpu.CompilerParams(vmem_limit_bytes=VMEM_LIMIT),
        **specs,
    )


def local(
    stamps,
    stamp_gain,
    stamp_invvar,
    stamp_dest,
    stamp_obj,
    phi_tpl,
    psi_tpl,
    theta_init,
    nb_id,
    nb_weight,
):
    n_sky = lax.axis_size("sky")
    n_band = lax.axis_size("band")
    stamp_dev, bands, pix = stamps.shape
    size_k, obj_dev = theta_init.shape
    nei = nb_id.shape[1]
    cap = 2 * stamp_dev // n_sky
    half = cap // 2
    total = n_sky * cap
    n_all = n_sky * obj_dev
    extra = size_k * (size_k + 1) // 2 - LANES
    wide = LANES + -(-extra // 16) * 16
    assert n_band == 2 and half % SUB == 0 and half // SUB <= LANES // GROUP
    assert 2 * obj_dev == LANES and 0 <= extra and extra + size_k < GROUP
    shape = jax.ShapeDtypeStruct
    chunk = max(c for c in range(LANES, 1024, LANES) if pix % c == 0)

    pixels = jnp.transpose(stamps, (1, 0, 2))
    payload, pixels, tpl, pair, sel, spread, full, base, tag, gain, owner = call(
        functools.partial(ready_kernel, (n_sky, cap, obj_dev, extra, chunk)),
        (
            shape((n_sky, 16, LANES), f32),
            shape((bands, stamp_dev, pix), bf16),
            shape((bands, 2 * size_k, pix), bf16),
            shape((bands, wide, pix), bf16),
            shape((total, stamp_dev), bf16),
            shape((3 * size_k, 4 * LANES), bf16),
            shape((size_k * size_k + size_k, 2 * LANES), bf16),
            shape((stamp_dev, LANES), f32),
            shape((stamp_dev, LANES), f32),
            shape((8, stamp_dev), f32),
            shape((8, stamp_dev), jnp.int32),
        ),
        [
            pltpu.VMEM((1, stamp_dev), jnp.int32),
            pltpu.VMEM((1, stamp_dev), jnp.int32),
            pltpu.VMEM((stamp_dev,), bf16),
            pltpu.VMEM((stamp_dev,), bf16),
            pltpu.VMEM((size_k, obj_dev), f32),
            pltpu.VMEM((nei, obj_dev), jnp.int32),
            pltpu.VMEM((nei, obj_dev), f32),
            pltpu.SemaphoreType.DMA((10,)),
        ],
        "h" * 10,
    )(
        hbm(stamp_dest.T),
        hbm(stamp_obj[None, :]),
        hbm(stamp_gain),
        hbm(stamp_invvar),
        hbm(phi_tpl),
        hbm(psi_tpl),
        hbm(theta_init),
        hbm(nb_id.T),
        hbm(nb_weight.T),
        hbm(pixels),
    )
    got = lax.all_to_all(payload, "sky", 0, 0, tiled=True)
    everyone, hot, blend = call(
        functools.partial(index_kernel, nei),
        (
            shape((n_sky, 8, LANES), f32),
            shape((n_all, stamp_dev), bf16),
            shape((n_all, 2 * stamp_dev), bf16),
        ),
        [pltpu.VMEM((16, n_all), f32)],
    )(got, owner)
    terms = call(
        functools.partial(terms_kernel, (n_sky, half, chunk, extra)),
        [shape((n_sky, SUB, (half // SUB + 1) * LANES), f32)] * 2,
        [
            pltpu.VMEM((size_k, n_all), f32),
            pltpu.VMEM((stamp_dev, 2 * LANES), f32),
            pltpu.VMEM((stamp_dev, LANES), f32),
            pltpu.VMEM((stamp_dev, 2 * size_k), bf16),
            pltpu.VMEM((total, 2 * LANES), f32),
        ],
    )
    swap = [(0, 1), (1, 0)]
    theta = theta_init
    member = None
    for sweep in range(ITERS):
        keep, give = terms(
            everyone, hot, blend, gain, base, tag, pixels, tpl, pair, sel, spread
        )
        sent = keep + lax.ppermute(give, "band", swap)
        recv = lax.all_to_all(sent, "sky", 0, 0, tiled=True)
        other = lax.ppermute(recv, "band", swap)
        learn, last = sweep == 0, sweep + 1 == ITERS
        sizes = (n_sky, half, n_band, extra + size_k, learn)

        def solve(*refs, learn=learn, last=last, sizes=sizes):
            refs = list(refs)
            if learn:
                refs.insert(2, None)
            if last:
                refs.insert(6, None)
            if not learn:
                refs.insert(8, None)
            solve_kernel(sizes, *refs)

        outs = [shape((n_sky, 8, LANES), f32)] * (not last)
        outs += [shape((size_k, obj_dev), f32)]
        outs += [shape((obj_dev, total), bf16)] * learn
        given = [recv, other] + [member] * (not learn) + [full, theta, theta_init]
        outs = call(solve, outs, [pltpu.VMEM((total, 2 * LANES), f32)])(*given)
        theta = outs[0 if last else 1]
        if learn:
            member = outs[-1]
        if not last:
            everyone = lax.all_to_all(outs[0], "sky", 0, 0, tiled=True)
    return theta


def solution(mesh):
    in_specs = (
        P("sky", "band", None),
        P("sky"),
        P("sky"),
        P("sky", None),
        P("sky"),
        P("band", None, None),
        P("band", None, None),
        P(None, "sky"),
        P("sky", None),
        P("sky", None),
    )
    out_specs = P(None, "sky")
    return jax.shard_map(local, mesh=mesh, in_specs=in_specs, out_specs=out_specs, check_vma=False)
```

```python
import functools

import jax
import jax.numpy as jnp
from jax import lax
from jax.experimental import pallas as pl
from jax.experimental.pallas import tpu as pltpu
from jax.sharding import PartitionSpec as P

ITERS = 3

ROBUST = 9.0
DAMPING = 0.1
PRIOR = 1.0
STEP_LIMIT = 0.5

LANES = 128
GROUP = 32
SUB = 4
VMEM_LIMIT = 24 * 1024 * 1024

f32 = jnp.float32
bf16 = jnp.bfloat16
NT = (((1,), (1,)), ((), ()))
TN = (((0,), (0,)), ((), ()))
NN = (((1,), (0,)), ((), ()))


def dot(a, b, dims=NN, precision=None):
    return lax.dot_general(a, b, dims, precision=precision, preferred_element_type=f32)


def split3(x):
    first = x.astype(bf16)
    rest = x - first.astype(f32)
    second = rest.astype(bf16)
    third = (rest - second.astype(f32)).astype(bf16)
    return first, second, third


def iota(shape, dim):
    return lax.broadcasted_iota(jnp.int32, shape, dim)


def dma(copies):
    for copy in copies:
        copy.start()
    return copies


def wait(copies):
    for copy in copies:
        copy.wait()


def offset(k, size_k):
    return lax.div(k * (2 * size_k + 1 - k), 2)


def column(shape, m):
    lane = iota(shape, 1)
    folded = jnp.where(lane < LANES, lane, LANES + lax.rem(lane, GROUP))
    return folded == m


def ready_kernel(
    sizes,
    dest_hbm,
    obj_hbm,
    gain_hbm,
    invvar_hbm,
    phi_hbm,
    psi_hbm,
    theta_hbm,
    nbi_hbm,
    nbw_hbm,
    pix_hbm,
    pay_ref,
    pix_ref,
    tpl_ref,
    pair_ref,
    sel_ref,
    wide_ref,
    full_ref,
    base_ref,
    tag_ref,
    gain_ref,
    owner_ref,
    dest_ref,
    obj_ref,
    gain_low_ref,
    invvar_ref,
    theta_ref,
    nbi_ref,
    nbw_ref,
    sem,
):
    n_sky, cap, obj_dev, extra, chunk = sizes
    bands, size_k, pix = phi_hbm.shape
    stamps = dest_ref.shape[1]
    total = n_sky * cap
    first = [
        pltpu.make_async_copy(phi_hbm, tpl_ref.at[:, 0:size_k, :], sem.at[0]),
        pltpu.make_async_copy(psi_hbm, tpl_ref.at[:, size_k : 2 * size_k, :], sem.at[1]),
        pltpu.make_async_copy(dest_hbm, dest_ref, sem.at[2]),
        pltpu.make_async_copy(obj_hbm, obj_ref, sem.at[3]),
        pltpu.make_async_copy(gain_hbm, gain_low_ref, sem.at[4]),
        pltpu.make_async_copy(invvar_hbm, invvar_ref, sem.at[5]),
        pltpu.make_async_copy(theta_hbm, theta_ref, sem.at[6]),
        pltpu.make_async_copy(nbi_hbm, nbi_ref, sem.at[7]),
        pltpu.make_async_copy(nbw_hbm, nbw_ref, sem.at[8]),
    ]
    last = [pltpu.make_async_copy(pix_hbm, pix_ref, sem.at[9])]
    dma(first)
    dma(last)

    pairs = LANES + extra
    shape = (pair_ref.shape[1], size_k)
    m = iota(shape, 0)
    k = iota(shape, 1)
    lows = jnp.where((m >= offset(k, size_k)) & (m < offset(k + 1, size_k)), 1.0, 0.0)
    of_m = jnp.sum(lows * k.astype(f32), axis=1, keepdims=True).astype(jnp.int32)
    highs = jnp.where((m < pairs) & (m - offset(of_m, size_k) + of_m == k), 1.0, 0.0)
    lows, highs = lows.astype(bf16), highs.astype(bf16)

    shape = (size_k, 2 * LANES)
    k = iota(shape, 0)
    lane = iota(shape, 1)
    spot = pairs + k
    left = (lane >= offset(k, size_k)) & (lane < offset(k + 1, size_k))
    left = jnp.where(left | (lane == spot), 1.0, 0.0)
    lane_k = jnp.sum(jnp.where(lane >= offset(k + 1, size_k), 1, 0), axis=0, keepdims=True)
    right = (lane[0:1] - offset(lane_k, size_k) + lane_k == k) & (lane < pairs)
    both = jnp.concatenate([left, jnp.where(right, 1.0, 0.0)], axis=1).astype(bf16)
    for part in range(3):
        wide_ref[part * size_k : (part + 1) * size_k, :] = both

    shape = full_ref.shape
    r = iota((shape[0], 1), 0)
    a, b = lax.div(r, size_k), lax.rem(r, size_k)
    low, high = jnp.minimum(a, b), jnp.maximum(a, b)
    m = jnp.where(r < size_k * size_k, offset(low, size_k) + high - low, pairs + b)
    full_ref[...] = jnp.where(column(shape, m), 1.0, 0.0).astype(bf16)

    wait(first)
    theta = theta_ref[...]
    folded = jnp.concatenate([theta[: size_k // 2], theta[size_k // 2 :]], axis=1)
    side = jnp.concatenate([nbi_ref[...].astype(f32), nbw_ref[...]], axis=1)
    side = jnp.concatenate([side, jnp.zeros((8 - side.shape[0], LANES), f32)], axis=0)
    for d in range(n_sky):
        pay_ref[d, 0:8, :] = folded
        pay_ref[d, 8:16, :] = side
    dest = dest_ref[...]
    obj = obj_ref[...]
    gain = gain_low_ref[...].astype(f32).reshape(1, stamps)
    gain_ref[...] = jnp.broadcast_to(gain, gain_ref.shape)
    variance = 1.0 / invvar_ref[...].astype(f32).reshape(1, stamps)
    base_ref[...] = jnp.broadcast_to(variance, (LANES, stamps)).T
    named = jnp.broadcast_to((obj + 1).astype(f32), (LANES, stamps)).T
    tag_ref[...] = jnp.where(
        iota((stamps, LANES), 1) == extra + size_k, named, 0.0
    )
    along = jnp.broadcast_to(dest.astype(f32), (stamps, stamps))
    before = iota((stamps, stamps), 0) < iota((stamps, stamps), 1)
    rank = jnp.sum(jnp.where(before & (along == along.T), 1.0, 0.0), axis=0, keepdims=True)
    owner_ref[...] = jnp.broadcast_to(dest * obj_dev + obj, owner_ref.shape)
    half = cap // 2
    rank = rank.astype(jnp.int32)
    given = jnp.where(rank >= half, 1, 0) != lax.axis_index("band")
    place = (dest + jnp.where(given, n_sky, 0)) * half + lax.rem(rank, half)
    sel_ref[...] = jnp.where(iota((total, stamps), 0) == place, 1.0, 0.0).astype(bf16)
    for b in range(bands):
        for c in range(pix // chunk):
            px = slice(c * chunk, (c + 1) * chunk)
            phi = tpl_ref[b, 0:size_k, px]
            pair_ref[b, :, px] = (dot(lows, phi) * dot(highs, phi)).astype(bf16)
    wait(last)


def unfold(ref, rows, lane, i, left):
    x, y = ref[2 * i, rows, :], ref[2 * i + 1, rows, :]
    if left:
        return jnp.where(lane < LANES // 2, x, pltpu.roll(y, LANES // 2, 1))
    return jnp.where(lane < LANES // 2, pltpu.roll(x, LANES // 2, 1), y)


def index_kernel(nei, got_ref, owner_ref, theta_ref, hot_ref, blend_ref, table_ref):
    n_sky = got_ref.shape[0]
    n_all, stamps = hot_ref.shape
    block = LANES
    owner = owner_ref[0:1, :]

    def hot(i, carry):
        rows = pl.ds(pl.multiple_of(i * block, block), block)
        hit = iota((block, stamps), 0) + i * block == owner
        hot_ref[rows, :] = jnp.where(hit, 1.0, 0.0).astype(bf16)
        return carry

    lax.fori_loop(0, n_all // block, hot, 0)
    lane = iota((8, LANES), 1)
    for d in range(n_sky):
        theta_ref[d] = got_ref[d, 0:8, :]
    for i in range(n_sky // 2):
        span = slice(i * LANES, (i + 1) * LANES)
        table_ref[0:8, span] = unfold(got_ref, slice(8, 16), lane, i, True)
        table_ref[8:16, span] = unfold(got_ref, slice(8, 16), lane, i, False)
    parts = jnp.concatenate(split3(table_ref[...]), axis=0)
    found = dot(parts, hot_ref[...])
    found = found[0:16] + found[16:32] + found[32:48]
    near_id = found[0:nei].astype(jnp.int32)
    near_w = found[8 : 8 + nei]

    def blend(i, carry):
        rows = pl.ds(pl.multiple_of(i * block, block), block)
        here = iota((block, stamps), 0) + i * block
        mix = jnp.zeros((block, stamps), f32)
        for j in range(nei):
            mix = mix + jnp.where(here == near_id[j : j + 1], near_w[j : j + 1], 0.0)
        high = mix.astype(bf16)
        blend_ref[rows, 0:stamps] = high
        blend_ref[rows, stamps : 2 * stamps] = (mix - high.astype(f32)).astype(bf16)
        return carry

    lax.fori_loop(0, n_all // block, blend, 0)


def terms_kernel(
    sizes,
    theta_ref,
    hot_ref,
    blend_ref,
    gain_ref,
    base_ref,
    tag_ref,
    pix_ref,
    tpl_ref,
    pair_ref,
    sel_ref,
    wide_ref,
    keep_ref,
    give_ref,
    amp_ref,
    acc_ref,
    proj_ref,
    lit_ref,
    rows_ref,
):
    n_sky, half, chunk, extra = sizes
    bands, stamps, pix = pix_ref.shape
    size_k = tpl_ref.shape[1] // 2
    steps = [
        (b, slice(c * chunk, (c + 1) * chunk)) for b in range(bands) for c in range(pix // chunk)
    ]
    lane = iota((8, LANES), 1)
    for i in range(n_sky // 2):
        span = slice(i * LANES, (i + 1) * LANES)
        amp_ref[0:8, span] = jnp.exp(unfold(theta_ref, slice(None), lane, i, True))
        amp_ref[8:16, span] = jnp.exp(unfold(theta_ref, slice(None), lane, i, False))
    parts = jnp.concatenate(split3(amp_ref[...]), axis=0)
    got = dot(parts, hot_ref[...])
    mix = dot(parts, blend_ref[...])
    k1, k2, k3 = slice(0, size_k), slice(size_k, 2 * size_k), slice(2 * size_k, 3 * size_k)
    slot_f = got[k1] + (got[k2] + got[k3])
    high, low = mix[:, :stamps], mix[:, stamps:]
    slot_u = high[k1] + (high[k2] + low[k1] + (high[k3] + low[k2]))
    scaled = gain_ref[0:1, :] * slot_f
    lit_ref[...] = jnp.concatenate([scaled, slot_u], axis=0).T.astype(bf16)
    acc_ref[...] = jnp.zeros_like(acc_ref)
    proj_ref[...] = jnp.zeros_like(proj_ref)
    lit = lit_ref[...]
    base = jnp.concatenate([base_ref[...]] * (chunk // LANES), axis=1)
    wide = pair_ref.shape[1]

    def model(b, px):
        return dot(lit, tpl_ref[b, :, px])

    def weigh(b, px, light):
        resid = pix_ref[b, :, px].astype(f32) - light
        under = base + (resid * resid) * (1.0 / ROBUST)
        guess = pltpu.reciprocal(under, approx=True)
        weight = guess * (2.0 - under * guess)
        return weight.astype(bf16), (weight * resid).astype(bf16)

    def gather(b, px, weight, wres):
        acc_ref[:, 0:wide] += dot(weight, pair_ref[b, :, px], NT)
        proj_ref[...] += dot(tpl_ref[b, 0:size_k, px], wres, NT)

    light = model(*steps[0])
    held = None
    for i, here in enumerate(steps):
        ahead = model(*steps[i + 1]) if i + 1 < len(steps) else None
        now = weigh(*here, light)
        if held is not None:
            gather(*steps[i - 1], *held)
        light, held = ahead, now
    gather(*steps[-1], *held)

    scales = dot(jnp.concatenate(split3(scaled), axis=0), wide_ref[...], TN)
    col = iota((1, 2 * LANES), 1) - (LANES + extra)
    is_grad = jnp.where((col >= 0) & (col < size_k), 1.0, 0.0)
    factor = scales[:, : 2 * LANES] * (scales[:, 2 * LANES :] + is_grad)
    proj = jnp.concatenate([jnp.zeros((extra, stamps), f32), proj_ref[...]], axis=0)
    proj = jnp.concatenate([proj, jnp.zeros((LANES - extra - size_k, stamps), f32)], axis=0)
    tail = acc_ref[:, LANES:] + proj.T
    terms = jnp.concatenate(
        [
            factor[:, :LANES] * acc_ref[:, :LANES],
            factor[:, LANES:] * tail + tag_ref[...],
        ],
        axis=1,
    )
    sel = sel_ref[...]
    t1, t2, t3 = split3(terms)
    rows_ref[...] = dot(sel, t1) + (dot(sel, t2) + dot(sel, t3))
    groups = half // SUB
    for part, out_ref in enumerate((keep_ref, give_ref)):
        for d in range(n_sky):
            at = (part * n_sky + d) * half
            for g in range(groups):
                line = rows_ref[at + g * SUB : at + (g + 1) * SUB, :]
                out_ref[d, :, g * LANES : (g + 1) * LANES] = line[:, :LANES]
                more = pltpu.roll(line[:, LANES:], g * GROUP, 1) if g else line[:, LANES:]
                tail = tail + more if g else more
            out_ref[d, :, groups * LANES :] = tail


def solve_kernel(
    sizes,
    recv_ref,
    other_ref,
    member_in_ref,
    full_ref,
    theta_ref,
    init_ref,
    pay_ref,
    new_ref,
    member_ref,
    rows_ref,
):
    n_sky, half, n_band, tag, learn = sizes
    size_k, obj_dev = theta_ref.shape
    total = 2 * n_sky * half
    groups = half // SUB
    group = iota((SUB, LANES), 1) // GROUP
    first = jnp.full((SUB, LANES), lax.axis_index("band")) == 0
    for d in range(n_sky):
        for g in range(groups + 1):
            span = slice(g * LANES, (g + 1) * LANES)
            mine, others = recv_ref[d, :, span], other_ref[d, :, span]
            pair = (jnp.where(first, mine, others), jnp.where(first, others, mine))
            for part, line in enumerate(pair):
                at = (part * n_sky + d) * half
                if g < groups:
                    rows_ref[at + g * SUB : at + (g + 1) * SUB, 0:LANES] = line
                else:
                    for h in range(groups):
                        rows_ref[at + h * SUB : at + (h + 1) * SUB, LANES:] = jnp.where(
                            group == h, line, 0.0
                        )
    p1, p2, p3 = split3(rows_ref[...])
    if learn:
        where_tag = jnp.where(column((8, 2 * LANES), LANES + tag), 1.0, 0.0).astype(bf16)
        ids = dot(where_tag, p1, NT) + (dot(where_tag, p2, NT) + dot(where_tag, p3, NT))
        named = (iota((obj_dev, total), 0) + 1) * n_band
        hit = named == ids[0:1, :].astype(jnp.int32)
        member_ref[...] = jnp.where(hit, 1.0, 0.0).astype(bf16)
        member = member_ref[...]
    else:
        member = member_in_ref[...]
    sums = dot(member, p1) + (dot(member, p2) + dot(member, p3))
    q1, q2, q3 = split3(sums)
    full = full_ref[...]
    wide = dot(full, q1, NT) + (dot(full, q2, NT) + dot(full, q3, NT))
    row = iota((size_k, obj_dev), 0)
    theta = theta_ref[...]
    target = wide[size_k * size_k :] - PRIOR * (theta - init_ref[...])
    matrix = []
    for k in range(size_k):
        line = wide[k * size_k : (k + 1) * size_k]
        matrix.append(jnp.where(row == k, line + (DAMPING * line + PRIOR), line))
    inverse = []
    for p in range(size_k):
        line = matrix[p]
        inv = 1.0 / line[p : p + 1]
        inverse.append(inv)
        if p + 1 < size_k:
            scaled = jnp.where(row > p, line * inv, 0.0)
            target = target - scaled * target[p : p + 1]
            for k in range(p + 1, size_k):
                matrix[k] = matrix[k] - scaled * line[k : k + 1]
    delta = jnp.zeros_like(target)
    for p in reversed(range(size_k)):
        value = target[p : p + 1] * inverse[p]
        delta = jnp.where(row == p, value, delta)
        if p:
            target = target - matrix[p] * value
    new = theta + STEP_LIMIT * jnp.tanh(delta / STEP_LIMIT)
    new_ref[...] = new
    if pay_ref is not None:
        half = size_k // 2
        folded = jnp.concatenate([new[:half], new[half:]], axis=1)
        for d in range(n_sky):
            pay_ref[d] = folded


def hbm(x):
    return pltpu.with_memory_space_constraint(x, pltpu.HBM)


def call(kernel, out_shape, scratch=(), spaces=None, flags=None):
    specs = {}
    if spaces:
        specs["in_specs"] = [
            pl.BlockSpec(memory_space=pltpu.HBM if s == "h" else pltpu.VMEM) for s in spaces
        ]
    return pl.pallas_call(
        kernel,
        out_shape=out_shape,
        scratch_shapes=list(scratch),
        compiler_params=pltpu.CompilerParams(vmem_limit_bytes=VMEM_LIMIT, flags=flags),
        **specs,
    )


def local(
    stamps,
    stamp_gain,
    stamp_invvar,
    stamp_dest,
    stamp_obj,
    phi_tpl,
    psi_tpl,
    theta_init,
    nb_id,
    nb_weight,
):
    n_sky = lax.axis_size("sky")
    n_band = lax.axis_size("band")
    stamp_dev, bands, pix = stamps.shape
    size_k, obj_dev = theta_init.shape
    nei = nb_id.shape[1]
    cap = 2 * stamp_dev // n_sky
    half = cap // 2
    total = n_sky * cap
    n_all = n_sky * obj_dev
    extra = size_k * (size_k + 1) // 2 - LANES
    wide = LANES + -(-extra // 16) * 16
    assert n_band == 2 and half % SUB == 0 and half // SUB <= LANES // GROUP
    assert 2 * obj_dev == LANES and 0 <= extra and extra + size_k < GROUP
    shape = jax.ShapeDtypeStruct
    wide_chunk = max(c for c in range(LANES, 1024, LANES) if pix % c == 0)
    chunk = max(c for c in range(LANES, 384, LANES) if pix % c == 0)

    pixels = jnp.transpose(stamps, (1, 0, 2))
    payload, pixels, tpl, pair, sel, spread, full, base, tag, gain, owner = call(
        functools.partial(ready_kernel, (n_sky, cap, obj_dev, extra, wide_chunk)),
        (
            shape((n_sky, 16, LANES), f32),
            shape((bands, stamp_dev, pix), bf16),
            shape((bands, 2 * size_k, pix), bf16),
            shape((bands, wide, pix), bf16),
            shape((total, stamp_dev), bf16),
            shape((3 * size_k, 4 * LANES), bf16),
            shape((size_k * size_k + size_k, 2 * LANES), bf16),
            shape((stamp_dev, LANES), f32),
            shape((stamp_dev, LANES), f32),
            shape((8, stamp_dev), f32),
            shape((8, stamp_dev), jnp.int32),
        ),
        [
            pltpu.VMEM((1, stamp_dev), jnp.int32),
            pltpu.VMEM((1, stamp_dev), jnp.int32),
            pltpu.VMEM((stamp_dev,), bf16),
            pltpu.VMEM((stamp_dev,), bf16),
            pltpu.VMEM((size_k, obj_dev), f32),
            pltpu.VMEM((nei, obj_dev), jnp.int32),
            pltpu.VMEM((nei, obj_dev), f32),
            pltpu.SemaphoreType.DMA((10,)),
        ],
        "h" * 10,
    )(
        hbm(stamp_dest.T),
        hbm(stamp_obj[None, :]),
        hbm(stamp_gain),
        hbm(stamp_invvar),
        hbm(phi_tpl),
        hbm(psi_tpl),
        hbm(theta_init),
        hbm(nb_id.T),
        hbm(nb_weight.T),
        hbm(pixels),
    )
    got = lax.all_to_all(payload, "sky", 0, 0, tiled=True)
    everyone, hot, blend = call(
        functools.partial(index_kernel, nei),
        (
            shape((n_sky, 8, LANES), f32),
            shape((n_all, stamp_dev), bf16),
            shape((n_all, 2 * stamp_dev), bf16),
        ),
        [pltpu.VMEM((16, n_all), f32)],
    )(got, owner)
    terms = call(
        functools.partial(terms_kernel, (n_sky, half, chunk, extra)),
        [shape((n_sky, SUB, (half // SUB + 1) * LANES), f32)] * 2,
        [
            pltpu.VMEM((size_k, n_all), f32),
            pltpu.VMEM((stamp_dev, 2 * LANES), f32),
            pltpu.VMEM((size_k, stamp_dev), f32),
            pltpu.VMEM((stamp_dev, 2 * size_k), bf16),
            pltpu.VMEM((total, 2 * LANES), f32),
        ],
    )
    swap = [(0, 1), (1, 0)]
    theta = theta_init
    member = None
    for sweep in range(ITERS):
        keep, give = terms(
            everyone, hot, blend, gain, base, tag, pixels, tpl, pair, sel, spread
        )
        sent = keep + lax.ppermute(give, "band", swap)
        recv = lax.all_to_all(sent, "sky", 0, 0, tiled=True)
        other = lax.ppermute(recv, "band", swap)
        learn, last = sweep == 0, sweep + 1 == ITERS
        sizes = (n_sky, half, n_band, extra + size_k, learn)

        def solve(*refs, learn=learn, last=last, sizes=sizes):
            refs = list(refs)
            if learn:
                refs.insert(2, None)
            if last:
                refs.insert(6, None)
            if not learn:
                refs.insert(8, None)
            solve_kernel(sizes, *refs)

        outs = [shape((n_sky, 8, LANES), f32)] * (not last)
        outs += [shape((size_k, obj_dev), f32)]
        outs += [shape((obj_dev, total), bf16)] * learn
        given = [recv, other] + [member] * (not learn) + [full, theta, theta_init]
        outs = call(solve, outs, [pltpu.VMEM((total, 2 * LANES), f32)])(*given)
        theta = outs[0 if last else 1]
        if learn:
            member = outs[-1]
        if not last:
            everyone = lax.all_to_all(outs[0], "sky", 0, 0, tiled=True)
    return theta


def solution(mesh):
    in_specs = (
        P("sky", "band", None),
        P("sky"),
        P("sky"),
        P("sky", None),
        P("sky"),
        P("band", None, None),
        P("band", None, None),
        P(None, "sky"),
        P("sky", None),
        P("sky", None),
    )
    out_specs = P(None, "sky")
    return jax.shard_map(local, mesh=mesh, in_specs=in_specs, out_specs=out_specs, check_vma=False)
```

```python
import functools

import jax
import jax.numpy as jnp
from jax import lax
from jax.experimental import pallas as pl
from jax.experimental.pallas import tpu as pltpu
from jax.sharding import PartitionSpec as P

ITERS = 3

ROBUST = 9.0
DAMPING = 0.1
PRIOR = 1.0
STEP_LIMIT = 0.5

LANES = 128
GROUP = 32
SUB = 4
VMEM_LIMIT = 24 * 1024 * 1024

f32 = jnp.float32
bf16 = jnp.bfloat16
NT = (((1,), (1,)), ((), ()))
TN = (((0,), (0,)), ((), ()))
NN = (((1,), (0,)), ((), ()))


def dot(a, b, dims=NN, precision=None):
    return lax.dot_general(a, b, dims, precision=precision, preferred_element_type=f32)


def split3(x):
    first = x.astype(bf16)
    rest = x - first.astype(f32)
    second = rest.astype(bf16)
    third = (rest - second.astype(f32)).astype(bf16)
    return first, second, third


def iota(shape, dim):
    return lax.broadcasted_iota(jnp.int32, shape, dim)


def dma(copies):
    for copy in copies:
        copy.start()
    return copies


def wait(copies):
    for copy in copies:
        copy.wait()


def offset(k, size_k):
    return lax.div(k * (2 * size_k + 1 - k), 2)


def column(shape, m):
    lane = iota(shape, 1)
    folded = jnp.where(lane < LANES, lane, LANES + lax.rem(lane, GROUP))
    return folded == m


def ready_kernel(
    sizes,
    dest_hbm,
    obj_hbm,
    gain_hbm,
    invvar_hbm,
    phi_hbm,
    psi_hbm,
    theta_hbm,
    nbi_hbm,
    nbw_hbm,
    pix_hbm,
    pay_ref,
    pix_ref,
    tpl_ref,
    pair_ref,
    sel_ref,
    wide_ref,
    full_ref,
    base_ref,
    tag_ref,
    gain_ref,
    owner_ref,
    dest_ref,
    obj_ref,
    gain_low_ref,
    invvar_ref,
    theta_ref,
    nbi_ref,
    nbw_ref,
    sem,
):
    n_sky, cap, obj_dev, extra, chunk = sizes
    bands, size_k, pix = phi_hbm.shape
    stamps = dest_ref.shape[1]
    total = n_sky * cap
    first = [
        pltpu.make_async_copy(phi_hbm, tpl_ref.at[:, 0:size_k, :], sem.at[0]),
        pltpu.make_async_copy(psi_hbm, tpl_ref.at[:, size_k : 2 * size_k, :], sem.at[1]),
        pltpu.make_async_copy(dest_hbm, dest_ref, sem.at[2]),
        pltpu.make_async_copy(obj_hbm, obj_ref, sem.at[3]),
        pltpu.make_async_copy(gain_hbm, gain_low_ref, sem.at[4]),
        pltpu.make_async_copy(invvar_hbm, invvar_ref, sem.at[5]),
        pltpu.make_async_copy(theta_hbm, theta_ref, sem.at[6]),
        pltpu.make_async_copy(nbi_hbm, nbi_ref, sem.at[7]),
        pltpu.make_async_copy(nbw_hbm, nbw_ref, sem.at[8]),
    ]
    last = [pltpu.make_async_copy(pix_hbm.at[0 : pix_ref.shape[0]], pix_ref, sem.at[9])]
    dma(first)
    dma(last)

    pairs = LANES + extra
    shape = (pair_ref.shape[1], size_k)
    m = iota(shape, 0)
    k = iota(shape, 1)
    lows = jnp.where((m >= offset(k, size_k)) & (m < offset(k + 1, size_k)), 1.0, 0.0)
    of_m = jnp.sum(lows * k.astype(f32), axis=1, keepdims=True).astype(jnp.int32)
    highs = jnp.where((m < pairs) & (m - offset(of_m, size_k) + of_m == k), 1.0, 0.0)
    lows, highs = lows.astype(bf16), highs.astype(bf16)

    shape = (size_k, 2 * LANES)
    k = iota(shape, 0)
    lane = iota(shape, 1)
    spot = pairs + k
    left = (lane >= offset(k, size_k)) & (lane < offset(k + 1, size_k))
    left = jnp.where(left | (lane == spot), 1.0, 0.0)
    lane_k = jnp.sum(jnp.where(lane >= offset(k + 1, size_k), 1, 0), axis=0, keepdims=True)
    right = (lane[0:1] - offset(lane_k, size_k) + lane_k == k) & (lane < pairs)
    both = jnp.concatenate([left, jnp.where(right, 1.0, 0.0)], axis=1).astype(bf16)
    for part in range(3):
        wide_ref[part * size_k : (part + 1) * size_k, :] = both

    shape = full_ref.shape
    r = iota((shape[0], 1), 0)
    a, b = lax.div(r, size_k), lax.rem(r, size_k)
    low, high = jnp.minimum(a, b), jnp.maximum(a, b)
    m = jnp.where(r < size_k * size_k, offset(low, size_k) + high - low, pairs + b)
    full_ref[...] = jnp.where(column(shape, m), 1.0, 0.0).astype(bf16)

    wait(first)
    theta = theta_ref[...]
    folded = jnp.concatenate([theta[: size_k // 2], theta[size_k // 2 :]], axis=1)
    side = jnp.concatenate([nbi_ref[...].astype(f32), nbw_ref[...]], axis=1)
    side = jnp.concatenate([side, jnp.zeros((8 - side.shape[0], LANES), f32)], axis=0)
    for d in range(n_sky):
        pay_ref[d, 0:8, :] = folded
        pay_ref[d, 8:16, :] = side
    dest = dest_ref[...]
    obj = obj_ref[...]
    gain = gain_low_ref[...].astype(f32).reshape(1, stamps)
    gain_ref[...] = jnp.broadcast_to(gain, gain_ref.shape)
    variance = 1.0 / invvar_ref[...].astype(f32).reshape(1, stamps)
    base_ref[...] = jnp.broadcast_to(variance, (LANES, stamps)).T
    named = jnp.broadcast_to((obj + 1).astype(f32), (LANES, stamps)).T
    tag_ref[...] = jnp.where(
        iota((stamps, LANES), 1) == extra + size_k, named, 0.0
    )
    along = jnp.broadcast_to(dest.astype(f32), (stamps, stamps))
    before = iota((stamps, stamps), 0) < iota((stamps, stamps), 1)
    rank = jnp.sum(jnp.where(before & (along == along.T), 1.0, 0.0), axis=0, keepdims=True)
    owner_ref[...] = jnp.broadcast_to(dest * obj_dev + obj, owner_ref.shape)
    half = cap // 2
    rank = rank.astype(jnp.int32)
    given = jnp.where(rank >= half, 1, 0) != lax.axis_index("band")
    place = (dest + jnp.where(given, n_sky, 0)) * half + lax.rem(rank, half)
    sel_ref[...] = jnp.where(iota((total, stamps), 0) == place, 1.0, 0.0).astype(bf16)
    for b in range(bands):
        for c in range(pix // chunk):
            px = slice(c * chunk, (c + 1) * chunk)
            phi = tpl_ref[b, 0:size_k, px]
            pair_ref[b, :, px] = (dot(lows, phi) * dot(highs, phi)).astype(bf16)
    wait(last)


def unfold(ref, rows, lane, i, left):
    x, y = ref[2 * i, rows, :], ref[2 * i + 1, rows, :]
    if left:
        return jnp.where(lane < LANES // 2, x, pltpu.roll(y, LANES // 2, 1))
    return jnp.where(lane < LANES // 2, pltpu.roll(x, LANES // 2, 1), y)


def index_kernel(
    nei, got_ref, owner_ref, pix_hbm, theta_ref, hot_ref, blend_ref, pix_ref, table_ref, sem
):
    from_band = pix_hbm.shape[0] - pix_ref.shape[0]
    load = dma([pltpu.make_async_copy(pix_hbm.at[from_band:], pix_ref, sem)])
    n_sky = got_ref.shape[0]
    n_all, stamps = hot_ref.shape
    block = LANES
    owner = owner_ref[0:1, :]

    def hot(i, carry):
        rows = pl.ds(pl.multiple_of(i * block, block), block)
        hit = iota((block, stamps), 0) + i * block == owner
        hot_ref[rows, :] = jnp.where(hit, 1.0, 0.0).astype(bf16)
        return carry

    lax.fori_loop(0, n_all // block, hot, 0)
    lane = iota((8, LANES), 1)
    for d in range(n_sky):
        theta_ref[d] = got_ref[d, 0:8, :]
    for i in range(n_sky // 2):
        span = slice(i * LANES, (i + 1) * LANES)
        table_ref[0:8, span] = unfold(got_ref, slice(8, 16), lane, i, True)
        table_ref[8:16, span] = unfold(got_ref, slice(8, 16), lane, i, False)
    parts = jnp.concatenate(split3(table_ref[...]), axis=0)
    found = dot(parts, hot_ref[...])
    found = found[0:16] + found[16:32] + found[32:48]
    near_id = found[0:nei].astype(jnp.int32)
    near_w = found[8 : 8 + nei]

    def blend(i, carry):
        rows = pl.ds(pl.multiple_of(i * block, block), block)
        here = iota((block, stamps), 0) + i * block
        mix = jnp.zeros((block, stamps), f32)
        for j in range(nei):
            mix = mix + jnp.where(here == near_id[j : j + 1], near_w[j : j + 1], 0.0)
        high = mix.astype(bf16)
        blend_ref[rows, 0:stamps] = high
        blend_ref[rows, stamps : 2 * stamps] = (mix - high.astype(f32)).astype(bf16)
        return carry

    lax.fori_loop(0, n_all // block, blend, 0)
    wait(load)


def terms_kernel(
    sizes,
    theta_ref,
    hot_ref,
    blend_ref,
    gain_ref,
    base_ref,
    tag_ref,
    front_ref,
    back_ref,
    tpl_ref,
    pair_ref,
    sel_ref,
    wide_ref,
    keep_ref,
    give_ref,
    amp_ref,
    acc_ref,
    proj_ref,
    lit_ref,
    rows_ref,
):
    n_sky, half, chunk, extra = sizes
    front, stamps, pix = front_ref.shape
    bands, size_k = tpl_ref.shape[0], tpl_ref.shape[1] // 2
    steps = [
        (b, slice(c * chunk, (c + 1) * chunk)) for b in range(bands) for c in range(pix // chunk)
    ]
    lane = iota((8, LANES), 1)
    for i in range(n_sky // 2):
        span = slice(i * LANES, (i + 1) * LANES)
        amp_ref[0:8, span] = jnp.exp(unfold(theta_ref, slice(None), lane, i, True))
        amp_ref[8:16, span] = jnp.exp(unfold(theta_ref, slice(None), lane, i, False))
    parts = jnp.concatenate(split3(amp_ref[...]), axis=0)
    got = dot(parts, hot_ref[...])
    mix = dot(parts, blend_ref[...])
    k1, k2, k3 = slice(0, size_k), slice(size_k, 2 * size_k), slice(2 * size_k, 3 * size_k)
    slot_f = got[k1] + (got[k2] + got[k3])
    high, low = mix[:, :stamps], mix[:, stamps:]
    slot_u = high[k1] + (high[k2] + low[k1] + (high[k3] + low[k2]))
    scaled = gain_ref[0:1, :] * slot_f
    lit_ref[...] = jnp.concatenate([scaled, slot_u], axis=0).T.astype(bf16)
    acc_ref[...] = jnp.zeros_like(acc_ref)
    proj_ref[...] = jnp.zeros_like(proj_ref)
    lit = lit_ref[...]
    base = jnp.concatenate([base_ref[...]] * (chunk // LANES), axis=1)
    wide = pair_ref.shape[1]

    def model(b, px):
        return dot(lit, tpl_ref[b, :, px])

    def weigh(b, px, light):
        seen = front_ref[b, :, px] if b < front else back_ref[b - front, :, px]
        resid = seen.astype(f32) - light
        under = base + (resid * resid) * (1.0 / ROBUST)
        guess = pltpu.reciprocal(under, approx=True)
        weight = guess * (2.0 - under * guess)
        return weight.astype(bf16), (weight * resid).astype(bf16)

    def gather(b, px, weight, wres):
        acc_ref[:, 0:wide] += dot(weight, pair_ref[b, :, px], NT)
        proj_ref[...] += dot(tpl_ref[b, 0:size_k, px], wres, NT)

    light = model(*steps[0])
    held = None
    for i, here in enumerate(steps):
        ahead = model(*steps[i + 1]) if i + 1 < len(steps) else None
        now = weigh(*here, light)
        if held is not None:
            gather(*steps[i - 1], *held)
        light, held = ahead, now
    gather(*steps[-1], *held)

    scales = dot(jnp.concatenate(split3(scaled), axis=0), wide_ref[...], TN)
    col = iota((1, 2 * LANES), 1) - (LANES + extra)
    is_grad = jnp.where((col >= 0) & (col < size_k), 1.0, 0.0)
    factor = scales[:, : 2 * LANES] * (scales[:, 2 * LANES :] + is_grad)
    proj = jnp.concatenate([jnp.zeros((extra, stamps), f32), proj_ref[...]], axis=0)
    proj = jnp.concatenate([proj, jnp.zeros((LANES - extra - size_k, stamps), f32)], axis=0)
    tail = acc_ref[:, LANES:] + proj.T
    terms = jnp.concatenate(
        [
            factor[:, :LANES] * acc_ref[:, :LANES],
            factor[:, LANES:] * tail + tag_ref[...],
        ],
        axis=1,
    )
    sel = sel_ref[...]
    t1, t2, t3 = split3(terms)
    rows_ref[...] = dot(sel, t1) + (dot(sel, t2) + dot(sel, t3))
    groups = half // SUB
    for part, out_ref in enumerate((keep_ref, give_ref)):
        for d in range(n_sky):
            at = (part * n_sky + d) * half
            for g in range(groups):
                line = rows_ref[at + g * SUB : at + (g + 1) * SUB, :]
                out_ref[d, :, g * LANES : (g + 1) * LANES] = line[:, :LANES]
                more = pltpu.roll(line[:, LANES:], g * GROUP, 1) if g else line[:, LANES:]
                tail = tail + more if g else more
            out_ref[d, :, groups * LANES :] = tail


def solve_kernel(
    sizes,
    recv_ref,
    other_ref,
    member_in_ref,
    full_ref,
    theta_ref,
    init_ref,
    pay_ref,
    new_ref,
    member_ref,
    rows_ref,
):
    n_sky, half, n_band, tag, learn = sizes
    size_k, obj_dev = theta_ref.shape
    total = 2 * n_sky * half
    groups = half // SUB
    group = iota((SUB, LANES), 1) // GROUP
    first = jnp.full((SUB, LANES), lax.axis_index("band")) == 0
    for d in range(n_sky):
        for g in range(groups + 1):
            span = slice(g * LANES, (g + 1) * LANES)
            mine, others = recv_ref[d, :, span], other_ref[d, :, span]
            pair = (jnp.where(first, mine, others), jnp.where(first, others, mine))
            for part, line in enumerate(pair):
                at = (part * n_sky + d) * half
                if g < groups:
                    rows_ref[at + g * SUB : at + (g + 1) * SUB, 0:LANES] = line
                else:
                    for h in range(groups):
                        rows_ref[at + h * SUB : at + (h + 1) * SUB, LANES:] = jnp.where(
                            group == h, line, 0.0
                        )
    p1, p2, p3 = split3(rows_ref[...])
    if learn:
        where_tag = jnp.where(column((8, 2 * LANES), LANES + tag), 1.0, 0.0).astype(bf16)
        ids = dot(where_tag, p1, NT) + (dot(where_tag, p2, NT) + dot(where_tag, p3, NT))
        named = (iota((obj_dev, total), 0) + 1) * n_band
        hit = named == ids[0:1, :].astype(jnp.int32)
        member_ref[...] = jnp.where(hit, 1.0, 0.0).astype(bf16)
        member = member_ref[...]
    else:
        member = member_in_ref[...]
    sums = dot(member, p1) + (dot(member, p2) + dot(member, p3))
    q1, q2, q3 = split3(sums)
    full = full_ref[...]
    wide = dot(full, q1, NT) + (dot(full, q2, NT) + dot(full, q3, NT))
    row = iota((size_k, obj_dev), 0)
    theta = theta_ref[...]
    target = wide[size_k * size_k :] - PRIOR * (theta - init_ref[...])
    matrix = []
    for k in range(size_k):
        line = wide[k * size_k : (k + 1) * size_k]
        matrix.append(jnp.where(row == k, line + (DAMPING * line + PRIOR), line))
    inverse = []
    for p in range(size_k):
        line = matrix[p]
        inv = 1.0 / line[p : p + 1]
        inverse.append(inv)
        if p + 1 < size_k:
            scaled = jnp.where(row > p, line * inv, 0.0)
            target = target - scaled * target[p : p + 1]
            for k in range(p + 1, size_k):
                matrix[k] = matrix[k] - scaled * line[k : k + 1]
    delta = jnp.zeros_like(target)
    for p in reversed(range(size_k)):
        value = target[p : p + 1] * inverse[p]
        delta = jnp.where(row == p, value, delta)
        if p:
            target = target - matrix[p] * value
    new = theta + STEP_LIMIT * jnp.tanh(delta / STEP_LIMIT)
    new_ref[...] = new
    if pay_ref is not None:
        half = size_k // 2
        folded = jnp.concatenate([new[:half], new[half:]], axis=1)
        for d in range(n_sky):
            pay_ref[d] = folded


def hbm(x):
    return pltpu.with_memory_space_constraint(x, pltpu.HBM)


def call(kernel, out_shape, scratch=(), spaces=None, flags=None):
    specs = {}
    if spaces:
        specs["in_specs"] = [
            pl.BlockSpec(memory_space=pltpu.HBM if s == "h" else pltpu.VMEM) for s in spaces
        ]
    return pl.pallas_call(
        kernel,
        out_shape=out_shape,
        scratch_shapes=list(scratch),
        compiler_params=pltpu.CompilerParams(vmem_limit_bytes=VMEM_LIMIT, flags=flags),
        **specs,
    )


def local(
    stamps,
    stamp_gain,
    stamp_invvar,
    stamp_dest,
    stamp_obj,
    phi_tpl,
    psi_tpl,
    theta_init,
    nb_id,
    nb_weight,
):
    n_sky = lax.axis_size("sky")
    n_band = lax.axis_size("band")
    stamp_dev, bands, pix = stamps.shape
    size_k, obj_dev = theta_init.shape
    nei = nb_id.shape[1]
    cap = 2 * stamp_dev // n_sky
    half = cap // 2
    total = n_sky * cap
    n_all = n_sky * obj_dev
    extra = size_k * (size_k + 1) // 2 - LANES
    wide = LANES + -(-extra // 16) * 16
    assert n_band == 2 and half % SUB == 0 and half // SUB <= LANES // GROUP
    assert 2 * obj_dev == LANES and bands >= 3 and 0 <= extra and extra + size_k < GROUP
    shape = jax.ShapeDtypeStruct
    wide_chunk = max(c for c in range(LANES, 1024, LANES) if pix % c == 0)
    chunk = max(c for c in range(LANES, 384, LANES) if pix % c == 0)

    pixels = jnp.transpose(stamps, (1, 0, 2))
    payload, front, tpl, pair, sel, spread, full, base, tag, gain, owner = call(
        functools.partial(ready_kernel, (n_sky, cap, obj_dev, extra, wide_chunk)),
        (
            shape((n_sky, 16, LANES), f32),
            shape((bands - bands // 3, stamp_dev, pix), bf16),
            shape((bands, 2 * size_k, pix), bf16),
            shape((bands, wide, pix), bf16),
            shape((total, stamp_dev), bf16),
            shape((3 * size_k, 4 * LANES), bf16),
            shape((size_k * size_k + size_k, 2 * LANES), bf16),
            shape((stamp_dev, LANES), f32),
            shape((stamp_dev, LANES), f32),
            shape((8, stamp_dev), f32),
            shape((8, stamp_dev), jnp.int32),
        ),
        [
            pltpu.VMEM((1, stamp_dev), jnp.int32),
            pltpu.VMEM((1, stamp_dev), jnp.int32),
            pltpu.VMEM((stamp_dev,), bf16),
            pltpu.VMEM((stamp_dev,), bf16),
            pltpu.VMEM((size_k, obj_dev), f32),
            pltpu.VMEM((nei, obj_dev), jnp.int32),
            pltpu.VMEM((nei, obj_dev), f32),
            pltpu.SemaphoreType.DMA((10,)),
        ],
        "h" * 10,
    )(
        hbm(stamp_dest.T),
        hbm(stamp_obj[None, :]),
        hbm(stamp_gain),
        hbm(stamp_invvar),
        hbm(phi_tpl),
        hbm(psi_tpl),
        hbm(theta_init),
        hbm(nb_id.T),
        hbm(nb_weight.T),
        hbm(pixels),
    )
    got = lax.all_to_all(payload, "sky", 0, 0, tiled=True)
    everyone, hot, blend, back = call(
        functools.partial(index_kernel, nei),
        (
            shape((n_sky, 8, LANES), f32),
            shape((n_all, stamp_dev), bf16),
            shape((n_all, 2 * stamp_dev), bf16),
            shape((bands // 3, stamp_dev, pix), bf16),
        ),
        [pltpu.VMEM((16, n_all), f32), pltpu.SemaphoreType.DMA(())],
        "vvh",
    )(got, owner, hbm(pixels))
    terms = call(
        functools.partial(terms_kernel, (n_sky, half, chunk, extra)),
        [shape((n_sky, SUB, (half // SUB + 1) * LANES), f32)] * 2,
        [
            pltpu.VMEM((size_k, n_all), f32),
            pltpu.VMEM((stamp_dev, 2 * LANES), f32),
            pltpu.VMEM((size_k, stamp_dev), f32),
            pltpu.VMEM((stamp_dev, 2 * size_k), bf16),
            pltpu.VMEM((total, 2 * LANES), f32),
        ],
    )
    swap = [(0, 1), (1, 0)]
    theta = theta_init
    member = None
    for sweep in range(ITERS):
        keep, give = terms(
            everyone, hot, blend, gain, base, tag, front, back, tpl, pair, sel, spread
        )
        sent = keep + lax.ppermute(give, "band", swap)
        recv = lax.all_to_all(sent, "sky", 0, 0, tiled=True)
        other = lax.ppermute(recv, "band", swap)
        learn, last = sweep == 0, sweep + 1 == ITERS
        sizes = (n_sky, half, n_band, extra + size_k, learn)

        def solve(*refs, learn=learn, last=last, sizes=sizes):
            refs = list(refs)
            if learn:
                refs.insert(2, None)
            if last:
                refs.insert(6, None)
            if not learn:
                refs.insert(8, None)
            solve_kernel(sizes, *refs)

        outs = [shape((n_sky, 8, LANES), f32)] * (not last)
        outs += [shape((size_k, obj_dev), f32)]
        outs += [shape((obj_dev, total), bf16)] * learn
        given = [recv, other] + [member] * (not learn) + [full, theta, theta_init]
        outs = call(solve, outs, [pltpu.VMEM((total, 2 * LANES), f32)])(*given)
        theta = outs[0 if last else 1]
        if learn:
            member = outs[-1]
        if not last:
            everyone = lax.all_to_all(outs[0], "sky", 0, 0, tiled=True)
    return theta


def solution(mesh):
    in_specs = (
        P("sky", "band", None),
        P("sky"),
        P("sky"),
        P("sky", None),
        P("sky"),
        P("band", None, None),
        P("band", None, None),
        P(None, "sky"),
        P("sky", None),
        P("sky", None),
    )
    out_specs = P(None, "sky")
    return jax.shard_map(local, mesh=mesh, in_specs=in_specs, out_specs=out_specs, check_vma=False)
```

```python
import functools

import jax
import jax.numpy as jnp
from jax import lax
from jax.experimental import pallas as pl
from jax.experimental.pallas import tpu as pltpu
from jax.sharding import PartitionSpec as P

ITERS = 3

ROBUST = 9.0
DAMPING = 0.1
PRIOR = 1.0
STEP_LIMIT = 0.5

LANES = 128
GROUP = 32
SUB = 4
VMEM_LIMIT = 24 * 1024 * 1024

f32 = jnp.float32
bf16 = jnp.bfloat16
NT = (((1,), (1,)), ((), ()))
TN = (((0,), (0,)), ((), ()))
NN = (((1,), (0,)), ((), ()))


def dot(a, b, dims=NN, precision=None):
    return lax.dot_general(a, b, dims, precision=precision, preferred_element_type=f32)


def split3(x):
    first = x.astype(bf16)
    rest = x - first.astype(f32)
    second = rest.astype(bf16)
    third = (rest - second.astype(f32)).astype(bf16)
    return first, second, third


def iota(shape, dim):
    return lax.broadcasted_iota(jnp.int32, shape, dim)


def dma(copies):
    for copy in copies:
        copy.start()
    return copies


def wait(copies):
    for copy in copies:
        copy.wait()


def offset(k, size_k):
    return lax.div(k * (2 * size_k + 1 - k), 2)


def column(shape, m):
    lane = iota(shape, 1)
    folded = jnp.where(lane < LANES, lane, LANES + lax.rem(lane, GROUP))
    return folded == m


def ready_kernel(
    sizes,
    dest_hbm,
    obj_hbm,
    gain_hbm,
    invvar_hbm,
    phi_hbm,
    psi_hbm,
    theta_hbm,
    nbi_hbm,
    nbw_hbm,
    pix_hbm,
    pay_ref,
    keep_ref,
    give_ref,
    tpl_ref,
    pair_ref,
    sel_ref,
    wide_ref,
    full_ref,
    base_ref,
    tag_ref,
    gain_ref,
    owner_ref,
    pix_ref,
    dest_ref,
    obj_ref,
    gain_low_ref,
    invvar_ref,
    theta_ref,
    nbi_ref,
    nbw_ref,
    sem,
):
    n_sky, cap, obj_dev, extra, chunk = sizes
    bands, size_k, pix = phi_hbm.shape
    stamps = dest_ref.shape[1]
    half = cap // 2
    first = [
        pltpu.make_async_copy(phi_hbm, tpl_ref.at[:, 0:size_k, :], sem.at[0]),
        pltpu.make_async_copy(psi_hbm, tpl_ref.at[:, size_k : 2 * size_k, :], sem.at[1]),
        pltpu.make_async_copy(dest_hbm, dest_ref, sem.at[2]),
        pltpu.make_async_copy(obj_hbm, obj_ref, sem.at[3]),
        pltpu.make_async_copy(gain_hbm, gain_low_ref, sem.at[4]),
        pltpu.make_async_copy(invvar_hbm, invvar_ref, sem.at[5]),
        pltpu.make_async_copy(theta_hbm, theta_ref, sem.at[6]),
        pltpu.make_async_copy(nbi_hbm, nbi_ref, sem.at[7]),
        pltpu.make_async_copy(nbw_hbm, nbw_ref, sem.at[8]),
    ]
    last = [pltpu.make_async_copy(pix_hbm, pix_ref, sem.at[9])]
    dma(first)
    dma(last)

    pairs = LANES + extra
    shape = (pair_ref.shape[1], size_k)
    m = iota(shape, 0)
    k = iota(shape, 1)
    lows = jnp.where((m >= offset(k, size_k)) & (m < offset(k + 1, size_k)), 1.0, 0.0)
    of_m = jnp.sum(lows * k.astype(f32), axis=1, keepdims=True).astype(jnp.int32)
    highs = jnp.where((m < pairs) & (m - offset(of_m, size_k) + of_m == k), 1.0, 0.0)
    lows, highs = lows.astype(bf16), highs.astype(bf16)

    shape = (size_k, 2 * LANES)
    k = iota(shape, 0)
    lane = iota(shape, 1)
    spot = pairs + k
    left = (lane >= offset(k, size_k)) & (lane < offset(k + 1, size_k))
    left = jnp.where(left | (lane == spot), 1.0, 0.0)
    lane_k = jnp.sum(jnp.where(lane >= offset(k + 1, size_k), 1, 0), axis=0, keepdims=True)
    right = (lane[0:1] - offset(lane_k, size_k) + lane_k == k) & (lane < pairs)
    both = jnp.concatenate([left, jnp.where(right, 1.0, 0.0)], axis=1).astype(bf16)
    for part in range(3):
        wide_ref[part * size_k : (part + 1) * size_k, :] = both

    shape = full_ref.shape
    r = iota((shape[0], 1), 0)
    a, b = lax.div(r, size_k), lax.rem(r, size_k)
    low, high = jnp.minimum(a, b), jnp.maximum(a, b)
    m = jnp.where(r < size_k * size_k, offset(low, size_k) + high - low, pairs + b)
    full_ref[...] = jnp.where(column(shape, m), 1.0, 0.0).astype(bf16)

    wait(first)
    theta = theta_ref[...]
    folded = jnp.concatenate([theta[: size_k // 2], theta[size_k // 2 :]], axis=1)
    side = jnp.concatenate([nbi_ref[...].astype(f32), nbw_ref[...]], axis=1)
    side = jnp.concatenate([side, jnp.zeros((8 - side.shape[0], LANES), f32)], axis=0)
    for d in range(n_sky):
        pay_ref[d, 0:8, :] = folded
        pay_ref[d, 8:16, :] = side
    dest = dest_ref[...]
    obj = obj_ref[...]
    along = jnp.broadcast_to(dest.astype(f32), (stamps, stamps))
    down = along.T
    before = iota((stamps, stamps), 0) < iota((stamps, stamps), 1)
    rank = jnp.sum(jnp.where(before & (along == down), 1.0, 0.0), axis=0, keepdims=True)
    lower = jnp.sum(jnp.where(down < along, 1.0, 0.0), axis=0, keepdims=True)
    rank = rank.astype(jnp.int32)
    order = lower.astype(jnp.int32) + rank
    spot = lax.div(order, 2)
    here = lax.rem(order, 2) == lax.axis_index("band")
    match = iota((stamps // 2, stamps), 0) == spot
    mine = jnp.where(match & here, 1.0, 0.0).astype(bf16)
    theirs = jnp.where(match & jnp.logical_not(here), 1.0, 0.0).astype(bf16)
    about = jnp.concatenate(
        [
            gain_low_ref[...].astype(f32).reshape(1, stamps),
            1.0 / invvar_ref[...].astype(f32).reshape(1, stamps),
            (dest * obj_dev + obj).astype(f32),
            (obj + 1).astype(f32),
            (dest * half + lax.div(rank, 2)).astype(f32),
            jnp.zeros((3, stamps), f32),
        ],
        axis=0,
    )
    p1, p2, p3 = split3(about)
    about = dot(p1, mine, NT) + (dot(p2, mine, NT) + dot(p3, mine, NT))
    count = stamps // 2
    gain_ref[...] = jnp.broadcast_to(about[0:1], gain_ref.shape)
    base_ref[...] = jnp.broadcast_to(about[1:2], (LANES, count)).T
    owner_ref[...] = jnp.broadcast_to(about[2:3].astype(jnp.int32), owner_ref.shape)
    named = jnp.broadcast_to(about[3:4], (LANES, count)).T
    tag_ref[...] = jnp.where(iota((count, LANES), 1) == extra + size_k, named, 0.0)
    place = about[4:5].astype(jnp.int32)
    sel_ref[...] = jnp.where(iota(sel_ref.shape, 0) == place, 1.0, 0.0).astype(bf16)
    for b in range(bands):
        for c in range(pix // chunk):
            px = slice(c * chunk, (c + 1) * chunk)
            phi = tpl_ref[b, 0:size_k, px]
            pair_ref[b, :, px] = (dot(lows, phi) * dot(highs, phi)).astype(bf16)
    wait(last)
    for b in range(bands):
        for c in range(pix // chunk):
            px = slice(c * chunk, (c + 1) * chunk)
            seen = pix_ref[b, :, px]
            keep_ref[b, :, px] = dot(mine, seen).astype(bf16)
            give_ref[b, :, px] = dot(theirs, seen).astype(bf16)


def unfold(ref, rows, lane, i, left):
    x, y = ref[2 * i, rows, :], ref[2 * i + 1, rows, :]
    if left:
        return jnp.where(lane < LANES // 2, x, pltpu.roll(y, LANES // 2, 1))
    return jnp.where(lane < LANES // 2, pltpu.roll(x, LANES // 2, 1), y)


def index_kernel(nei, got_ref, owner_ref, theta_ref, hot_ref, blend_ref, table_ref):
    n_sky = got_ref.shape[0]
    n_all, stamps = hot_ref.shape
    block = LANES
    owner = owner_ref[0:1, :]

    def hot(i, carry):
        rows = pl.ds(pl.multiple_of(i * block, block), block)
        hit = iota((block, stamps), 0) + i * block == owner
        hot_ref[rows, :] = jnp.where(hit, 1.0, 0.0).astype(bf16)
        return carry

    lax.fori_loop(0, n_all // block, hot, 0)
    lane = iota((8, LANES), 1)
    for d in range(n_sky):
        theta_ref[d] = got_ref[d, 0:8, :]
    for i in range(n_sky // 2):
        span = slice(i * LANES, (i + 1) * LANES)
        table_ref[0:8, span] = unfold(got_ref, slice(8, 16), lane, i, True)
        table_ref[8:16, span] = unfold(got_ref, slice(8, 16), lane, i, False)
    parts = jnp.concatenate(split3(table_ref[...]), axis=0)
    found = dot(parts, hot_ref[...])
    found = found[0:16] + found[16:32] + found[32:48]
    near_id = found[0:nei].astype(jnp.int32)
    near_w = found[8 : 8 + nei]

    def blend(i, carry):
        rows = pl.ds(pl.multiple_of(i * block, block), block)
        here = iota((block, stamps), 0) + i * block
        mix = jnp.zeros((block, stamps), f32)
        for j in range(nei):
            mix = mix + jnp.where(here == near_id[j : j + 1], near_w[j : j + 1], 0.0)
        high = mix.astype(bf16)
        blend_ref[rows, 0:stamps] = high
        blend_ref[rows, stamps : 2 * stamps] = (mix - high.astype(f32)).astype(bf16)
        return carry

    lax.fori_loop(0, n_all // block, blend, 0)


def terms_kernel(
    sizes,
    theta_ref,
    hot_ref,
    blend_ref,
    gain_ref,
    base_ref,
    tag_ref,
    pix_ref,
    pix2_ref,
    tpl_ref,
    tpl2_ref,
    pair_ref,
    pair2_ref,
    sel_ref,
    wide_ref,
    out_ref,
    amp_ref,
    acc_ref,
    proj_ref,
    lit_ref,
    rows_ref,
):
    n_sky, half, chunk, extra = sizes
    bands, stamps, pix = pix_ref.shape
    size_k = tpl_ref.shape[1] // 2
    seen = [ref.at[b] for ref in (pix_ref, pix2_ref) for b in range(bands)]
    tpl = [ref.at[b] for ref in (tpl_ref, tpl2_ref) for b in range(bands)]
    pair = [ref.at[b] for ref in (pair_ref, pair2_ref) for b in range(bands)]
    steps = [
        (b, slice(c * chunk, (c + 1) * chunk))
        for b in range(2 * bands)
        for c in range(pix // chunk)
    ]
    lane = iota((8, LANES), 1)
    for i in range(n_sky // 2):
        span = slice(i * LANES, (i + 1) * LANES)
        amp_ref[0:8, span] = jnp.exp(unfold(theta_ref, slice(None), lane, i, True))
        amp_ref[8:16, span] = jnp.exp(unfold(theta_ref, slice(None), lane, i, False))
    parts = jnp.concatenate(split3(amp_ref[...]), axis=0)
    got = dot(parts, hot_ref[...])
    mix = dot(parts, blend_ref[...])
    k1, k2, k3 = slice(0, size_k), slice(size_k, 2 * size_k), slice(2 * size_k, 3 * size_k)
    slot_f = got[k1] + (got[k2] + got[k3])
    high, low = mix[:, :stamps], mix[:, stamps:]
    slot_u = high[k1] + (high[k2] + low[k1] + (high[k3] + low[k2]))
    scaled = gain_ref[0:1, :] * slot_f
    lit_ref[...] = jnp.concatenate([scaled, slot_u], axis=0).T.astype(bf16)
    acc_ref[...] = jnp.zeros_like(acc_ref)
    proj_ref[...] = jnp.zeros_like(proj_ref)
    lit = lit_ref[...]
    base = jnp.concatenate([base_ref[...]] * (chunk // LANES), axis=1)
    wide = pair_ref.shape[1]

    def model(b, px):
        return dot(lit, tpl[b][:, px])

    def weigh(b, px, light):
        resid = seen[b][:, px].astype(f32) - light
        under = base + (resid * resid) * (1.0 / ROBUST)
        guess = pltpu.reciprocal(under, approx=True)
        weight = guess * (2.0 - under * guess)
        return weight.astype(bf16), (weight * resid).astype(bf16)

    def gather(b, px, weight, wres):
        acc_ref[:, 0:wide] += dot(weight, pair[b][:, px], NT)
        proj_ref[...] += dot(tpl[b][0:size_k, px], wres, NT)

    light = model(*steps[0])
    held = None
    for i, here in enumerate(steps):
        ahead = model(*steps[i + 1]) if i + 1 < len(steps) else None
        now = weigh(*here, light)
        if held is not None:
            gather(*steps[i - 1], *held)
        light, held = ahead, now
    gather(*steps[-1], *held)

    scales = dot(jnp.concatenate(split3(scaled), axis=0), wide_ref[...], TN)
    col = iota((1, 2 * LANES), 1) - (LANES + extra)
    is_grad = jnp.where((col >= 0) & (col < size_k), 1.0, 0.0)
    factor = scales[:, : 2 * LANES] * (scales[:, 2 * LANES :] + is_grad)
    proj = jnp.concatenate([jnp.zeros((extra, stamps), f32), proj_ref[...]], axis=0)
    proj = jnp.concatenate([proj, jnp.zeros((LANES - extra - size_k, stamps), f32)], axis=0)
    tail = acc_ref[:, LANES:] + proj.T
    terms = jnp.concatenate(
        [
            factor[:, :LANES] * acc_ref[:, :LANES],
            factor[:, LANES:] * tail + tag_ref[...],
        ],
        axis=1,
    )
    sel = sel_ref[...]
    t1, t2, t3 = split3(terms)
    rows_ref[...] = dot(sel, t1) + (dot(sel, t2) + dot(sel, t3))
    groups = half // SUB
    for d in range(n_sky):
        at = d * half
        for g in range(groups):
            line = rows_ref[at + g * SUB : at + (g + 1) * SUB, :]
            out_ref[d, :, g * LANES : (g + 1) * LANES] = line[:, :LANES]
            more = pltpu.roll(line[:, LANES:], g * GROUP, 1) if g else line[:, LANES:]
            tail = tail + more if g else more
        out_ref[d, :, groups * LANES :] = tail


def solve_kernel(
    sizes,
    recv_ref,
    other_ref,
    member_in_ref,
    full_ref,
    theta_ref,
    init_ref,
    pay_ref,
    new_ref,
    member_ref,
    rows_ref,
):
    n_sky, half, tag, learn = sizes
    size_k, obj_dev = theta_ref.shape
    total = 2 * n_sky * half
    groups = half // SUB
    group = iota((SUB, LANES), 1) // GROUP
    first = jnp.full((SUB, LANES), lax.axis_index("band")) == 0
    for d in range(n_sky):
        for g in range(groups + 1):
            span = slice(g * LANES, (g + 1) * LANES)
            mine, others = recv_ref[d, :, span], other_ref[d, :, span]
            pair = (jnp.where(first, mine, others), jnp.where(first, others, mine))
            for part, line in enumerate(pair):
                at = (part * n_sky + d) * half
                if g < groups:
                    rows_ref[at + g * SUB : at + (g + 1) * SUB, 0:LANES] = line
                else:
                    for h in range(groups):
                        rows_ref[at + h * SUB : at + (h + 1) * SUB, LANES:] = jnp.where(
                            group == h, line, 0.0
                        )
    p1, p2, p3 = split3(rows_ref[...])
    if learn:
        where_tag = jnp.where(column((8, 2 * LANES), LANES + tag), 1.0, 0.0).astype(bf16)
        ids = dot(where_tag, p1, NT) + (dot(where_tag, p2, NT) + dot(where_tag, p3, NT))
        hit = iota((obj_dev, total), 0) + 1 == ids[0:1, :].astype(jnp.int32)
        member_ref[...] = jnp.where(hit, 1.0, 0.0).astype(bf16)
        member = member_ref[...]
    else:
        member = member_in_ref[...]
    sums = dot(member, p1) + (dot(member, p2) + dot(member, p3))
    q1, q2, q3 = split3(sums)
    full = full_ref[...]
    wide = dot(full, q1, NT) + (dot(full, q2, NT) + dot(full, q3, NT))
    row = iota((size_k, obj_dev), 0)
    theta = theta_ref[...]
    target = wide[size_k * size_k :] - PRIOR * (theta - init_ref[...])
    matrix = []
    for k in range(size_k):
        line = wide[k * size_k : (k + 1) * size_k]
        matrix.append(jnp.where(row == k, line + (DAMPING * line + PRIOR), line))
    inverse = []
    for p in range(size_k):
        line = matrix[p]
        inv = 1.0 / line[p : p + 1]
        inverse.append(inv)
        if p + 1 < size_k:
            scaled = jnp.where(row > p, line * inv, 0.0)
            target = target - scaled * target[p : p + 1]
            for k in range(p + 1, size_k):
                matrix[k] = matrix[k] - scaled * line[k : k + 1]
    delta = jnp.zeros_like(target)
    for p in reversed(range(size_k)):
        value = target[p : p + 1] * inverse[p]
        delta = jnp.where(row == p, value, delta)
        if p:
            target = target - matrix[p] * value
    new = theta + STEP_LIMIT * jnp.tanh(delta / STEP_LIMIT)
    new_ref[...] = new
    if pay_ref is not None:
        half = size_k // 2
        folded = jnp.concatenate([new[:half], new[half:]], axis=1)
        for d in range(n_sky):
            pay_ref[d] = folded


def hbm(x):
    return pltpu.with_memory_space_constraint(x, pltpu.HBM)


def call(kernel, out_shape, scratch=(), spaces=None, flags=None):
    specs = {}
    if spaces:
        specs["in_specs"] = [
            pl.BlockSpec(memory_space=pltpu.HBM if s == "h" else pltpu.VMEM) for s in spaces
        ]
    return pl.pallas_call(
        kernel,
        out_shape=out_shape,
        scratch_shapes=list(scratch),
        compiler_params=pltpu.CompilerParams(vmem_limit_bytes=VMEM_LIMIT, flags=flags),
        **specs,
    )


def local(
    stamps,
    stamp_gain,
    stamp_invvar,
    stamp_dest,
    stamp_obj,
    phi_tpl,
    psi_tpl,
    theta_init,
    nb_id,
    nb_weight,
):
    n_sky = lax.axis_size("sky")
    n_band = lax.axis_size("band")
    stamp_dev, bands, pix = stamps.shape
    size_k, obj_dev = theta_init.shape
    nei = nb_id.shape[1]
    cap = 2 * stamp_dev // n_sky
    half = cap // 2
    core_dev = stamp_dev // 2
    total = n_sky * cap
    n_all = n_sky * obj_dev
    extra = size_k * (size_k + 1) // 2 - LANES
    wide = LANES + -(-extra // 16) * 16
    assert n_band == 2 and half % SUB == 0 and half // SUB <= LANES // GROUP
    assert 2 * obj_dev == LANES and 0 <= extra and extra + size_k < GROUP
    shape = jax.ShapeDtypeStruct
    wide_chunk = max(c for c in range(LANES, 1024, LANES) if pix % c == 0)
    chunk = max(c for c in range(LANES, 512, LANES) if pix % c == 0)

    pixels = jnp.transpose(stamps, (1, 0, 2))
    payload, keep, give, tpl, pair, sel, spread, full, base, tag, gain, owner = call(
        functools.partial(ready_kernel, (n_sky, cap, obj_dev, extra, wide_chunk)),
        (
            shape((n_sky, 16, LANES), f32),
            shape((bands, core_dev, pix), bf16),
            shape((bands, core_dev, pix), bf16),
            shape((bands, 2 * size_k, pix), bf16),
            shape((bands, wide, pix), bf16),
            shape((n_sky * half, core_dev), bf16),
            shape((3 * size_k, 4 * LANES), bf16),
            shape((size_k * size_k + size_k, 2 * LANES), bf16),
            shape((core_dev, LANES), f32),
            shape((core_dev, LANES), f32),
            shape((8, core_dev), f32),
            shape((8, core_dev), jnp.int32),
        ),
        [
            pltpu.VMEM((bands, stamp_dev, pix), bf16),
            pltpu.VMEM((1, stamp_dev), jnp.int32),
            pltpu.VMEM((1, stamp_dev), jnp.int32),
            pltpu.VMEM((stamp_dev,), bf16),
            pltpu.VMEM((stamp_dev,), bf16),
            pltpu.VMEM((size_k, obj_dev), f32),
            pltpu.VMEM((nei, obj_dev), jnp.int32),
            pltpu.VMEM((nei, obj_dev), f32),
            pltpu.SemaphoreType.DMA((10,)),
        ],
        "h" * 10,
    )(
        hbm(stamp_dest.T),
        hbm(stamp_obj[None, :]),
        hbm(stamp_gain),
        hbm(stamp_invvar),
        hbm(phi_tpl),
        hbm(psi_tpl),
        hbm(theta_init),
        hbm(nb_id.T),
        hbm(nb_weight.T),
        hbm(pixels),
    )
    swap = [(0, 1), (1, 0)]
    keep2, tpl2, pair2 = [lax.ppermute(x, "band", swap) for x in (give, tpl, pair)]
    got = lax.all_to_all(payload, "sky", 0, 0, tiled=True)
    everyone, hot, blend = call(
        functools.partial(index_kernel, nei),
        (
            shape((n_sky, 8, LANES), f32),
            shape((n_all, core_dev), bf16),
            shape((n_all, 2 * core_dev), bf16),
        ),
        [pltpu.VMEM((16, n_all), f32)],
    )(got, owner)
    terms = call(
        functools.partial(terms_kernel, (n_sky, half, chunk, extra)),
        shape((n_sky, SUB, (half // SUB + 1) * LANES), f32),
        [
            pltpu.VMEM((size_k, n_all), f32),
            pltpu.VMEM((core_dev, 2 * LANES), f32),
            pltpu.VMEM((size_k, core_dev), f32),
            pltpu.VMEM((core_dev, 2 * size_k), bf16),
            pltpu.VMEM((n_sky * half, 2 * LANES), f32),
        ],
    )
    theta = theta_init
    member = None
    for sweep in range(ITERS):
        sent = terms(
            everyone,
            hot,
            blend,
            gain,
            base,
            tag,
            keep,
            keep2,
            tpl,
            tpl2,
            pair,
            pair2,
            sel,
            spread,
        )
        recv = lax.all_to_all(sent, "sky", 0, 0, tiled=True)
        other = lax.ppermute(recv, "band", swap)
        learn, last = sweep == 0, sweep + 1 == ITERS
        sizes = (n_sky, half, extra + size_k, learn)

        def solve(*refs, learn=learn, last=last, sizes=sizes):
            refs = list(refs)
            if learn:
                refs.insert(2, None)
            if last:
                refs.insert(6, None)
            if not learn:
                refs.insert(8, None)
            solve_kernel(sizes, *refs)

        outs = [shape((n_sky, 8, LANES), f32)] * (not last)
        outs += [shape((size_k, obj_dev), f32)]
        outs += [shape((obj_dev, total), bf16)] * learn
        given = [recv, other] + [member] * (not learn) + [full, theta, theta_init]
        outs = call(solve, outs, [pltpu.VMEM((total, 2 * LANES), f32)])(*given)
        theta = outs[0 if last else 1]
        if learn:
            member = outs[-1]
        if not last:
            everyone = lax.all_to_all(outs[0], "sky", 0, 0, tiled=True)
    return theta


def solution(mesh):
    in_specs = (
        P("sky", "band", None),
        P("sky"),
        P("sky"),
        P("sky", None),
        P("sky"),
        P("band", None, None),
        P("band", None, None),
        P(None, "sky"),
        P("sky", None),
        P("sky", None),
    )
    out_specs = P(None, "sky")
    return jax.shard_map(local, mesh=mesh, in_specs=in_specs, out_specs=out_specs, check_vma=False)
```

```python
import functools

import jax
import jax.numpy as jnp
from jax import lax
from jax.experimental import pallas as pl
from jax.experimental.pallas import tpu as pltpu
from jax.sharding import PartitionSpec as P

ITERS = 3

ROBUST = 9.0
DAMPING = 0.1
PRIOR = 1.0
STEP_LIMIT = 0.5

LANES = 128
GROUP = 32
SUB = 4
VMEM_LIMIT = 24 * 1024 * 1024

f32 = jnp.float32
bf16 = jnp.bfloat16
NT = (((1,), (1,)), ((), ()))
TN = (((0,), (0,)), ((), ()))
NN = (((1,), (0,)), ((), ()))


def dot(a, b, dims=NN, precision=None):
    return lax.dot_general(a, b, dims, precision=precision, preferred_element_type=f32)


def split3(x):
    first = x.astype(bf16)
    rest = x - first.astype(f32)
    second = rest.astype(bf16)
    third = (rest - second.astype(f32)).astype(bf16)
    return first, second, third


def iota(shape, dim):
    return lax.broadcasted_iota(jnp.int32, shape, dim)


def dma(copies):
    for copy in copies:
        copy.start()
    return copies


def wait(copies):
    for copy in copies:
        copy.wait()


def offset(k, size_k):
    return lax.div(k * (2 * size_k + 1 - k), 2)


def column(shape, m):
    lane = iota(shape, 1)
    folded = jnp.where(lane < LANES, lane, LANES + lax.rem(lane, GROUP))
    return folded == m


def ready_kernel(
    sizes,
    dest_hbm,
    obj_hbm,
    gain_hbm,
    invvar_hbm,
    phi_hbm,
    psi_hbm,
    theta_hbm,
    nbi_hbm,
    nbw_hbm,
    pix_hbm,
    pay_ref,
    keep_ref,
    give_ref,
    tpl_ref,
    pair_ref,
    sel_ref,
    wide_ref,
    full_ref,
    base_ref,
    tag_ref,
    gain_ref,
    owner_ref,
    pix_ref,
    dest_ref,
    obj_ref,
    gain_low_ref,
    invvar_ref,
    theta_ref,
    nbi_ref,
    nbw_ref,
    sem,
):
    n_sky, cap, obj_dev, extra, chunk = sizes
    bands, size_k, pix = phi_hbm.shape
    stamps = dest_ref.shape[1]
    half = cap // 2
    first = [
        pltpu.make_async_copy(phi_hbm, tpl_ref.at[:, 0:size_k, :], sem.at[0]),
        pltpu.make_async_copy(psi_hbm, tpl_ref.at[:, size_k : 2 * size_k, :], sem.at[1]),
        pltpu.make_async_copy(dest_hbm, dest_ref, sem.at[2]),
        pltpu.make_async_copy(obj_hbm, obj_ref, sem.at[3]),
        pltpu.make_async_copy(gain_hbm, gain_low_ref, sem.at[4]),
        pltpu.make_async_copy(invvar_hbm, invvar_ref, sem.at[5]),
        pltpu.make_async_copy(theta_hbm, theta_ref, sem.at[6]),
        pltpu.make_async_copy(nbi_hbm, nbi_ref, sem.at[7]),
        pltpu.make_async_copy(nbw_hbm, nbw_ref, sem.at[8]),
    ]
    last = [pltpu.make_async_copy(pix_hbm, pix_ref, sem.at[9])]
    dma(first)
    dma(last)

    pairs = LANES + extra
    shape = (pair_ref.shape[1], size_k)
    m = iota(shape, 0)
    k = iota(shape, 1)
    lows = jnp.where((m >= offset(k, size_k)) & (m < offset(k + 1, size_k)), 1.0, 0.0)
    of_m = jnp.sum(lows * k.astype(f32), axis=1, keepdims=True).astype(jnp.int32)
    highs = jnp.where((m < pairs) & (m - offset(of_m, size_k) + of_m == k), 1.0, 0.0)
    lows_highs = jnp.concatenate([lows, highs], axis=0).astype(bf16)
    many = pair_ref.shape[1]

    shape = (size_k, 2 * LANES)
    k = iota(shape, 0)
    lane = iota(shape, 1)
    spot = pairs + k
    left = (lane >= offset(k, size_k)) & (lane < offset(k + 1, size_k))
    left = jnp.where(left | (lane == spot), 1.0, 0.0)
    lane_k = jnp.sum(jnp.where(lane >= offset(k + 1, size_k), 1, 0), axis=0, keepdims=True)
    right = (lane[0:1] - offset(lane_k, size_k) + lane_k == k) & (lane < pairs)
    both = jnp.concatenate([left, jnp.where(right, 1.0, 0.0)], axis=1).astype(bf16)
    for part in range(3):
        wide_ref[part * size_k : (part + 1) * size_k, :] = both

    shape = full_ref.shape
    r = iota((shape[0], 1), 0)
    a, b = lax.div(r, size_k), lax.rem(r, size_k)
    low, high = jnp.minimum(a, b), jnp.maximum(a, b)
    m = jnp.where(r < size_k * size_k, offset(low, size_k) + high - low, pairs + b)
    full_ref[...] = jnp.where(column(shape, m), 1.0, 0.0).astype(bf16)

    wait(first)
    theta = theta_ref[...]
    folded = jnp.concatenate([theta[: size_k // 2], theta[size_k // 2 :]], axis=1)
    side = jnp.concatenate([nbi_ref[...].astype(f32), nbw_ref[...]], axis=1)
    side = jnp.concatenate([side, jnp.zeros((8 - side.shape[0], LANES), f32)], axis=0)
    for d in range(n_sky):
        pay_ref[d, 0:8, :] = folded
        pay_ref[d, 8:16, :] = side
    dest = dest_ref[...]
    obj = obj_ref[...]
    along = jnp.broadcast_to(dest.astype(f32), (stamps, stamps))
    down = along.T
    before = iota((stamps, stamps), 0) < iota((stamps, stamps), 1)
    rank = jnp.sum(jnp.where(before & (along == down), 1.0, 0.0), axis=0, keepdims=True)
    lower = jnp.sum(jnp.where(down < along, 1.0, 0.0), axis=0, keepdims=True)
    rank = rank.astype(jnp.int32)
    order = lower.astype(jnp.int32) + rank
    spot = lax.div(order, 2)
    here = lax.rem(order, 2) == lax.axis_index("band")
    match = iota((stamps // 2, stamps), 0) == spot
    mine = jnp.where(match & here, 1.0, 0.0).astype(bf16)
    theirs = jnp.where(match & jnp.logical_not(here), 1.0, 0.0).astype(bf16)
    parted = jnp.concatenate([mine, theirs], axis=0)
    about = jnp.concatenate(
        [
            gain_low_ref[...].astype(f32).reshape(1, stamps),
            1.0 / invvar_ref[...].astype(f32).reshape(1, stamps),
            (dest * obj_dev + obj).astype(f32),
            (obj + 1).astype(f32),
            (dest * half + lax.div(rank, 2)).astype(f32),
            jnp.zeros((3, stamps), f32),
        ],
        axis=0,
    )
    p1, p2, p3 = split3(about)
    about = dot(p1, mine, NT) + (dot(p2, mine, NT) + dot(p3, mine, NT))
    count = stamps // 2
    gain_ref[...] = jnp.broadcast_to(about[0:1], gain_ref.shape)
    base_ref[...] = jnp.broadcast_to(about[1:2], (LANES, count)).T
    owner_ref[...] = jnp.broadcast_to(about[2:3].astype(jnp.int32), owner_ref.shape)
    named = jnp.broadcast_to(about[3:4], (LANES, count)).T
    tag_ref[...] = jnp.where(iota((count, LANES), 1) == extra + size_k, named, 0.0)
    place = about[4:5].astype(jnp.int32)
    sel_ref[...] = jnp.where(iota(sel_ref.shape, 0) == place, 1.0, 0.0).astype(bf16)
    for b in range(bands):
        for c in range(pix // chunk):
            px = slice(c * chunk, (c + 1) * chunk)
            phi = tpl_ref[b, 0:size_k, px]
            two = dot(lows_highs, phi)
            pair_ref[b, :, px] = (two[:many] * two[many:]).astype(bf16)
    wait(last)
    for b in range(bands):
        for c in range(pix // chunk):
            px = slice(c * chunk, (c + 1) * chunk)
            seen = pix_ref[b, :, px]
            rows = dot(parted, seen).astype(bf16)
            keep_ref[b, :, px] = rows[:count]
            give_ref[b, :, px] = rows[count:]


def unfold(ref, rows, lane, i, left):
    x, y = ref[2 * i, rows, :], ref[2 * i + 1, rows, :]
    if left:
        return jnp.where(lane < LANES // 2, x, pltpu.roll(y, LANES // 2, 1))
    return jnp.where(lane < LANES // 2, pltpu.roll(x, LANES // 2, 1), y)


def index_kernel(nei, got_ref, owner_ref, theta_ref, hot_ref, blend_ref, table_ref):
    n_sky = got_ref.shape[0]
    n_all, stamps = hot_ref.shape
    block = LANES
    owner = owner_ref[0:1, :]

    def hot(i, carry):
        rows = pl.ds(pl.multiple_of(i * block, block), block)
        hit = iota((block, stamps), 0) + i * block == owner
        hot_ref[rows, :] = jnp.where(hit, 1.0, 0.0).astype(bf16)
        return carry

    lax.fori_loop(0, n_all // block, hot, 0)
    lane = iota((8, LANES), 1)
    for d in range(n_sky):
        theta_ref[d] = got_ref[d, 0:8, :]
    for i in range(n_sky // 2):
        span = slice(i * LANES, (i + 1) * LANES)
        table_ref[0:8, span] = unfold(got_ref, slice(8, 16), lane, i, True)
        table_ref[8:16, span] = unfold(got_ref, slice(8, 16), lane, i, False)
    parts = jnp.concatenate(split3(table_ref[...]), axis=0)
    found = dot(parts, hot_ref[...])
    found = found[0:16] + found[16:32] + found[32:48]
    near_id = found[0:nei].astype(jnp.int32)
    near_w = found[8 : 8 + nei]

    def blend(i, carry):
        rows = pl.ds(pl.multiple_of(i * block, block), block)
        here = iota((block, stamps), 0) + i * block
        mix = jnp.zeros((block, stamps), f32)
        for j in range(nei):
            mix = mix + jnp.where(here == near_id[j : j + 1], near_w[j : j + 1], 0.0)
        high = mix.astype(bf16)
        blend_ref[rows, 0:stamps] = high
        blend_ref[rows, stamps : 2 * stamps] = (mix - high.astype(f32)).astype(bf16)
        return carry

    lax.fori_loop(0, n_all // block, blend, 0)


def terms_kernel(
    sizes,
    theta_ref,
    hot_ref,
    blend_ref,
    gain_ref,
    base_ref,
    tag_ref,
    pix_ref,
    pix2_ref,
    tpl_ref,
    tpl2_ref,
    pair_ref,
    pair2_ref,
    sel_ref,
    wide_ref,
    out_ref,
    amp_ref,
    acc_ref,
    proj_ref,
    lit_ref,
    rows_ref,
):
    n_sky, half, chunk, extra = sizes
    bands, stamps, pix = pix_ref.shape
    size_k = tpl_ref.shape[1] // 2
    seen = [ref.at[b] for ref in (pix_ref, pix2_ref) for b in range(bands)]
    tpl = [ref.at[b] for ref in (tpl_ref, tpl2_ref) for b in range(bands)]
    pair = [ref.at[b] for ref in (pair_ref, pair2_ref) for b in range(bands)]
    steps = [
        (b, slice(c * chunk, (c + 1) * chunk))
        for b in range(2 * bands)
        for c in range(pix // chunk)
    ]
    lane = iota((8, LANES), 1)
    for i in range(n_sky // 2):
        span = slice(i * LANES, (i + 1) * LANES)
        amp_ref[0:8, span] = jnp.exp(unfold(theta_ref, slice(None), lane, i, True))
        amp_ref[8:16, span] = jnp.exp(unfold(theta_ref, slice(None), lane, i, False))
    parts = jnp.concatenate(split3(amp_ref[...]), axis=0)
    got = dot(parts, hot_ref[...])
    mix = dot(parts, blend_ref[...])
    k1, k2, k3 = slice(0, size_k), slice(size_k, 2 * size_k), slice(2 * size_k, 3 * size_k)
    slot_f = got[k1] + (got[k2] + got[k3])
    high, low = mix[:, :stamps], mix[:, stamps:]
    slot_u = high[k1] + (high[k2] + low[k1] + (high[k3] + low[k2]))
    scaled = gain_ref[0:1, :] * slot_f
    lit_ref[...] = jnp.concatenate([scaled, slot_u], axis=0).T.astype(bf16)
    acc_ref[...] = jnp.zeros_like(acc_ref)
    proj_ref[...] = jnp.zeros_like(proj_ref)
    lit = lit_ref[...]
    base = jnp.concatenate([base_ref[...]] * (chunk // LANES), axis=1)
    wide = pair_ref.shape[1]

    def model(b, px):
        return dot(lit, tpl[b][:, px])

    def weigh(b, px, light):
        resid = seen[b][:, px].astype(f32) - light
        under = base + (resid * resid) * (1.0 / ROBUST)
        guess = pltpu.reciprocal(under, approx=True)
        weight = guess * (2.0 - under * guess)
        return weight.astype(bf16), (weight * resid).astype(bf16)

    def gather(b, px, weight, wres):
        acc_ref[:, 0:wide] += dot(weight, pair[b][:, px], NT)
        proj_ref[...] += dot(tpl[b][0:size_k, px], wres, NT)

    light = model(*steps[0])
    held = None
    for i, here in enumerate(steps):
        ahead = model(*steps[i + 1]) if i + 1 < len(steps) else None
        now = weigh(*here, light)
        if held is not None:
            gather(*steps[i - 1], *held)
        light, held = ahead, now
    gather(*steps[-1], *held)

    scales = dot(jnp.concatenate(split3(scaled), axis=0), wide_ref[...], TN)
    col = iota((1, 2 * LANES), 1) - (LANES + extra)
    is_grad = jnp.where((col >= 0) & (col < size_k), 1.0, 0.0)
    factor = scales[:, : 2 * LANES] * (scales[:, 2 * LANES :] + is_grad)
    proj = jnp.concatenate([jnp.zeros((extra, stamps), f32), proj_ref[...]], axis=0)
    proj = jnp.concatenate([proj, jnp.zeros((LANES - extra - size_k, stamps), f32)], axis=0)
    tail = acc_ref[:, LANES:] + proj.T
    terms = jnp.concatenate(
        [
            factor[:, :LANES] * acc_ref[:, :LANES],
            factor[:, LANES:] * tail + tag_ref[...],
        ],
        axis=1,
    )
    sel = sel_ref[...]
    t1, t2, t3 = split3(terms)
    rows_ref[...] = dot(sel, t1) + (dot(sel, t2) + dot(sel, t3))
    groups = half // SUB
    for d in range(n_sky):
        at = d * half
        for g in range(groups):
            line = rows_ref[at + g * SUB : at + (g + 1) * SUB, :]
            out_ref[d, :, g * LANES : (g + 1) * LANES] = line[:, :LANES]
            more = pltpu.roll(line[:, LANES:], g * GROUP, 1) if g else line[:, LANES:]
            tail = tail + more if g else more
        out_ref[d, :, groups * LANES :] = tail


def solve_kernel(
    sizes,
    recv_ref,
    other_ref,
    member_in_ref,
    full_ref,
    theta_ref,
    init_ref,
    pay_ref,
    new_ref,
    member_ref,
    rows_ref,
):
    n_sky, half, tag, learn = sizes
    size_k, obj_dev = theta_ref.shape
    total = 2 * n_sky * half
    groups = half // SUB
    group = iota((SUB, LANES), 1) // GROUP
    first = jnp.full((SUB, LANES), lax.axis_index("band")) == 0
    for d in range(n_sky):
        for g in range(groups + 1):
            span = slice(g * LANES, (g + 1) * LANES)
            mine, others = recv_ref[d, :, span], other_ref[d, :, span]
            pair = (jnp.where(first, mine, others), jnp.where(first, others, mine))
            for part, line in enumerate(pair):
                at = (part * n_sky + d) * half
                if g < groups:
                    rows_ref[at + g * SUB : at + (g + 1) * SUB, 0:LANES] = line
                else:
                    for h in range(groups):
                        rows_ref[at + h * SUB : at + (h + 1) * SUB, LANES:] = jnp.where(
                            group == h, line, 0.0
                        )
    p1, p2, p3 = split3(rows_ref[...])
    if learn:
        where_tag = jnp.where(column((8, 2 * LANES), LANES + tag), 1.0, 0.0).astype(bf16)
        ids = dot(where_tag, p1, NT) + (dot(where_tag, p2, NT) + dot(where_tag, p3, NT))
        hit = iota((obj_dev, total), 0) + 1 == ids[0:1, :].astype(jnp.int32)
        member_ref[...] = jnp.where(hit, 1.0, 0.0).astype(bf16)
        member = member_ref[...]
    else:
        member = member_in_ref[...]
    sums = dot(member, p1) + (dot(member, p2) + dot(member, p3))
    q1, q2, q3 = split3(sums)
    full = full_ref[...]
    wide = dot(full, q1, NT) + (dot(full, q2, NT) + dot(full, q3, NT))
    row = iota((size_k, obj_dev), 0)
    theta = theta_ref[...]
    target = wide[size_k * size_k :] - PRIOR * (theta - init_ref[...])
    matrix = []
    for k in range(size_k):
        line = wide[k * size_k : (k + 1) * size_k]
        matrix.append(jnp.where(row == k, line + (DAMPING * line + PRIOR), line))
    inverse = []
    for p in range(size_k):
        line = matrix[p]
        inv = 1.0 / line[p : p + 1]
        inverse.append(inv)
        if p + 1 < size_k:
            scaled = jnp.where(row > p, line * inv, 0.0)
            target = target - scaled * target[p : p + 1]
            for k in range(p + 1, size_k):
                matrix[k] = matrix[k] - scaled * line[k : k + 1]
    delta = jnp.zeros_like(target)
    for p in reversed(range(size_k)):
        value = target[p : p + 1] * inverse[p]
        delta = jnp.where(row == p, value, delta)
        if p:
            target = target - matrix[p] * value
    new = theta + STEP_LIMIT * jnp.tanh(delta / STEP_LIMIT)
    new_ref[...] = new
    if pay_ref is not None:
        half = size_k // 2
        folded = jnp.concatenate([new[:half], new[half:]], axis=1)
        for d in range(n_sky):
            pay_ref[d] = folded


def hbm(x):
    return pltpu.with_memory_space_constraint(x, pltpu.HBM)


def call(kernel, out_shape, scratch=(), spaces=None, flags=None):
    specs = {}
    if spaces:
        specs["in_specs"] = [
            pl.BlockSpec(memory_space=pltpu.HBM if s == "h" else pltpu.VMEM) for s in spaces
        ]
    return pl.pallas_call(
        kernel,
        out_shape=out_shape,
        scratch_shapes=list(scratch),
        compiler_params=pltpu.CompilerParams(vmem_limit_bytes=VMEM_LIMIT, flags=flags),
        **specs,
    )


def local(
    stamps,
    stamp_gain,
    stamp_invvar,
    stamp_dest,
    stamp_obj,
    phi_tpl,
    psi_tpl,
    theta_init,
    nb_id,
    nb_weight,
):
    n_sky = lax.axis_size("sky")
    n_band = lax.axis_size("band")
    stamp_dev, bands, pix = stamps.shape
    size_k, obj_dev = theta_init.shape
    nei = nb_id.shape[1]
    cap = 2 * stamp_dev // n_sky
    half = cap // 2
    core_dev = stamp_dev // 2
    total = n_sky * cap
    n_all = n_sky * obj_dev
    extra = size_k * (size_k + 1) // 2 - LANES
    wide = LANES + -(-extra // 16) * 16
    assert n_band == 2 and half % SUB == 0 and half // SUB <= LANES // GROUP
    assert 2 * obj_dev == LANES and 0 <= extra and extra + size_k < GROUP
    shape = jax.ShapeDtypeStruct
    chunk = max(c for c in range(LANES, 1024, LANES) if pix % c == 0)

    pixels = jnp.transpose(stamps, (1, 0, 2))
    payload, keep, give, tpl, pair, sel, spread, full, base, tag, gain, owner = call(
        functools.partial(ready_kernel, (n_sky, cap, obj_dev, extra, chunk)),
        (
            shape((n_sky, 16, LANES), f32),
            shape((bands, core_dev, pix), bf16),
            shape((bands, core_dev, pix), bf16),
            shape((bands, 2 * size_k, pix), bf16),
            shape((bands, wide, pix), bf16),
            shape((n_sky * half, core_dev), bf16),
            shape((3 * size_k, 4 * LANES), bf16),
            shape((size_k * size_k + size_k, 2 * LANES), bf16),
            shape((core_dev, LANES), f32),
            shape((core_dev, LANES), f32),
            shape((8, core_dev), f32),
            shape((8, core_dev), jnp.int32),
        ),
        [
            pltpu.VMEM((bands, stamp_dev, pix), bf16),
            pltpu.VMEM((1, stamp_dev), jnp.int32),
            pltpu.VMEM((1, stamp_dev), jnp.int32),
            pltpu.VMEM((stamp_dev,), bf16),
            pltpu.VMEM((stamp_dev,), bf16),
            pltpu.VMEM((size_k, obj_dev), f32),
            pltpu.VMEM((nei, obj_dev), jnp.int32),
            pltpu.VMEM((nei, obj_dev), f32),
            pltpu.SemaphoreType.DMA((10,)),
        ],
        "h" * 10,
    )(
        hbm(stamp_dest.T),
        hbm(stamp_obj[None, :]),
        hbm(stamp_gain),
        hbm(stamp_invvar),
        hbm(phi_tpl),
        hbm(psi_tpl),
        hbm(theta_init),
        hbm(nb_id.T),
        hbm(nb_weight.T),
        hbm(pixels),
    )
    swap = [(0, 1), (1, 0)]
    keep2, tpl2, pair2 = [lax.ppermute(x, "band", swap) for x in (give, tpl, pair)]
    got = lax.all_to_all(payload, "sky", 0, 0, tiled=True)
    everyone, hot, blend = call(
        functools.partial(index_kernel, nei),
        (
            shape((n_sky, 8, LANES), f32),
            shape((n_all, core_dev), bf16),
            shape((n_all, 2 * core_dev), bf16),
        ),
        [pltpu.VMEM((16, n_all), f32)],
    )(got, owner)
    terms = call(
        functools.partial(terms_kernel, (n_sky, half, chunk, extra)),
        shape((n_sky, SUB, (half // SUB + 1) * LANES), f32),
        [
            pltpu.VMEM((size_k, n_all), f32),
            pltpu.VMEM((core_dev, 2 * LANES), f32),
            pltpu.VMEM((size_k, core_dev), f32),
            pltpu.VMEM((core_dev, 2 * size_k), bf16),
            pltpu.VMEM((n_sky * half, 2 * LANES), f32),
        ],
    )
    theta = theta_init
    member = None
    for sweep in range(ITERS):
        sent = terms(
            everyone,
            hot,
            blend,
            gain,
            base,
            tag,
            keep,
            keep2,
            tpl,
            tpl2,
            pair,
            pair2,
            sel,
            spread,
        )
        recv = lax.all_to_all(sent, "sky", 0, 0, tiled=True)
        other = lax.ppermute(recv, "band", swap)
        learn, last = sweep == 0, sweep + 1 == ITERS
        sizes = (n_sky, half, extra + size_k, learn)

        def solve(*refs, learn=learn, last=last, sizes=sizes):
            refs = list(refs)
            if learn:
                refs.insert(2, None)
            if last:
                refs.insert(6, None)
            if not learn:
                refs.insert(8, None)
            solve_kernel(sizes, *refs)

        outs = [shape((n_sky, 8, LANES), f32)] * (not last)
        outs += [shape((size_k, obj_dev), f32)]
        outs += [shape((obj_dev, total), bf16)] * learn
        given = [recv, other] + [member] * (not learn) + [full, theta, theta_init]
        outs = call(solve, outs, [pltpu.VMEM((total, 2 * LANES), f32)])(*given)
        theta = outs[0 if last else 1]
        if learn:
            member = outs[-1]
        if not last:
            everyone = lax.all_to_all(outs[0], "sky", 0, 0, tiled=True)
    return theta


def solution(mesh):
    in_specs = (
        P("sky", "band", None),
        P("sky"),
        P("sky"),
        P("sky", None),
        P("sky"),
        P("band", None, None),
        P("band", None, None),
        P(None, "sky"),
        P("sky", None),
        P("sky", None),
    )
    out_specs = P(None, "sky")
    return jax.shard_map(local, mesh=mesh, in_specs=in_specs, out_specs=out_specs, check_vma=False)
```

```python
import functools

import jax
import jax.numpy as jnp
from jax import lax
from jax.experimental import pallas as pl
from jax.experimental.pallas import tpu as pltpu
from jax.sharding import PartitionSpec as P

ITERS = 3

ROBUST = 9.0
DAMPING = 0.1
PRIOR = 1.0
STEP_LIMIT = 0.5

LANES = 128
GROUP = 32
SUB = 4
VMEM_LIMIT = 24 * 1024 * 1024

f32 = jnp.float32
bf16 = jnp.bfloat16
NT = (((1,), (1,)), ((), ()))
TN = (((0,), (0,)), ((), ()))
NN = (((1,), (0,)), ((), ()))


def dot(a, b, dims=NN, precision=None):
    return lax.dot_general(a, b, dims, precision=precision, preferred_element_type=f32)


def split3(x):
    first = x.astype(bf16)
    rest = x - first.astype(f32)
    second = rest.astype(bf16)
    third = (rest - second.astype(f32)).astype(bf16)
    return first, second, third


def iota(shape, dim):
    return lax.broadcasted_iota(jnp.int32, shape, dim)


def dma(copies):
    for copy in copies:
        copy.start()
    return copies


def wait(copies):
    for copy in copies:
        copy.wait()


def offset(k, size_k):
    return lax.div(k * (2 * size_k + 1 - k), 2)


def column(shape, m):
    lane = iota(shape, 1)
    folded = jnp.where(lane < LANES, lane, LANES + lax.rem(lane, GROUP))
    return folded == m


def ready_kernel(
    sizes,
    dest_hbm,
    obj_hbm,
    gain_hbm,
    invvar_hbm,
    phi_hbm,
    psi_hbm,
    theta_hbm,
    nbi_hbm,
    nbw_hbm,
    pix_hbm,
    pay_ref,
    keep_ref,
    give_ref,
    tpl_ref,
    pair_ref,
    sel_ref,
    wide_ref,
    full_ref,
    base_ref,
    tag_ref,
    gain_ref,
    owner_ref,
    pix_ref,
    dest_ref,
    obj_ref,
    gain_low_ref,
    invvar_ref,
    theta_ref,
    nbi_ref,
    nbw_ref,
    sem,
):
    n_sky, cap, obj_dev, extra, chunk = sizes
    bands, size_k, pix = phi_hbm.shape
    stamps = dest_ref.shape[1]
    half = cap // 2
    first = [
        pltpu.make_async_copy(phi_hbm, tpl_ref.at[:, 0:size_k, :], sem.at[0]),
        pltpu.make_async_copy(psi_hbm, tpl_ref.at[:, size_k : 2 * size_k, :], sem.at[1]),
        pltpu.make_async_copy(dest_hbm, dest_ref, sem.at[2]),
        pltpu.make_async_copy(obj_hbm, obj_ref, sem.at[3]),
        pltpu.make_async_copy(gain_hbm, gain_low_ref, sem.at[4]),
        pltpu.make_async_copy(invvar_hbm, invvar_ref, sem.at[5]),
        pltpu.make_async_copy(theta_hbm, theta_ref, sem.at[6]),
        pltpu.make_async_copy(nbi_hbm, nbi_ref, sem.at[7]),
        pltpu.make_async_copy(nbw_hbm, nbw_ref, sem.at[8]),
    ]
    last = [
        pltpu.make_async_copy(pix_hbm.at[b], pix_ref.at[b], sem.at[9 + b]) for b in range(bands)
    ]
    dma(first)
    dma(last)

    pairs = LANES + extra
    shape = (pair_ref.shape[1], size_k)
    m = iota(shape, 0)
    k = iota(shape, 1)
    lows = jnp.where((m >= offset(k, size_k)) & (m < offset(k + 1, size_k)), 1.0, 0.0)
    of_m = jnp.sum(lows * k.astype(f32), axis=1, keepdims=True).astype(jnp.int32)
    highs = jnp.where((m < pairs) & (m - offset(of_m, size_k) + of_m == k), 1.0, 0.0)
    lows_highs = jnp.concatenate([lows, highs], axis=0).astype(bf16)
    many = pair_ref.shape[1]

    shape = (size_k, 2 * LANES)
    k = iota(shape, 0)
    lane = iota(shape, 1)
    spot = pairs + k
    left = (lane >= offset(k, size_k)) & (lane < offset(k + 1, size_k))
    left = jnp.where(left | (lane == spot), 1.0, 0.0)
    lane_k = jnp.sum(jnp.where(lane >= offset(k + 1, size_k), 1, 0), axis=0, keepdims=True)
    right = (lane[0:1] - offset(lane_k, size_k) + lane_k == k) & (lane < pairs)
    both = jnp.concatenate([left, jnp.where(right, 1.0, 0.0)], axis=1).astype(bf16)
    for part in range(3):
        wide_ref[part * size_k : (part + 1) * size_k, :] = both

    shape = full_ref.shape
    r = iota((shape[0], 1), 0)
    a, b = lax.div(r, size_k), lax.rem(r, size_k)
    low, high = jnp.minimum(a, b), jnp.maximum(a, b)
    m = jnp.where(r < size_k * size_k, offset(low, size_k) + high - low, pairs + b)
    full_ref[...] = jnp.where(column(shape, m), 1.0, 0.0).astype(bf16)

    wait(first)
    theta = theta_ref[...]
    folded = jnp.concatenate([theta[: size_k // 2], theta[size_k // 2 :]], axis=1)
    side = jnp.concatenate([nbi_ref[...].astype(f32), nbw_ref[...]], axis=1)
    side = jnp.concatenate([side, jnp.zeros((8 - side.shape[0], LANES), f32)], axis=0)
    for d in range(n_sky):
        pay_ref[d, 0:8, :] = folded
        pay_ref[d, 8:16, :] = side
    dest = dest_ref[...]
    obj = obj_ref[...]
    along = jnp.broadcast_to(dest.astype(f32), (stamps, stamps))
    down = along.T
    before = iota((stamps, stamps), 0) < iota((stamps, stamps), 1)
    rank = jnp.sum(jnp.where(before & (along == down), 1.0, 0.0), axis=0, keepdims=True)
    lower = jnp.sum(jnp.where(down < along, 1.0, 0.0), axis=0, keepdims=True)
    rank = rank.astype(jnp.int32)
    order = lower.astype(jnp.int32) + rank
    spot = lax.div(order, 2)
    here = lax.rem(order, 2) == lax.axis_index("band")
    match = iota((stamps // 2, stamps), 0) == spot
    mine = jnp.where(match & here, 1.0, 0.0).astype(bf16)
    theirs = jnp.where(match & jnp.logical_not(here), 1.0, 0.0).astype(bf16)
    parted = jnp.concatenate([mine, theirs], axis=0)
    about = jnp.concatenate(
        [
            gain_low_ref[...].astype(f32).reshape(1, stamps),
            1.0 / invvar_ref[...].astype(f32).reshape(1, stamps),
            (dest * obj_dev + obj).astype(f32),
            (obj + 1).astype(f32),
            (dest * half + lax.div(rank, 2)).astype(f32),
            jnp.zeros((3, stamps), f32),
        ],
        axis=0,
    )
    p1, p2, p3 = split3(about)
    about = dot(p1, mine, NT) + (dot(p2, mine, NT) + dot(p3, mine, NT))
    count = stamps // 2
    gain_ref[...] = jnp.broadcast_to(about[0:1], gain_ref.shape)
    base_ref[...] = jnp.broadcast_to(about[1:2], (LANES, count)).T
    owner_ref[...] = jnp.broadcast_to(about[2:3].astype(jnp.int32), owner_ref.shape)
    named = jnp.broadcast_to(about[3:4], (LANES, count)).T
    tag_ref[...] = jnp.where(iota((count, LANES), 1) == extra + size_k, named, 0.0)
    place = about[4:5].astype(jnp.int32)
    sel_ref[...] = jnp.where(iota(sel_ref.shape, 0) == place, 1.0, 0.0).astype(bf16)
    for b in range(bands):
        for c in range(pix // chunk):
            px = slice(c * chunk, (c + 1) * chunk)
            phi = tpl_ref[b, 0:size_k, px]
            two = dot(lows_highs, phi)
            pair_ref[b, :, px] = (two[:many] * two[many:]).astype(bf16)
    for b in range(bands):
        last[b].wait()
        for c in range(pix // chunk):
            px = slice(c * chunk, (c + 1) * chunk)
            seen = pix_ref[b, :, px]
            rows = dot(parted, seen).astype(bf16)
            keep_ref[b, :, px] = rows[:count]
            give_ref[b, :, px] = rows[count:]


def unfold(ref, rows, lane, i, left):
    x, y = ref[2 * i, rows, :], ref[2 * i + 1, rows, :]
    if left:
        return jnp.where(lane < LANES // 2, x, pltpu.roll(y, LANES // 2, 1))
    return jnp.where(lane < LANES // 2, pltpu.roll(x, LANES // 2, 1), y)


def index_kernel(nei, got_ref, owner_ref, theta_ref, hot_ref, blend_ref, table_ref):
    n_sky = got_ref.shape[0]
    n_all, stamps = hot_ref.shape
    block = LANES
    owner = owner_ref[0:1, :]

    def hot(i, carry):
        rows = pl.ds(pl.multiple_of(i * block, block), block)
        hit = iota((block, stamps), 0) + i * block == owner
        hot_ref[rows, :] = jnp.where(hit, 1.0, 0.0).astype(bf16)
        return carry

    lax.fori_loop(0, n_all // block, hot, 0)
    lane = iota((8, LANES), 1)
    for d in range(n_sky):
        theta_ref[d] = got_ref[d, 0:8, :]
    for i in range(n_sky // 2):
        span = slice(i * LANES, (i + 1) * LANES)
        table_ref[0:8, span] = unfold(got_ref, slice(8, 16), lane, i, True)
        table_ref[8:16, span] = unfold(got_ref, slice(8, 16), lane, i, False)
    parts = jnp.concatenate(split3(table_ref[...]), axis=0)
    found = dot(parts, hot_ref[...])
    found = found[0:16] + found[16:32] + found[32:48]
    near_id = found[0:nei].astype(jnp.int32)
    near_w = found[8 : 8 + nei]

    def blend(i, carry):
        rows = pl.ds(pl.multiple_of(i * block, block), block)
        here = iota((block, stamps), 0) + i * block
        mix = jnp.zeros((block, stamps), f32)
        for j in range(nei):
            mix = mix + jnp.where(here == near_id[j : j + 1], near_w[j : j + 1], 0.0)
        high = mix.astype(bf16)
        blend_ref[rows, 0:stamps] = high
        blend_ref[rows, stamps : 2 * stamps] = (mix - high.astype(f32)).astype(bf16)
        return carry

    lax.fori_loop(0, n_all // block, blend, 0)


def terms_kernel(
    sizes,
    theta_ref,
    hot_ref,
    blend_ref,
    gain_ref,
    base_ref,
    tag_ref,
    pix_ref,
    pix2_ref,
    tpl_ref,
    tpl2_ref,
    pair_ref,
    pair2_ref,
    sel_ref,
    wide_ref,
    out_ref,
    amp_ref,
    acc_ref,
    proj_ref,
    lit_ref,
    rows_ref,
):
    n_sky, half, chunk, extra = sizes
    bands, stamps, pix = pix_ref.shape
    size_k = tpl_ref.shape[1] // 2
    seen = [ref.at[b] for ref in (pix_ref, pix2_ref) for b in range(bands)]
    tpl = [ref.at[b] for ref in (tpl_ref, tpl2_ref) for b in range(bands)]
    pair = [ref.at[b] for ref in (pair_ref, pair2_ref) for b in range(bands)]
    steps = [
        (b, slice(c * chunk, (c + 1) * chunk))
        for b in range(2 * bands)
        for c in range(pix // chunk)
    ]
    lane = iota((8, LANES), 1)
    for i in range(n_sky // 2):
        span = slice(i * LANES, (i + 1) * LANES)
        amp_ref[0:8, span] = jnp.exp(unfold(theta_ref, slice(None), lane, i, True))
        amp_ref[8:16, span] = jnp.exp(unfold(theta_ref, slice(None), lane, i, False))
    parts = jnp.concatenate(split3(amp_ref[...]), axis=0)
    got = dot(parts, hot_ref[...])
    mix = dot(parts, blend_ref[...])
    k1, k2, k3 = slice(0, size_k), slice(size_k, 2 * size_k), slice(2 * size_k, 3 * size_k)
    slot_f = got[k1] + (got[k2] + got[k3])
    high, low = mix[:, :stamps], mix[:, stamps:]
    slot_u = high[k1] + (high[k2] + low[k1] + (high[k3] + low[k2]))
    scaled = gain_ref[0:1, :] * slot_f
    lit_ref[...] = jnp.concatenate([scaled, slot_u], axis=0).T.astype(bf16)
    acc_ref[...] = jnp.zeros_like(acc_ref)
    proj_ref[...] = jnp.zeros_like(proj_ref)
    lit = lit_ref[...]
    base = jnp.concatenate([base_ref[...]] * (chunk // LANES), axis=1)
    wide = pair_ref.shape[1]

    def model(b, px):
        return dot(lit, tpl[b][:, px])

    def weigh(b, px, light):
        resid = seen[b][:, px].astype(f32) - light
        under = base + (resid * resid) * (1.0 / ROBUST)
        guess = pltpu.reciprocal(under, approx=True)
        weight = guess * (2.0 - under * guess)
        return weight.astype(bf16), (weight * resid).astype(bf16)

    def gather(b, px, weight, wres):
        acc_ref[:, 0:wide] += dot(weight, pair[b][:, px], NT)
        proj_ref[...] += dot(tpl[b][0:size_k, px], wres, NT)

    light = model(*steps[0])
    held = None
    for i, here in enumerate(steps):
        ahead = model(*steps[i + 1]) if i + 1 < len(steps) else None
        now = weigh(*here, light)
        if held is not None:
            gather(*steps[i - 1], *held)
        light, held = ahead, now
    gather(*steps[-1], *held)

    scales = dot(jnp.concatenate(split3(scaled), axis=0), wide_ref[...], TN)
    col = iota((1, 2 * LANES), 1) - (LANES + extra)
    is_grad = jnp.where((col >= 0) & (col < size_k), 1.0, 0.0)
    factor = scales[:, : 2 * LANES] * (scales[:, 2 * LANES :] + is_grad)
    proj = jnp.concatenate([jnp.zeros((extra, stamps), f32), proj_ref[...]], axis=0)
    proj = jnp.concatenate([proj, jnp.zeros((LANES - extra - size_k, stamps), f32)], axis=0)
    tail = acc_ref[:, LANES:] + proj.T
    terms = jnp.concatenate(
        [
            factor[:, :LANES] * acc_ref[:, :LANES],
            factor[:, LANES:] * tail + tag_ref[...],
        ],
        axis=1,
    )
    sel = sel_ref[...]
    t1, t2, t3 = split3(terms)
    rows_ref[...] = dot(sel, t1) + (dot(sel, t2) + dot(sel, t3))
    groups = half // SUB
    for d in range(n_sky):
        at = d * half
        for g in range(groups):
            line = rows_ref[at + g * SUB : at + (g + 1) * SUB, :]
            out_ref[d, :, g * LANES : (g + 1) * LANES] = line[:, :LANES]
            more = pltpu.roll(line[:, LANES:], g * GROUP, 1) if g else line[:, LANES:]
            tail = tail + more if g else more
        out_ref[d, :, groups * LANES :] = tail


def solve_kernel(
    sizes,
    recv_ref,
    other_ref,
    member_in_ref,
    full_ref,
    theta_ref,
    init_ref,
    pay_ref,
    new_ref,
    member_ref,
    rows_ref,
):
    n_sky, half, tag, learn = sizes
    size_k, obj_dev = theta_ref.shape
    total = 2 * n_sky * half
    groups = half // SUB
    group = iota((SUB, LANES), 1) // GROUP
    first = jnp.full((SUB, LANES), lax.axis_index("band")) == 0
    for d in range(n_sky):
        for g in range(groups + 1):
            span = slice(g * LANES, (g + 1) * LANES)
            mine, others = recv_ref[d, :, span], other_ref[d, :, span]
            pair = (jnp.where(first, mine, others), jnp.where(first, others, mine))
            for part, line in enumerate(pair):
                at = (part * n_sky + d) * half
                if g < groups:
                    rows_ref[at + g * SUB : at + (g + 1) * SUB, 0:LANES] = line
                else:
                    for h in range(groups):
                        rows_ref[at + h * SUB : at + (h + 1) * SUB, LANES:] = jnp.where(
                            group == h, line, 0.0
                        )
    p1, p2, p3 = split3(rows_ref[...])
    if learn:
        where_tag = jnp.where(column((8, 2 * LANES), LANES + tag), 1.0, 0.0).astype(bf16)
        ids = dot(where_tag, p1, NT) + (dot(where_tag, p2, NT) + dot(where_tag, p3, NT))
        hit = iota((obj_dev, total), 0) + 1 == ids[0:1, :].astype(jnp.int32)
        member_ref[...] = jnp.where(hit, 1.0, 0.0).astype(bf16)
        member = member_ref[...]
    else:
        member = member_in_ref[...]
    sums = dot(member, p1) + (dot(member, p2) + dot(member, p3))
    q1, q2, q3 = split3(sums)
    full = full_ref[...]
    wide = dot(full, q1, NT) + (dot(full, q2, NT) + dot(full, q3, NT))
    row = iota((size_k, obj_dev), 0)
    theta = theta_ref[...]
    target = wide[size_k * size_k :] - PRIOR * (theta - init_ref[...])
    matrix = []
    for k in range(size_k):
        line = wide[k * size_k : (k + 1) * size_k]
        matrix.append(jnp.where(row == k, line + (DAMPING * line + PRIOR), line))
    inverse = []
    for p in range(size_k):
        line = matrix[p]
        inv = 1.0 / line[p : p + 1]
        inverse.append(inv)
        if p + 1 < size_k:
            scaled = jnp.where(row > p, line * inv, 0.0)
            target = target - scaled * target[p : p + 1]
            for k in range(p + 1, size_k):
                matrix[k] = matrix[k] - scaled * line[k : k + 1]
    delta = jnp.zeros_like(target)
    for p in reversed(range(size_k)):
        value = target[p : p + 1] * inverse[p]
        delta = jnp.where(row == p, value, delta)
        if p:
            target = target - matrix[p] * value
    new = theta + STEP_LIMIT * jnp.tanh(delta / STEP_LIMIT)
    new_ref[...] = new
    if pay_ref is not None:
        half = size_k // 2
        folded = jnp.concatenate([new[:half], new[half:]], axis=1)
        for d in range(n_sky):
            pay_ref[d] = folded


def hbm(x):
    return pltpu.with_memory_space_constraint(x, pltpu.HBM)


def call(kernel, out_shape, scratch=(), spaces=None, flags=None):
    specs = {}
    if spaces:
        specs["in_specs"] = [
            pl.BlockSpec(memory_space=pltpu.HBM if s == "h" else pltpu.VMEM) for s in spaces
        ]
    return pl.pallas_call(
        kernel,
        out_shape=out_shape,
        scratch_shapes=list(scratch),
        compiler_params=pltpu.CompilerParams(vmem_limit_bytes=VMEM_LIMIT, flags=flags),
        **specs,
    )


def local(
    stamps,
    stamp_gain,
    stamp_invvar,
    stamp_dest,
    stamp_obj,
    phi_tpl,
    psi_tpl,
    theta_init,
    nb_id,
    nb_weight,
):
    n_sky = lax.axis_size("sky")
    n_band = lax.axis_size("band")
    stamp_dev, bands, pix = stamps.shape
    size_k, obj_dev = theta_init.shape
    nei = nb_id.shape[1]
    cap = 2 * stamp_dev // n_sky
    half = cap // 2
    core_dev = stamp_dev // 2
    total = n_sky * cap
    n_all = n_sky * obj_dev
    extra = size_k * (size_k + 1) // 2 - LANES
    wide = LANES + -(-extra // 16) * 16
    assert n_band == 2 and half % SUB == 0 and half // SUB <= LANES // GROUP
    assert 2 * obj_dev == LANES and 0 <= extra and extra + size_k < GROUP
    shape = jax.ShapeDtypeStruct
    chunk = max(c for c in range(LANES, 1024, LANES) if pix % c == 0)

    pixels = jnp.transpose(stamps, (1, 0, 2))
    payload, keep, give, tpl, pair, sel, spread, full, base, tag, gain, owner = call(
        functools.partial(ready_kernel, (n_sky, cap, obj_dev, extra, chunk)),
        (
            shape((n_sky, 16, LANES), f32),
            shape((bands, core_dev, pix), bf16),
            shape((bands, core_dev, pix), bf16),
            shape((bands, 2 * size_k, pix), bf16),
            shape((bands, wide, pix), bf16),
            shape((n_sky * half, core_dev), bf16),
            shape((3 * size_k, 4 * LANES), bf16),
            shape((size_k * size_k + size_k, 2 * LANES), bf16),
            shape((core_dev, LANES), f32),
            shape((core_dev, LANES), f32),
            shape((8, core_dev), f32),
            shape((8, core_dev), jnp.int32),
        ),
        [
            pltpu.VMEM((bands, stamp_dev, pix), bf16),
            pltpu.VMEM((1, stamp_dev), jnp.int32),
            pltpu.VMEM((1, stamp_dev), jnp.int32),
            pltpu.VMEM((stamp_dev,), bf16),
            pltpu.VMEM((stamp_dev,), bf16),
            pltpu.VMEM((size_k, obj_dev), f32),
            pltpu.VMEM((nei, obj_dev), jnp.int32),
            pltpu.VMEM((nei, obj_dev), f32),
            pltpu.SemaphoreType.DMA((9 + bands,)),
        ],
        "h" * 10,
    )(
        hbm(stamp_dest.T),
        hbm(stamp_obj[None, :]),
        hbm(stamp_gain),
        hbm(stamp_invvar),
        hbm(phi_tpl),
        hbm(psi_tpl),
        hbm(theta_init),
        hbm(nb_id.T),
        hbm(nb_weight.T),
        hbm(pixels),
    )
    swap = [(0, 1), (1, 0)]
    keep2, tpl2, pair2 = [lax.ppermute(x, "band", swap) for x in (give, tpl, pair)]
    got = lax.all_to_all(payload, "sky", 0, 0, tiled=True)
    everyone, hot, blend = call(
        functools.partial(index_kernel, nei),
        (
            shape((n_sky, 8, LANES), f32),
            shape((n_all, core_dev), bf16),
            shape((n_all, 2 * core_dev), bf16),
        ),
        [pltpu.VMEM((16, n_all), f32)],
    )(got, owner)
    terms = call(
        functools.partial(terms_kernel, (n_sky, half, chunk, extra)),
        shape((n_sky, SUB, (half // SUB + 1) * LANES), f32),
        [
            pltpu.VMEM((size_k, n_all), f32),
            pltpu.VMEM((core_dev, 2 * LANES), f32),
            pltpu.VMEM((size_k, core_dev), f32),
            pltpu.VMEM((core_dev, 2 * size_k), bf16),
            pltpu.VMEM((n_sky * half, 2 * LANES), f32),
        ],
    )
    theta = theta_init
    member = None
    for sweep in range(ITERS):
        sent = terms(
            everyone,
            hot,
            blend,
            gain,
            base,
            tag,
            keep,
            keep2,
            tpl,
            tpl2,
            pair,
            pair2,
            sel,
            spread,
        )
        recv = lax.all_to_all(sent, "sky", 0, 0, tiled=True)
        other = lax.ppermute(recv, "band", swap)
        learn, last = sweep == 0, sweep + 1 == ITERS
        sizes = (n_sky, half, extra + size_k, learn)

        def solve(*refs, learn=learn, last=last, sizes=sizes):
            refs = list(refs)
            if learn:
                refs.insert(2, None)
            if last:
                refs.insert(6, None)
            if not learn:
                refs.insert(8, None)
            solve_kernel(sizes, *refs)

        outs = [shape((n_sky, 8, LANES), f32)] * (not last)
        outs += [shape((size_k, obj_dev), f32)]
        outs += [shape((obj_dev, total), bf16)] * learn
        given = [recv, other] + [member] * (not learn) + [full, theta, theta_init]
        outs = call(solve, outs, [pltpu.VMEM((total, 2 * LANES), f32)])(*given)
        theta = outs[0 if last else 1]
        if learn:
            member = outs[-1]
        if not last:
            everyone = lax.all_to_all(outs[0], "sky", 0, 0, tiled=True)
    return theta


def solution(mesh):
    in_specs = (
        P("sky", "band", None),
        P("sky"),
        P("sky"),
        P("sky", None),
        P("sky"),
        P("band", None, None),
        P("band", None, None),
        P(None, "sky"),
        P("sky", None),
        P("sky", None),
    )
    out_specs = P(None, "sky")
    return jax.shard_map(local, mesh=mesh, in_specs=in_specs, out_specs=out_specs, check_vma=False)
```

```python
import functools

import jax
import jax.numpy as jnp
from jax import lax
from jax.experimental import pallas as pl
from jax.experimental.pallas import tpu as pltpu
from jax.sharding import PartitionSpec as P

ITERS = 3

ROBUST = 9.0
DAMPING = 0.1
PRIOR = 1.0
STEP_LIMIT = 0.5

LANES = 128
GROUP = 32
SUB = 4
VMEM_LIMIT = 24 * 1024 * 1024

f32 = jnp.float32
bf16 = jnp.bfloat16
NT = (((1,), (1,)), ((), ()))
TN = (((0,), (0,)), ((), ()))
NN = (((1,), (0,)), ((), ()))


def dot(a, b, dims=NN, precision=None):
    return lax.dot_general(a, b, dims, precision=precision, preferred_element_type=f32)


def split3(x):
    first = x.astype(bf16)
    rest = x - first.astype(f32)
    second = rest.astype(bf16)
    third = (rest - second.astype(f32)).astype(bf16)
    return first, second, third


def iota(shape, dim):
    return lax.broadcasted_iota(jnp.int32, shape, dim)


def dma(copies):
    for copy in copies:
        copy.start()
    return copies


def wait(copies):
    for copy in copies:
        copy.wait()


def column(shape, m):
    lane = iota(shape, 1)
    folded = jnp.where(lane < LANES, lane, LANES + lax.rem(lane, GROUP))
    return folded == m


def ready_kernel(
    sizes,
    dest_hbm,
    obj_hbm,
    gain_hbm,
    invvar_hbm,
    phi_hbm,
    psi_hbm,
    theta_hbm,
    nbi_hbm,
    nbw_hbm,
    pix_hbm,
    pay_ref,
    keep_ref,
    give_ref,
    tpl_ref,
    pair_ref,
    sel_ref,
    wide_ref,
    full_ref,
    base_ref,
    tag_ref,
    gain_ref,
    owner_ref,
    pix_ref,
    dest_ref,
    obj_ref,
    gain_low_ref,
    invvar_ref,
    theta_ref,
    nbi_ref,
    nbw_ref,
    sem,
):
    n_sky, cap, obj_dev, extra, chunk = sizes
    bands, size_k, pix = phi_hbm.shape
    stamps = dest_ref.shape[1]
    half = cap // 2
    first = [
        pltpu.make_async_copy(phi_hbm, tpl_ref.at[:, 0:size_k, :], sem.at[0]),
        pltpu.make_async_copy(psi_hbm, tpl_ref.at[:, size_k : 2 * size_k, :], sem.at[1]),
        pltpu.make_async_copy(dest_hbm, dest_ref, sem.at[2]),
        pltpu.make_async_copy(obj_hbm, obj_ref, sem.at[3]),
        pltpu.make_async_copy(gain_hbm, gain_low_ref, sem.at[4]),
        pltpu.make_async_copy(invvar_hbm, invvar_ref, sem.at[5]),
        pltpu.make_async_copy(theta_hbm, theta_ref, sem.at[6]),
        pltpu.make_async_copy(nbi_hbm, nbi_ref, sem.at[7]),
        pltpu.make_async_copy(nbw_hbm, nbw_ref, sem.at[8]),
    ]
    last = [pltpu.make_async_copy(pix_hbm, pix_ref, sem.at[9])]
    dma(first)
    dma(last)

    pairs = LANES + extra
    shape = (size_k, 2 * LANES)
    k = iota(shape, 0)
    lane = iota(shape, 1)
    spot = pairs + k
    lane_k = lax.rem(lane, size_k)
    left = ((lane_k == k) & (lane < pairs)) | (lane == spot)
    left = jnp.where(left, 1.0, 0.0)
    right = (lax.rem(lane_k + lax.div(lane, size_k), size_k) == k) & (lane < pairs)
    both = jnp.concatenate([left, jnp.where(right, 1.0, 0.0)], axis=1).astype(bf16)
    for part in range(3):
        wide_ref[part * size_k : (part + 1) * size_k, :] = both

    shape = full_ref.shape
    r = iota((shape[0], 1), 0)
    a, b = lax.div(r, size_k), lax.rem(r, size_k)
    ahead = lax.rem(b - a + size_k, size_k)
    near = (2 * ahead < size_k) | ((2 * ahead == size_k) & (2 * a < size_k))
    m = jnp.where(near, ahead * size_k + a, lax.rem(size_k - ahead, size_k) * size_k + b)
    m = jnp.where(r < size_k * size_k, m, pairs + b)
    full_ref[...] = jnp.where(column(shape, m), 1.0, 0.0).astype(bf16)

    wait(first)
    theta = theta_ref[...]
    folded = jnp.concatenate([theta[: size_k // 2], theta[size_k // 2 :]], axis=1)
    side = jnp.concatenate([nbi_ref[...].astype(f32), nbw_ref[...]], axis=1)
    side = jnp.concatenate([side, jnp.zeros((8 - side.shape[0], LANES), f32)], axis=0)
    for d in range(n_sky):
        pay_ref[d, 0:8, :] = folded
        pay_ref[d, 8:16, :] = side
    dest = dest_ref[...]
    obj = obj_ref[...]
    along = jnp.broadcast_to(dest.astype(f32), (stamps, stamps))
    down = along.T
    before = iota((stamps, stamps), 0) < iota((stamps, stamps), 1)
    rank = jnp.sum(jnp.where(before & (along == down), 1.0, 0.0), axis=0, keepdims=True)
    lower = jnp.sum(jnp.where(down < along, 1.0, 0.0), axis=0, keepdims=True)
    rank = rank.astype(jnp.int32)
    order = lower.astype(jnp.int32) + rank
    spot = lax.div(order, 2)
    here = lax.rem(order, 2) == lax.axis_index("band")
    match = iota((stamps // 2, stamps), 0) == spot
    mine = jnp.where(match & here, 1.0, 0.0).astype(bf16)
    theirs = jnp.where(match & jnp.logical_not(here), 1.0, 0.0).astype(bf16)
    parted = jnp.concatenate([mine, theirs], axis=0)
    about = jnp.concatenate(
        [
            gain_low_ref[...].astype(f32).reshape(1, stamps),
            1.0 / invvar_ref[...].astype(f32).reshape(1, stamps),
            (dest * obj_dev + obj).astype(f32),
            (obj + 1).astype(f32),
            (dest * half + lax.div(rank, 2)).astype(f32),
            jnp.zeros((3, stamps), f32),
        ],
        axis=0,
    )
    p1, p2, p3 = split3(about)
    about = dot(p1, mine, NT) + (dot(p2, mine, NT) + dot(p3, mine, NT))
    count = stamps // 2
    gain_ref[...] = jnp.broadcast_to(about[0:1], gain_ref.shape)
    base_ref[...] = jnp.broadcast_to(about[1:2], (LANES, count)).T
    owner_ref[...] = jnp.broadcast_to(about[2:3].astype(jnp.int32), owner_ref.shape)
    named = jnp.broadcast_to(about[3:4], (LANES, count)).T
    tag_ref[...] = jnp.where(iota((count, LANES), 1) == extra + size_k, named, 0.0)
    place = about[4:5].astype(jnp.int32)
    sel_ref[...] = jnp.where(iota(sel_ref.shape, 0) == place, 1.0, 0.0).astype(bf16)
    for b in range(bands):
        for c in range(pix // chunk):
            px = slice(c * chunk, (c + 1) * chunk)
            phi = tpl_ref[b, 0:size_k, px].astype(f32)
            for j in range(size_k // 2):
                turned = pltpu.roll(phi, size_k - j, 0) if j else phi
                rows = slice(j * size_k, (j + 1) * size_k)
                pair_ref[b, rows, px] = (phi * turned).astype(bf16)
            across = phi[:extra] * phi[extra:]
            rest = jnp.zeros((pair_ref.shape[1] - pairs, chunk), f32)
            pair_ref[b, LANES:, px] = jnp.concatenate([across, rest], axis=0).astype(bf16)
    wait(last)
    for b in range(bands):
        for c in range(pix // chunk):
            px = slice(c * chunk, (c + 1) * chunk)
            seen = pix_ref[b, :, px]
            rows = dot(parted, seen).astype(bf16)
            keep_ref[b, :, px] = rows[:count]
            give_ref[b, :, px] = rows[count:]


def unfold(ref, rows, lane, i, left):
    x, y = ref[2 * i, rows, :], ref[2 * i + 1, rows, :]
    if left:
        return jnp.where(lane < LANES // 2, x, pltpu.roll(y, LANES // 2, 1))
    return jnp.where(lane < LANES // 2, pltpu.roll(x, LANES // 2, 1), y)


def index_kernel(nei, got_ref, owner_ref, theta_ref, hot_ref, blend_ref, table_ref):
    n_sky = got_ref.shape[0]
    n_all, stamps = hot_ref.shape
    block = LANES
    owner = owner_ref[0:1, :]

    def hot(i, carry):
        rows = pl.ds(pl.multiple_of(i * block, block), block)
        hit = iota((block, stamps), 0) + i * block == owner
        hot_ref[rows, :] = jnp.where(hit, 1.0, 0.0).astype(bf16)
        return carry

    lax.fori_loop(0, n_all // block, hot, 0)
    lane = iota((8, LANES), 1)
    for d in range(n_sky):
        theta_ref[d] = got_ref[d, 0:8, :]
    for i in range(n_sky // 2):
        span = slice(i * LANES, (i + 1) * LANES)
        table_ref[0:8, span] = unfold(got_ref, slice(8, 16), lane, i, True)
        table_ref[8:16, span] = unfold(got_ref, slice(8, 16), lane, i, False)
    parts = jnp.concatenate(split3(table_ref[...]), axis=0)
    found = dot(parts, hot_ref[...])
    found = found[0:16] + found[16:32] + found[32:48]
    near_id = found[0:nei].astype(jnp.int32)
    near_w = found[8 : 8 + nei]

    def blend(i, carry):
        rows = pl.ds(pl.multiple_of(i * block, block), block)
        here = iota((block, stamps), 0) + i * block
        mix = jnp.zeros((block, stamps), f32)
        for j in range(nei):
            mix = mix + jnp.where(here == near_id[j : j + 1], near_w[j : j + 1], 0.0)
        high = mix.astype(bf16)
        blend_ref[rows, 0:stamps] = high
        blend_ref[rows, stamps : 2 * stamps] = (mix - high.astype(f32)).astype(bf16)
        return carry

    lax.fori_loop(0, n_all // block, blend, 0)


def terms_kernel(
    sizes,
    theta_ref,
    hot_ref,
    blend_ref,
    gain_ref,
    base_ref,
    tag_ref,
    pix_ref,
    pix2_ref,
    tpl_ref,
    tpl2_ref,
    pair_ref,
    pair2_ref,
    sel_ref,
    wide_ref,
    out_ref,
    amp_ref,
    acc_ref,
    proj_ref,
    lit_ref,
    rows_ref,
):
    n_sky, half, chunk, extra = sizes
    bands, stamps, pix = pix_ref.shape
    size_k = tpl_ref.shape[1] // 2
    seen = [ref.at[b] for ref in (pix_ref, pix2_ref) for b in range(bands)]
    tpl = [ref.at[b] for ref in (tpl_ref, tpl2_ref) for b in range(bands)]
    pair = [ref.at[b] for ref in (pair_ref, pair2_ref) for b in range(bands)]
    steps = [
        (b, slice(c * chunk, (c + 1) * chunk))
        for b in range(2 * bands)
        for c in range(pix // chunk)
    ]
    lane = iota((8, LANES), 1)
    for i in range(n_sky // 2):
        span = slice(i * LANES, (i + 1) * LANES)
        amp_ref[0:8, span] = jnp.exp(unfold(theta_ref, slice(None), lane, i, True))
        amp_ref[8:16, span] = jnp.exp(unfold(theta_ref, slice(None), lane, i, False))
    parts = jnp.concatenate(split3(amp_ref[...]), axis=0)
    got = dot(parts, hot_ref[...])
    mix = dot(parts, blend_ref[...])
    k1, k2, k3 = slice(0, size_k), slice(size_k, 2 * size_k), slice(2 * size_k, 3 * size_k)
    slot_f = got[k1] + (got[k2] + got[k3])
    high, low = mix[:, :stamps], mix[:, stamps:]
    slot_u = high[k1] + (high[k2] + low[k1] + (high[k3] + low[k2]))
    scaled = gain_ref[0:1, :] * slot_f
    lit_ref[...] = jnp.concatenate([scaled, slot_u], axis=0).T.astype(bf16)
    acc_ref[...] = jnp.zeros_like(acc_ref)
    proj_ref[...] = jnp.zeros_like(proj_ref)
    lit = lit_ref[...]
    base = jnp.concatenate([base_ref[...]] * (chunk // LANES), axis=1)
    wide = pair_ref.shape[1]

    def model(b, px):
        return dot(lit, tpl[b][:, px])

    def weigh(b, px, light):
        resid = seen[b][:, px].astype(f32) - light
        under = base + (resid * resid) * (1.0 / ROBUST)
        guess = pltpu.reciprocal(under, approx=True)
        weight = guess * (2.0 - under * guess)
        return weight.astype(bf16), (weight * resid).astype(bf16)

    def gather(b, px, weight, wres):
        acc_ref[:, 0:wide] += dot(weight, pair[b][:, px], NT)
        proj_ref[...] += dot(tpl[b][0:size_k, px], wres, NT)

    light = model(*steps[0])
    held = None
    for i, here in enumerate(steps):
        ahead = model(*steps[i + 1]) if i + 1 < len(steps) else None
        now = weigh(*here, light)
        if held is not None:
            gather(*steps[i - 1], *held)
        light, held = ahead, now
    gather(*steps[-1], *held)

    scales = dot(jnp.concatenate(split3(scaled), axis=0), wide_ref[...], TN)
    col = iota((1, 2 * LANES), 1) - (LANES + extra)
    is_grad = jnp.where((col >= 0) & (col < size_k), 1.0, 0.0)
    factor = scales[:, : 2 * LANES] * (scales[:, 2 * LANES :] + is_grad)
    proj = jnp.concatenate([jnp.zeros((extra, stamps), f32), proj_ref[...]], axis=0)
    proj = jnp.concatenate([proj, jnp.zeros((LANES - extra - size_k, stamps), f32)], axis=0)
    tail = acc_ref[:, LANES:] + proj.T
    terms = jnp.concatenate(
        [
            factor[:, :LANES] * acc_ref[:, :LANES],
            factor[:, LANES:] * tail + tag_ref[...],
        ],
        axis=1,
    )
    sel = sel_ref[...]
    t1, t2, t3 = split3(terms)
    rows_ref[...] = dot(sel, t1) + (dot(sel, t2) + dot(sel, t3))
    groups = half // SUB
    for d in range(n_sky):
        at = d * half
        for g in range(groups):
            line = rows_ref[at + g * SUB : at + (g + 1) * SUB, :]
            out_ref[d, :, g * LANES : (g + 1) * LANES] = line[:, :LANES]
            more = pltpu.roll(line[:, LANES:], g * GROUP, 1) if g else line[:, LANES:]
            tail = tail + more if g else more
        out_ref[d, :, groups * LANES :] = tail


def solve_kernel(
    sizes,
    recv_ref,
    other_ref,
    member_in_ref,
    full_ref,
    theta_ref,
    init_ref,
    pay_ref,
    new_ref,
    member_ref,
    rows_ref,
):
    n_sky, half, tag, learn = sizes
    size_k, obj_dev = theta_ref.shape
    total = 2 * n_sky * half
    groups = half // SUB
    group = iota((SUB, LANES), 1) // GROUP
    first = jnp.full((SUB, LANES), lax.axis_index("band")) == 0
    for d in range(n_sky):
        for g in range(groups + 1):
            span = slice(g * LANES, (g + 1) * LANES)
            mine, others = recv_ref[d, :, span], other_ref[d, :, span]
            pair = (jnp.where(first, mine, others), jnp.where(first, others, mine))
            for part, line in enumerate(pair):
                at = (part * n_sky + d) * half
                if g < groups:
                    rows_ref[at + g * SUB : at + (g + 1) * SUB, 0:LANES] = line
                else:
                    for h in range(groups):
                        rows_ref[at + h * SUB : at + (h + 1) * SUB, LANES:] = jnp.where(
                            group == h, line, 0.0
                        )
    p1, p2, p3 = split3(rows_ref[...])
    if learn:
        where_tag = jnp.where(column((8, 2 * LANES), LANES + tag), 1.0, 0.0).astype(bf16)
        ids = dot(where_tag, p1, NT) + (dot(where_tag, p2, NT) + dot(where_tag, p3, NT))
        hit = iota((obj_dev, total), 0) + 1 == ids[0:1, :].astype(jnp.int32)
        member_ref[...] = jnp.where(hit, 1.0, 0.0).astype(bf16)
        member = member_ref[...]
    else:
        member = member_in_ref[...]
    sums = dot(member, p1) + (dot(member, p2) + dot(member, p3))
    q1, q2, q3 = split3(sums)
    full = full_ref[...]
    wide = dot(full, q1, NT) + (dot(full, q2, NT) + dot(full, q3, NT))
    row = iota((size_k, obj_dev), 0)
    theta = theta_ref[...]
    target = wide[size_k * size_k :] - PRIOR * (theta - init_ref[...])
    matrix = []
    for k in range(size_k):
        line = wide[k * size_k : (k + 1) * size_k]
        matrix.append(jnp.where(row == k, line + (DAMPING * line + PRIOR), line))
    inverse = []
    for p in range(size_k):
        line = matrix[p]
        inv = 1.0 / line[p : p + 1]
        inverse.append(inv)
        if p + 1 < size_k:
            scaled = jnp.where(row > p, line * inv, 0.0)
            target = target - scaled * target[p : p + 1]
            for k in range(p + 1, size_k):
                matrix[k] = matrix[k] - scaled * line[k : k + 1]
    delta = jnp.zeros_like(target)
    for p in reversed(range(size_k)):
        value = target[p : p + 1] * inverse[p]
        delta = jnp.where(row == p, value, delta)
        if p:
            target = target - matrix[p] * value
    new = theta + STEP_LIMIT * jnp.tanh(delta / STEP_LIMIT)
    new_ref[...] = new
    if pay_ref is not None:
        half = size_k // 2
        folded = jnp.concatenate([new[:half], new[half:]], axis=1)
        for d in range(n_sky):
            pay_ref[d] = folded


def hbm(x):
    return pltpu.with_memory_space_constraint(x, pltpu.HBM)


def call(kernel, out_shape, scratch=(), spaces=None, flags=None):
    specs = {}
    if spaces:
        specs["in_specs"] = [
            pl.BlockSpec(memory_space=pltpu.HBM if s == "h" else pltpu.VMEM) for s in spaces
        ]
    return pl.pallas_call(
        kernel,
        out_shape=out_shape,
        scratch_shapes=list(scratch),
        compiler_params=pltpu.CompilerParams(vmem_limit_bytes=VMEM_LIMIT, flags=flags),
        **specs,
    )


def local(
    stamps,
    stamp_gain,
    stamp_invvar,
    stamp_dest,
    stamp_obj,
    phi_tpl,
    psi_tpl,
    theta_init,
    nb_id,
    nb_weight,
):
    n_sky = lax.axis_size("sky")
    n_band = lax.axis_size("band")
    stamp_dev, bands, pix = stamps.shape
    size_k, obj_dev = theta_init.shape
    nei = nb_id.shape[1]
    cap = 2 * stamp_dev // n_sky
    half = cap // 2
    core_dev = stamp_dev // 2
    total = n_sky * cap
    n_all = n_sky * obj_dev
    extra = size_k * (size_k + 1) // 2 - LANES
    wide = LANES + -(-extra // 16) * 16
    assert n_band == 2 and half % SUB == 0 and half // SUB <= LANES // GROUP
    assert 2 * obj_dev == LANES and size_k * size_k == 2 * LANES and extra + size_k < GROUP
    shape = jax.ShapeDtypeStruct
    chunk = max(c for c in range(LANES, 1024, LANES) if pix % c == 0)

    pixels = jnp.transpose(stamps, (1, 0, 2))
    payload, keep, give, tpl, pair, sel, spread, full, base, tag, gain, owner = call(
        functools.partial(ready_kernel, (n_sky, cap, obj_dev, extra, chunk)),
        (
            shape((n_sky, 16, LANES), f32),
            shape((bands, core_dev, pix), bf16),
            shape((bands, core_dev, pix), bf16),
            shape((bands, 2 * size_k, pix), bf16),
            shape((bands, wide, pix), bf16),
            shape((n_sky * half, core_dev), bf16),
            shape((3 * size_k, 4 * LANES), bf16),
            shape((size_k * size_k + size_k, 2 * LANES), bf16),
            shape((core_dev, LANES), f32),
            shape((core_dev, LANES), f32),
            shape((8, core_dev), f32),
            shape((8, core_dev), jnp.int32),
        ),
        [
            pltpu.VMEM((bands, stamp_dev, pix), bf16),
            pltpu.VMEM((1, stamp_dev), jnp.int32),
            pltpu.VMEM((1, stamp_dev), jnp.int32),
            pltpu.VMEM((stamp_dev,), bf16),
            pltpu.VMEM((stamp_dev,), bf16),
            pltpu.VMEM((size_k, obj_dev), f32),
            pltpu.VMEM((nei, obj_dev), jnp.int32),
            pltpu.VMEM((nei, obj_dev), f32),
            pltpu.SemaphoreType.DMA((10,)),
        ],
        "h" * 10,
    )(
        hbm(stamp_dest.T),
        hbm(stamp_obj[None, :]),
        hbm(stamp_gain),
        hbm(stamp_invvar),
        hbm(phi_tpl),
        hbm(psi_tpl),
        hbm(theta_init),
        hbm(nb_id.T),
        hbm(nb_weight.T),
        hbm(pixels),
    )
    swap = [(0, 1), (1, 0)]
    keep2, tpl2, pair2 = [lax.ppermute(x, "band", swap) for x in (give, tpl, pair)]
    got = lax.all_to_all(payload, "sky", 0, 0, tiled=True)
    everyone, hot, blend = call(
        functools.partial(index_kernel, nei),
        (
            shape((n_sky, 8, LANES), f32),
            shape((n_all, core_dev), bf16),
            shape((n_all, 2 * core_dev), bf16),
        ),
        [pltpu.VMEM((16, n_all), f32)],
    )(got, owner)
    terms = call(
        functools.partial(terms_kernel, (n_sky, half, chunk, extra)),
        shape((n_sky, SUB, (half // SUB + 1) * LANES), f32),
        [
            pltpu.VMEM((size_k, n_all), f32),
            pltpu.VMEM((core_dev, 2 * LANES), f32),
            pltpu.VMEM((size_k, core_dev), f32),
            pltpu.VMEM((core_dev, 2 * size_k), bf16),
            pltpu.VMEM((n_sky * half, 2 * LANES), f32),
        ],
    )
    theta = theta_init
    member = None
    for sweep in range(ITERS):
        sent = terms(
            everyone,
            hot,
            blend,
            gain,
            base,
            tag,
            keep,
            keep2,
            tpl,
            tpl2,
            pair,
            pair2,
            sel,
            spread,
        )
        recv = lax.all_to_all(sent, "sky", 0, 0, tiled=True)
        other = lax.ppermute(recv, "band", swap)
        learn, last = sweep == 0, sweep + 1 == ITERS
        sizes = (n_sky, half, extra + size_k, learn)

        def solve(*refs, learn=learn, last=last, sizes=sizes):
            refs = list(refs)
            if learn:
                refs.insert(2, None)
            if last:
                refs.insert(6, None)
            if not learn:
                refs.insert(8, None)
            solve_kernel(sizes, *refs)

        outs = [shape((n_sky, 8, LANES), f32)] * (not last)
        outs += [shape((size_k, obj_dev), f32)]
        outs += [shape((obj_dev, total), bf16)] * learn
        given = [recv, other] + [member] * (not learn) + [full, theta, theta_init]
        outs = call(solve, outs, [pltpu.VMEM((total, 2 * LANES), f32)])(*given)
        theta = outs[0 if last else 1]
        if learn:
            member = outs[-1]
        if not last:
            everyone = lax.all_to_all(outs[0], "sky", 0, 0, tiled=True)
    return theta


def solution(mesh):
    in_specs = (
        P("sky", "band", None),
        P("sky"),
        P("sky"),
        P("sky", None),
        P("sky"),
        P("band", None, None),
        P("band", None, None),
        P(None, "sky"),
        P("sky", None),
        P("sky", None),
    )
    out_specs = P(None, "sky")
    return jax.shard_map(local, mesh=mesh, in_specs=in_specs, out_specs=out_specs, check_vma=False)
```

```python
import functools

import jax
import jax.numpy as jnp
from jax import lax
from jax.experimental import pallas as pl
from jax.experimental.pallas import tpu as pltpu
from jax.sharding import PartitionSpec as P

ITERS = 3

ROBUST = 9.0
DAMPING = 0.1
PRIOR = 1.0
STEP_LIMIT = 0.5

LANES = 128
GROUP = 32
SUB = 4
VMEM_LIMIT = 24 * 1024 * 1024

f32 = jnp.float32
bf16 = jnp.bfloat16
NT = (((1,), (1,)), ((), ()))
TN = (((0,), (0,)), ((), ()))
NN = (((1,), (0,)), ((), ()))


def dot(a, b, dims=NN, precision=None):
    return lax.dot_general(a, b, dims, precision=precision, preferred_element_type=f32)


def split3(x):
    first = x.astype(bf16)
    rest = x - first.astype(f32)
    second = rest.astype(bf16)
    third = (rest - second.astype(f32)).astype(bf16)
    return first, second, third


def iota(shape, dim):
    return lax.broadcasted_iota(jnp.int32, shape, dim)


def dma(copies):
    for copy in copies:
        copy.start()
    return copies


def wait(copies):
    for copy in copies:
        copy.wait()


def column(shape, m):
    lane = iota(shape, 1)
    folded = jnp.where(lane < LANES, lane, LANES + lax.rem(lane, GROUP))
    return folded == m


def ready_kernel(
    sizes,
    dest_hbm,
    obj_hbm,
    gain_hbm,
    invvar_hbm,
    phi_hbm,
    psi_hbm,
    theta_hbm,
    nbi_hbm,
    nbw_hbm,
    pix_hbm,
    pay_ref,
    keep_ref,
    give_ref,
    tpl_ref,
    pair_ref,
    sel_ref,
    wide_ref,
    full_ref,
    base_ref,
    tag_ref,
    gain_ref,
    owner_ref,
    pix_ref,
    dest_ref,
    obj_ref,
    gain_low_ref,
    invvar_ref,
    theta_ref,
    nbi_ref,
    nbw_ref,
    sem,
):
    n_sky, cap, obj_dev, extra, chunk = sizes
    bands, size_k, pix = phi_hbm.shape
    stamps = dest_ref.shape[1]
    half = cap // 2
    first = [
        pltpu.make_async_copy(phi_hbm, tpl_ref.at[:, 0:size_k, :], sem.at[0]),
        pltpu.make_async_copy(psi_hbm, tpl_ref.at[:, size_k : 2 * size_k, :], sem.at[1]),
        pltpu.make_async_copy(dest_hbm, dest_ref, sem.at[2]),
        pltpu.make_async_copy(obj_hbm, obj_ref, sem.at[3]),
        pltpu.make_async_copy(gain_hbm, gain_low_ref, sem.at[4]),
        pltpu.make_async_copy(invvar_hbm, invvar_ref, sem.at[5]),
        pltpu.make_async_copy(theta_hbm, theta_ref, sem.at[6]),
        pltpu.make_async_copy(nbi_hbm, nbi_ref, sem.at[7]),
        pltpu.make_async_copy(nbw_hbm, nbw_ref, sem.at[8]),
    ]
    last = [
        pltpu.make_async_copy(pix_hbm.at[b], pix_ref.at[b], sem.at[9 + b]) for b in range(bands)
    ]
    dma(first)
    dma(last)

    pairs = LANES + extra
    shape = (size_k, 2 * LANES)
    k = iota(shape, 0)
    lane = iota(shape, 1)
    spot = pairs + k
    lane_k = lax.rem(lane, size_k)
    left = ((lane_k == k) & (lane < pairs)) | (lane == spot)
    left = jnp.where(left, 1.0, 0.0)
    right = (lax.rem(lane_k + lax.div(lane, size_k), size_k) == k) & (lane < pairs)
    both = jnp.concatenate([left, jnp.where(right, 1.0, 0.0)], axis=1).astype(bf16)
    for part in range(3):
        wide_ref[part * size_k : (part + 1) * size_k, :] = both

    shape = full_ref.shape
    r = iota((shape[0], 1), 0)
    a, b = lax.div(r, size_k), lax.rem(r, size_k)
    ahead = lax.rem(b - a + size_k, size_k)
    near = (2 * ahead < size_k) | ((2 * ahead == size_k) & (2 * a < size_k))
    m = jnp.where(near, ahead * size_k + a, lax.rem(size_k - ahead, size_k) * size_k + b)
    m = jnp.where(r < size_k * size_k, m, pairs + b)
    full_ref[...] = jnp.where(column(shape, m), 1.0, 0.0).astype(bf16)

    wait(first)
    theta = theta_ref[...]
    folded = jnp.concatenate([theta[: size_k // 2], theta[size_k // 2 :]], axis=1)
    side = jnp.concatenate([nbi_ref[...].astype(f32), nbw_ref[...]], axis=1)
    side = jnp.concatenate([side, jnp.zeros((8 - side.shape[0], LANES), f32)], axis=0)
    for d in range(n_sky):
        pay_ref[d, 0:8, :] = folded
        pay_ref[d, 8:16, :] = side
    dest = dest_ref[...]
    obj = obj_ref[...]
    along = jnp.broadcast_to(dest.astype(f32), (stamps, stamps))
    down = along.T
    before = iota((stamps, stamps), 0) < iota((stamps, stamps), 1)
    rank = jnp.sum(jnp.where(before & (along == down), 1.0, 0.0), axis=0, keepdims=True)
    lower = jnp.sum(jnp.where(down < along, 1.0, 0.0), axis=0, keepdims=True)
    rank = rank.astype(jnp.int32)
    order = lower.astype(jnp.int32) + rank
    spot = lax.div(order, 2)
    here = lax.rem(order, 2) == lax.axis_index("band")
    match = iota((stamps // 2, stamps), 0) == spot
    mine = jnp.where(match & here, 1.0, 0.0).astype(bf16)
    theirs = jnp.where(match & jnp.logical_not(here), 1.0, 0.0).astype(bf16)
    parted = jnp.concatenate([mine, theirs], axis=0)
    about = jnp.concatenate(
        [
            gain_low_ref[...].astype(f32).reshape(1, stamps),
            1.0 / invvar_ref[...].astype(f32).reshape(1, stamps),
            (dest * obj_dev + obj).astype(f32),
            (obj + 1).astype(f32),
            (dest * half + lax.div(rank, 2)).astype(f32),
            jnp.zeros((3, stamps), f32),
        ],
        axis=0,
    )
    p1, p2, p3 = split3(about)
    about = dot(p1, mine, NT) + (dot(p2, mine, NT) + dot(p3, mine, NT))
    count = stamps // 2
    gain_ref[...] = jnp.broadcast_to(about[0:1], gain_ref.shape)
    base_ref[...] = jnp.broadcast_to(about[1:2], (LANES, count)).T
    owner_ref[...] = jnp.broadcast_to(about[2:3].astype(jnp.int32), owner_ref.shape)
    named = jnp.broadcast_to(about[3:4], (LANES, count)).T
    tag_ref[...] = jnp.where(iota((count, LANES), 1) == extra + size_k, named, 0.0)
    place = about[4:5].astype(jnp.int32)
    sel_ref[...] = jnp.where(iota(sel_ref.shape, 0) == place, 1.0, 0.0).astype(bf16)
    for b in range(bands):
        for c in range(pix // chunk):
            px = slice(c * chunk, (c + 1) * chunk)
            phi = tpl_ref[b, 0:size_k, px].astype(f32)
            for j in range(size_k // 2):
                turned = pltpu.roll(phi, size_k - j, 0) if j else phi
                rows = slice(j * size_k, (j + 1) * size_k)
                pair_ref[b, rows, px] = (phi * turned).astype(bf16)
            across = phi[:extra] * phi[extra:]
            rest = jnp.zeros((pair_ref.shape[1] - pairs, chunk), f32)
            pair_ref[b, LANES:, px] = jnp.concatenate([across, rest], axis=0).astype(bf16)
    for b in range(bands):
        last[b].wait()
        for c in range(pix // chunk):
            px = slice(c * chunk, (c + 1) * chunk)
            seen = pix_ref[b, :, px]
            rows = dot(parted, seen).astype(bf16)
            keep_ref[b, :, px] = rows[:count]
            give_ref[b, :, px] = rows[count:]


def unfold(ref, rows, lane, i, left):
    x, y = ref[2 * i, rows, :], ref[2 * i + 1, rows, :]
    if left:
        return jnp.where(lane < LANES // 2, x, pltpu.roll(y, LANES // 2, 1))
    return jnp.where(lane < LANES // 2, pltpu.roll(x, LANES // 2, 1), y)


def index_kernel(nei, got_ref, owner_ref, theta_ref, hot_ref, blend_ref, table_ref):
    n_sky = got_ref.shape[0]
    n_all, stamps = hot_ref.shape
    block = LANES
    owner = owner_ref[0:1, :]

    def hot(i, carry):
        rows = pl.ds(pl.multiple_of(i * block, block), block)
        hit = iota((block, stamps), 0) + i * block == owner
        hot_ref[rows, :] = jnp.where(hit, 1.0, 0.0).astype(bf16)
        return carry

    lax.fori_loop(0, n_all // block, hot, 0)
    lane = iota((8, LANES), 1)
    for d in range(n_sky):
        theta_ref[d] = got_ref[d, 0:8, :]
    for i in range(n_sky // 2):
        span = slice(i * LANES, (i + 1) * LANES)
        table_ref[0:8, span] = unfold(got_ref, slice(8, 16), lane, i, True)
        table_ref[8:16, span] = unfold(got_ref, slice(8, 16), lane, i, False)
    parts = jnp.concatenate(split3(table_ref[...]), axis=0)
    found = dot(parts, hot_ref[...])
    found = found[0:16] + found[16:32] + found[32:48]
    near_id = found[0:nei].astype(jnp.int32)
    near_w = found[8 : 8 + nei]

    def blend(i, carry):
        rows = pl.ds(pl.multiple_of(i * block, block), block)
        here = iota((block, stamps), 0) + i * block
        mix = jnp.zeros((block, stamps), f32)
        for j in range(nei):
            mix = mix + jnp.where(here == near_id[j : j + 1], near_w[j : j + 1], 0.0)
        high = mix.astype(bf16)
        blend_ref[rows, 0:stamps] = high
        blend_ref[rows, stamps : 2 * stamps] = (mix - high.astype(f32)).astype(bf16)
        return carry

    lax.fori_loop(0, n_all // block, blend, 0)


def terms_kernel(
    sizes,
    theta_ref,
    hot_ref,
    blend_ref,
    gain_ref,
    base_ref,
    tag_ref,
    pix_ref,
    pix2_ref,
    tpl_ref,
    tpl2_ref,
    pair_ref,
    pair2_ref,
    sel_ref,
    wide_ref,
    out_ref,
    amp_ref,
    acc_ref,
    proj_ref,
    lit_ref,
    rows_ref,
):
    n_sky, half, chunk, extra = sizes
    bands, stamps, pix = pix_ref.shape
    size_k = tpl_ref.shape[1] // 2
    seen = [ref.at[b] for ref in (pix_ref, pix2_ref) for b in range(bands)]
    tpl = [ref.at[b] for ref in (tpl_ref, tpl2_ref) for b in range(bands)]
    pair = [ref.at[b] for ref in (pair_ref, pair2_ref) for b in range(bands)]
    steps = [
        (b, slice(c * chunk, (c + 1) * chunk))
        for b in range(2 * bands)
        for c in range(pix // chunk)
    ]
    lane = iota((8, LANES), 1)
    for i in range(n_sky // 2):
        span = slice(i * LANES, (i + 1) * LANES)
        amp_ref[0:8, span] = jnp.exp(unfold(theta_ref, slice(None), lane, i, True))
        amp_ref[8:16, span] = jnp.exp(unfold(theta_ref, slice(None), lane, i, False))
    parts = jnp.concatenate(split3(amp_ref[...]), axis=0)
    got = dot(parts, hot_ref[...])
    mix = dot(parts, blend_ref[...])
    k1, k2, k3 = slice(0, size_k), slice(size_k, 2 * size_k), slice(2 * size_k, 3 * size_k)
    slot_f = got[k1] + (got[k2] + got[k3])
    high, low = mix[:, :stamps], mix[:, stamps:]
    slot_u = high[k1] + (high[k2] + low[k1] + (high[k3] + low[k2]))
    scaled = gain_ref[0:1, :] * slot_f
    lit_ref[...] = jnp.concatenate([scaled, slot_u], axis=0).T.astype(bf16)
    acc_ref[...] = jnp.zeros_like(acc_ref)
    proj_ref[...] = jnp.zeros_like(proj_ref)
    lit = lit_ref[...]
    base = jnp.concatenate([base_ref[...]] * (chunk // LANES), axis=1)
    wide = pair_ref.shape[1]

    def model(b, px):
        return dot(lit, tpl[b][:, px])

    def weigh(b, px, light):
        resid = seen[b][:, px].astype(f32) - light
        under = base + (resid * resid) * (1.0 / ROBUST)
        guess = pltpu.reciprocal(under, approx=True)
        weight = guess * (2.0 - under * guess)
        return weight.astype(bf16), (weight * resid).astype(bf16)

    def gather(b, px, weight, wres):
        acc_ref[:, 0:wide] += dot(weight, pair[b][:, px], NT)
        proj_ref[...] += dot(tpl[b][0:size_k, px], wres, NT)

    light = model(*steps[0])
    held = None
    for i, here in enumerate(steps):
        ahead = model(*steps[i + 1]) if i + 1 < len(steps) else None
        now = weigh(*here, light)
        if held is not None:
            gather(*steps[i - 1], *held)
        light, held = ahead, now
    gather(*steps[-1], *held)

    scales = dot(jnp.concatenate(split3(scaled), axis=0), wide_ref[...], TN)
    col = iota((1, 2 * LANES), 1) - (LANES + extra)
    is_grad = jnp.where((col >= 0) & (col < size_k), 1.0, 0.0)
    factor = scales[:, : 2 * LANES] * (scales[:, 2 * LANES :] + is_grad)
    proj = jnp.concatenate([jnp.zeros((extra, stamps), f32), proj_ref[...]], axis=0)
    proj = jnp.concatenate([proj, jnp.zeros((LANES - extra - size_k, stamps), f32)], axis=0)
    tail = acc_ref[:, LANES:] + proj.T
    terms = jnp.concatenate(
        [
            factor[:, :LANES] * acc_ref[:, :LANES],
            factor[:, LANES:] * tail + tag_ref[...],
        ],
        axis=1,
    )
    sel = sel_ref[...]
    t1, t2, t3 = split3(terms)
    rows_ref[...] = dot(sel, t1) + (dot(sel, t2) + dot(sel, t3))
    groups = half // SUB
    for d in range(n_sky):
        at = d * half
        for g in range(groups):
            line = rows_ref[at + g * SUB : at + (g + 1) * SUB, :]
            out_ref[d, :, g * LANES : (g + 1) * LANES] = line[:, :LANES]
            more = pltpu.roll(line[:, LANES:], g * GROUP, 1) if g else line[:, LANES:]
            tail = tail + more if g else more
        out_ref[d, :, groups * LANES :] = tail


def solve_kernel(
    sizes,
    recv_ref,
    other_ref,
    member_in_ref,
    full_ref,
    theta_ref,
    init_ref,
    pay_ref,
    new_ref,
    member_ref,
    rows_ref,
):
    n_sky, half, tag, learn = sizes
    size_k, obj_dev = theta_ref.shape
    total = 2 * n_sky * half
    groups = half // SUB
    group = iota((SUB, LANES), 1) // GROUP
    first = jnp.full((SUB, LANES), lax.axis_index("band")) == 0
    for d in range(n_sky):
        for g in range(groups + 1):
            span = slice(g * LANES, (g + 1) * LANES)
            mine, others = recv_ref[d, :, span], other_ref[d, :, span]
            pair = (jnp.where(first, mine, others), jnp.where(first, others, mine))
            for part, line in enumerate(pair):
                at = (part * n_sky + d) * half
                if g < groups:
                    rows_ref[at + g * SUB : at + (g + 1) * SUB, 0:LANES] = line
                else:
                    for h in range(groups):
                        rows_ref[at + h * SUB : at + (h + 1) * SUB, LANES:] = jnp.where(
                            group == h, line, 0.0
                        )
    p1, p2, p3 = split3(rows_ref[...])
    if learn:
        where_tag = jnp.where(column((8, 2 * LANES), LANES + tag), 1.0, 0.0).astype(bf16)
        ids = dot(where_tag, p1, NT) + (dot(where_tag, p2, NT) + dot(where_tag, p3, NT))
        hit = iota((obj_dev, total), 0) + 1 == ids[0:1, :].astype(jnp.int32)
        member_ref[...] = jnp.where(hit, 1.0, 0.0).astype(bf16)
        member = member_ref[...]
    else:
        member = member_in_ref[...]
    sums = dot(member, p1) + (dot(member, p2) + dot(member, p3))
    q1, q2, q3 = split3(sums)
    full = full_ref[...]
    wide = dot(full, q1, NT) + (dot(full, q2, NT) + dot(full, q3, NT))
    row = iota((size_k, obj_dev), 0)
    theta = theta_ref[...]
    target = wide[size_k * size_k :] - PRIOR * (theta - init_ref[...])
    matrix = []
    for k in range(size_k):
        line = wide[k * size_k : (k + 1) * size_k]
        matrix.append(jnp.where(row == k, line + (DAMPING * line + PRIOR), line))
    inverse = []
    for p in range(size_k):
        line = matrix[p]
        inv = 1.0 / line[p : p + 1]
        inverse.append(inv)
        if p + 1 < size_k:
            scaled = jnp.where(row > p, line * inv, 0.0)
            target = target - scaled * target[p : p + 1]
            for k in range(p + 1, size_k):
                matrix[k] = matrix[k] - scaled * line[k : k + 1]
    delta = jnp.zeros_like(target)
    for p in reversed(range(size_k)):
        value = target[p : p + 1] * inverse[p]
        delta = jnp.where(row == p, value, delta)
        if p:
            target = target - matrix[p] * value
    new = theta + STEP_LIMIT * jnp.tanh(delta / STEP_LIMIT)
    new_ref[...] = new
    if pay_ref is not None:
        half = size_k // 2
        folded = jnp.concatenate([new[:half], new[half:]], axis=1)
        for d in range(n_sky):
            pay_ref[d] = folded


def hbm(x):
    return pltpu.with_memory_space_constraint(x, pltpu.HBM)


def call(kernel, out_shape, scratch=(), spaces=None, flags=None):
    specs = {}
    if spaces:
        specs["in_specs"] = [
            pl.BlockSpec(memory_space=pltpu.HBM if s == "h" else pltpu.VMEM) for s in spaces
        ]
    return pl.pallas_call(
        kernel,
        out_shape=out_shape,
        scratch_shapes=list(scratch),
        compiler_params=pltpu.CompilerParams(vmem_limit_bytes=VMEM_LIMIT, flags=flags),
        **specs,
    )


def local(
    stamps,
    stamp_gain,
    stamp_invvar,
    stamp_dest,
    stamp_obj,
    phi_tpl,
    psi_tpl,
    theta_init,
    nb_id,
    nb_weight,
):
    n_sky = lax.axis_size("sky")
    n_band = lax.axis_size("band")
    stamp_dev, bands, pix = stamps.shape
    size_k, obj_dev = theta_init.shape
    nei = nb_id.shape[1]
    cap = 2 * stamp_dev // n_sky
    half = cap // 2
    core_dev = stamp_dev // 2
    total = n_sky * cap
    n_all = n_sky * obj_dev
    extra = size_k * (size_k + 1) // 2 - LANES
    wide = LANES + -(-extra // 16) * 16
    assert n_band == 2 and half % SUB == 0 and half // SUB <= LANES // GROUP
    assert 2 * obj_dev == LANES and size_k * size_k == 2 * LANES and extra + size_k < GROUP
    shape = jax.ShapeDtypeStruct
    chunk = max(c for c in range(LANES, 1024, LANES) if pix % c == 0)

    pixels = jnp.transpose(stamps, (1, 0, 2))
    payload, keep, give, tpl, pair, sel, spread, full, base, tag, gain, owner = call(
        functools.partial(ready_kernel, (n_sky, cap, obj_dev, extra, chunk)),
        (
            shape((n_sky, 16, LANES), f32),
            shape((bands, core_dev, pix), bf16),
            shape((bands, core_dev, pix), bf16),
            shape((bands, 2 * size_k, pix), bf16),
            shape((bands, wide, pix), bf16),
            shape((n_sky * half, core_dev), bf16),
            shape((3 * size_k, 4 * LANES), bf16),
            shape((size_k * size_k + size_k, 2 * LANES), bf16),
            shape((core_dev, LANES), f32),
            shape((core_dev, LANES), f32),
            shape((8, core_dev), f32),
            shape((8, core_dev), jnp.int32),
        ),
        [
            pltpu.VMEM((bands, stamp_dev, pix), bf16),
            pltpu.VMEM((1, stamp_dev), jnp.int32),
            pltpu.VMEM((1, stamp_dev), jnp.int32),
            pltpu.VMEM((stamp_dev,), bf16),
            pltpu.VMEM((stamp_dev,), bf16),
            pltpu.VMEM((size_k, obj_dev), f32),
            pltpu.VMEM((nei, obj_dev), jnp.int32),
            pltpu.VMEM((nei, obj_dev), f32),
            pltpu.SemaphoreType.DMA((9 + bands,)),
        ],
        "h" * 10,
    )(
        hbm(stamp_dest.T),
        hbm(stamp_obj[None, :]),
        hbm(stamp_gain),
        hbm(stamp_invvar),
        hbm(phi_tpl),
        hbm(psi_tpl),
        hbm(theta_init),
        hbm(nb_id.T),
        hbm(nb_weight.T),
        hbm(pixels),
    )
    swap = [(0, 1), (1, 0)]
    keep2, tpl2, pair2 = [lax.ppermute(x, "band", swap) for x in (give, tpl, pair)]
    got = lax.all_to_all(payload, "sky", 0, 0, tiled=True)
    everyone, hot, blend = call(
        functools.partial(index_kernel, nei),
        (
            shape((n_sky, 8, LANES), f32),
            shape((n_all, core_dev), bf16),
            shape((n_all, 2 * core_dev), bf16),
        ),
        [pltpu.VMEM((16, n_all), f32)],
    )(got, owner)
    terms = call(
        functools.partial(terms_kernel, (n_sky, half, chunk, extra)),
        shape((n_sky, SUB, (half // SUB + 1) * LANES), f32),
        [
            pltpu.VMEM((size_k, n_all), f32),
            pltpu.VMEM((core_dev, 2 * LANES), f32),
            pltpu.VMEM((size_k, core_dev), f32),
            pltpu.VMEM((core_dev, 2 * size_k), bf16),
            pltpu.VMEM((n_sky * half, 2 * LANES), f32),
        ],
    )
    theta = theta_init
    member = None
    for sweep in range(ITERS):
        sent = terms(
            everyone,
            hot,
            blend,
            gain,
            base,
            tag,
            keep,
            keep2,
            tpl,
            tpl2,
            pair,
            pair2,
            sel,
            spread,
        )
        recv = lax.all_to_all(sent, "sky", 0, 0, tiled=True)
        other = lax.ppermute(recv, "band", swap)
        learn, last = sweep == 0, sweep + 1 == ITERS
        sizes = (n_sky, half, extra + size_k, learn)

        def solve(*refs, learn=learn, last=last, sizes=sizes):
            refs = list(refs)
            if learn:
                refs.insert(2, None)
            if last:
                refs.insert(6, None)
            if not learn:
                refs.insert(8, None)
            solve_kernel(sizes, *refs)

        outs = [shape((n_sky, 8, LANES), f32)] * (not last)
        outs += [shape((size_k, obj_dev), f32)]
        outs += [shape((obj_dev, total), bf16)] * learn
        given = [recv, other] + [member] * (not learn) + [full, theta, theta_init]
        outs = call(solve, outs, [pltpu.VMEM((total, 2 * LANES), f32)])(*given)
        theta = outs[0 if last else 1]
        if learn:
            member = outs[-1]
        if not last:
            everyone = lax.all_to_all(outs[0], "sky", 0, 0, tiled=True)
    return theta


def solution(mesh):
    in_specs = (
        P("sky", "band", None),
        P("sky"),
        P("sky"),
        P("sky", None),
        P("sky"),
        P("band", None, None),
        P("band", None, None),
        P(None, "sky"),
        P("sky", None),
        P("sky", None),
    )
    out_specs = P(None, "sky")
    return jax.shard_map(local, mesh=mesh, in_specs=in_specs, out_specs=out_specs, check_vma=False)
```

```python
import functools

import jax
import jax.numpy as jnp
from jax import lax
from jax.experimental import pallas as pl
from jax.experimental.pallas import tpu as pltpu
from jax.sharding import PartitionSpec as P

ITERS = 3

ROBUST = 9.0
DAMPING = 0.1
PRIOR = 1.0
STEP_LIMIT = 0.5

LANES = 128
GROUP = 32
SUB = 4
VMEM_LIMIT = 24 * 1024 * 1024

f32 = jnp.float32
bf16 = jnp.bfloat16
NT = (((1,), (1,)), ((), ()))
TN = (((0,), (0,)), ((), ()))
NN = (((1,), (0,)), ((), ()))


def dot(a, b, dims=NN, precision=None):
    return lax.dot_general(a, b, dims, precision=precision, preferred_element_type=f32)


def split3(x):
    first = x.astype(bf16)
    rest = x - first.astype(f32)
    second = rest.astype(bf16)
    third = (rest - second.astype(f32)).astype(bf16)
    return first, second, third


def iota(shape, dim):
    return lax.broadcasted_iota(jnp.int32, shape, dim)


def dma(copies):
    for copy in copies:
        copy.start()
    return copies


def wait(copies):
    for copy in copies:
        copy.wait()


def column(shape, m):
    lane = iota(shape, 1)
    folded = jnp.where(lane < LANES, lane, LANES + lax.rem(lane, GROUP))
    return folded == m


def ready_kernel(
    sizes,
    dest_hbm,
    obj_hbm,
    gain_hbm,
    invvar_hbm,
    phi_hbm,
    psi_hbm,
    theta_hbm,
    nbi_hbm,
    nbw_hbm,
    pix_hbm,
    pay_ref,
    keep_ref,
    ship_ref,
    sel_ref,
    wide_ref,
    full_ref,
    base_ref,
    tag_ref,
    gain_ref,
    owner_ref,
    pix_ref,
    dest_ref,
    obj_ref,
    gain_low_ref,
    invvar_ref,
    theta_ref,
    nbi_ref,
    nbw_ref,
    sem,
):
    n_sky, cap, obj_dev, extra, chunk = sizes
    bands, size_k, pix = phi_hbm.shape
    stamps = dest_ref.shape[1]
    half = cap // 2
    count = keep_ref.shape[1]
    give_ref = ship_ref.at[:, 0:count, :]
    tpl_ref = ship_ref.at[:, count : count + 2 * size_k, :]
    pair_ref = ship_ref.at[:, count + 2 * size_k :, :]
    first = [
        pltpu.make_async_copy(phi_hbm, tpl_ref.at[:, 0:size_k, :], sem.at[0]),
        pltpu.make_async_copy(psi_hbm, tpl_ref.at[:, size_k : 2 * size_k, :], sem.at[1]),
        pltpu.make_async_copy(dest_hbm, dest_ref, sem.at[2]),
        pltpu.make_async_copy(obj_hbm, obj_ref, sem.at[3]),
        pltpu.make_async_copy(gain_hbm, gain_low_ref, sem.at[4]),
        pltpu.make_async_copy(invvar_hbm, invvar_ref, sem.at[5]),
        pltpu.make_async_copy(theta_hbm, theta_ref, sem.at[6]),
        pltpu.make_async_copy(nbi_hbm, nbi_ref, sem.at[7]),
        pltpu.make_async_copy(nbw_hbm, nbw_ref, sem.at[8]),
    ]
    last = [pltpu.make_async_copy(pix_hbm, pix_ref, sem.at[9])]
    dma(first)
    dma(last)

    pairs = LANES + extra
    shape = (size_k, 2 * LANES)
    k = iota(shape, 0)
    lane = iota(shape, 1)
    spot = pairs + k
    lane_k = lax.rem(lane, size_k)
    left = ((lane_k == k) & (lane < pairs)) | (lane == spot)
    left = jnp.where(left, 1.0, 0.0)
    right = (lax.rem(lane_k + lax.div(lane, size_k), size_k) == k) & (lane < pairs)
    both = jnp.concatenate([left, jnp.where(right, 1.0, 0.0)], axis=1).astype(bf16)
    for part in range(3):
        wide_ref[part * size_k : (part + 1) * size_k, :] = both

    shape = full_ref.shape
    r = iota((shape[0], 1), 0)
    a, b = lax.div(r, size_k), lax.rem(r, size_k)
    ahead = lax.rem(b - a + size_k, size_k)
    near = (2 * ahead < size_k) | ((2 * ahead == size_k) & (2 * a < size_k))
    m = jnp.where(near, ahead * size_k + a, lax.rem(size_k - ahead, size_k) * size_k + b)
    m = jnp.where(r < size_k * size_k, m, pairs + b)
    full_ref[...] = jnp.where(column(shape, m), 1.0, 0.0).astype(bf16)

    wait(first)
    theta = theta_ref[...]
    folded = jnp.concatenate([theta[: size_k // 2], theta[size_k // 2 :]], axis=1)
    side = jnp.concatenate([nbi_ref[...].astype(f32), nbw_ref[...]], axis=1)
    side = jnp.concatenate([side, jnp.zeros((8 - side.shape[0], LANES), f32)], axis=0)
    for d in range(n_sky):
        pay_ref[d, 0:8, :] = folded
        pay_ref[d, 8:16, :] = side
    dest = dest_ref[...]
    obj = obj_ref[...]
    along = jnp.broadcast_to(dest.astype(f32), (stamps, stamps))
    down = along.T
    before = iota((stamps, stamps), 0) < iota((stamps, stamps), 1)
    rank = jnp.sum(jnp.where(before & (along == down), 1.0, 0.0), axis=0, keepdims=True)
    lower = jnp.sum(jnp.where(down < along, 1.0, 0.0), axis=0, keepdims=True)
    rank = rank.astype(jnp.int32)
    order = lower.astype(jnp.int32) + rank
    spot = lax.div(order, 2)
    here = lax.rem(order, 2) == lax.axis_index("band")
    match = iota((stamps // 2, stamps), 0) == spot
    mine = jnp.where(match & here, 1.0, 0.0).astype(bf16)
    theirs = jnp.where(match & jnp.logical_not(here), 1.0, 0.0).astype(bf16)
    parted = jnp.concatenate([mine, theirs], axis=0)
    about = jnp.concatenate(
        [
            gain_low_ref[...].astype(f32).reshape(1, stamps),
            1.0 / invvar_ref[...].astype(f32).reshape(1, stamps),
            (dest * obj_dev + obj).astype(f32),
            (obj + 1).astype(f32),
            (dest * half + lax.div(rank, 2)).astype(f32),
            jnp.zeros((3, stamps), f32),
        ],
        axis=0,
    )
    p1, p2, p3 = split3(about)
    about = dot(p1, mine, NT) + (dot(p2, mine, NT) + dot(p3, mine, NT))
    count = stamps // 2
    gain_ref[...] = jnp.broadcast_to(about[0:1], gain_ref.shape)
    base_ref[...] = jnp.broadcast_to(about[1:2], (LANES, count)).T
    owner_ref[...] = jnp.broadcast_to(about[2:3].astype(jnp.int32), owner_ref.shape)
    named = jnp.broadcast_to(about[3:4], (LANES, count)).T
    tag_ref[...] = jnp.where(iota((count, LANES), 1) == extra + size_k, named, 0.0)
    place = about[4:5].astype(jnp.int32)
    sel_ref[...] = jnp.where(iota(sel_ref.shape, 0) == place, 1.0, 0.0).astype(bf16)
    for b in range(bands):
        for c in range(pix // chunk):
            px = slice(c * chunk, (c + 1) * chunk)
            phi = tpl_ref[b, 0:size_k, px].astype(f32)
            for j in range(size_k // 2):
                turned = pltpu.roll(phi, size_k - j, 0) if j else phi
                rows = slice(j * size_k, (j + 1) * size_k)
                pair_ref[b, rows, px] = (phi * turned).astype(bf16)
            across = phi[:extra] * phi[extra:]
            rest = jnp.zeros((pair_ref.shape[1] - pairs, chunk), f32)
            pair_ref[b, LANES:, px] = jnp.concatenate([across, rest], axis=0).astype(bf16)
    wait(last)
    for b in range(bands):
        for c in range(pix // chunk):
            px = slice(c * chunk, (c + 1) * chunk)
            seen = pix_ref[b, :, px]
            rows = dot(parted, seen).astype(bf16)
            keep_ref[b, :, px] = rows[:count]
            give_ref[b, :, px] = rows[count:]


def unfold(ref, rows, lane, i, left):
    x, y = ref[2 * i, rows, :], ref[2 * i + 1, rows, :]
    if left:
        return jnp.where(lane < LANES // 2, x, pltpu.roll(y, LANES // 2, 1))
    return jnp.where(lane < LANES // 2, pltpu.roll(x, LANES // 2, 1), y)


def index_kernel(nei, got_ref, owner_ref, theta_ref, hot_ref, blend_ref, table_ref):
    n_sky = got_ref.shape[0]
    n_all, stamps = hot_ref.shape
    block = LANES
    owner = owner_ref[0:1, :]

    def hot(i, carry):
        rows = pl.ds(pl.multiple_of(i * block, block), block)
        hit = iota((block, stamps), 0) + i * block == owner
        hot_ref[rows, :] = jnp.where(hit, 1.0, 0.0).astype(bf16)
        return carry

    lax.fori_loop(0, n_all // block, hot, 0)
    lane = iota((8, LANES), 1)
    for d in range(n_sky):
        theta_ref[d] = got_ref[d, 0:8, :]
    for i in range(n_sky // 2):
        span = slice(i * LANES, (i + 1) * LANES)
        table_ref[0:8, span] = unfold(got_ref, slice(8, 16), lane, i, True)
        table_ref[8:16, span] = unfold(got_ref, slice(8, 16), lane, i, False)
    parts = jnp.concatenate(split3(table_ref[...]), axis=0)
    found = dot(parts, hot_ref[...])
    found = found[0:16] + found[16:32] + found[32:48]
    near_id = found[0:nei].astype(jnp.int32)
    near_w = found[8 : 8 + nei]

    def blend(i, carry):
        rows = pl.ds(pl.multiple_of(i * block, block), block)
        here = iota((block, stamps), 0) + i * block
        mix = jnp.zeros((block, stamps), f32)
        for j in range(nei):
            mix = mix + jnp.where(here == near_id[j : j + 1], near_w[j : j + 1], 0.0)
        high = mix.astype(bf16)
        blend_ref[rows, 0:stamps] = high
        blend_ref[rows, stamps : 2 * stamps] = (mix - high.astype(f32)).astype(bf16)
        return carry

    lax.fori_loop(0, n_all // block, blend, 0)


def terms_kernel(
    sizes,
    theta_ref,
    hot_ref,
    blend_ref,
    gain_ref,
    base_ref,
    tag_ref,
    pix_ref,
    ship_ref,
    ship2_ref,
    sel_ref,
    wide_ref,
    out_ref,
    amp_ref,
    acc_ref,
    proj_ref,
    lit_ref,
    rows_ref,
):
    n_sky, half, chunk, extra = sizes
    bands, stamps, pix = pix_ref.shape
    size_k = amp_ref.shape[0]
    top = stamps + 2 * size_k
    pix2_ref = ship2_ref.at[:, 0:stamps, :]
    tpl_ref, tpl2_ref = [r.at[:, stamps:top, :] for r in (ship_ref, ship2_ref)]
    pair_ref, pair2_ref = [r.at[:, top:, :] for r in (ship_ref, ship2_ref)]
    seen = [ref.at[b] for ref in (pix_ref, pix2_ref) for b in range(bands)]
    tpl = [ref.at[b] for ref in (tpl_ref, tpl2_ref) for b in range(bands)]
    pair = [ref.at[b] for ref in (pair_ref, pair2_ref) for b in range(bands)]
    steps = [
        (b, slice(c * chunk, (c + 1) * chunk))
        for b in range(2 * bands)
        for c in range(pix // chunk)
    ]
    lane = iota((8, LANES), 1)
    for i in range(n_sky // 2):
        span = slice(i * LANES, (i + 1) * LANES)
        amp_ref[0:8, span] = jnp.exp(unfold(theta_ref, slice(None), lane, i, True))
        amp_ref[8:16, span] = jnp.exp(unfold(theta_ref, slice(None), lane, i, False))
    parts = jnp.concatenate(split3(amp_ref[...]), axis=0)
    got = dot(parts, hot_ref[...])
    mix = dot(parts, blend_ref[...])
    k1, k2, k3 = slice(0, size_k), slice(size_k, 2 * size_k), slice(2 * size_k, 3 * size_k)
    slot_f = got[k1] + (got[k2] + got[k3])
    high, low = mix[:, :stamps], mix[:, stamps:]
    slot_u = high[k1] + (high[k2] + low[k1] + (high[k3] + low[k2]))
    scaled = gain_ref[0:1, :] * slot_f
    lit_ref[...] = jnp.concatenate([scaled, slot_u], axis=0).T.astype(bf16)
    acc_ref[...] = jnp.zeros_like(acc_ref)
    proj_ref[...] = jnp.zeros_like(proj_ref)
    lit = lit_ref[...]
    base = jnp.concatenate([base_ref[...]] * (chunk // LANES), axis=1)
    wide = pair_ref.shape[1]

    def model(b, px):
        return dot(lit, tpl[b][:, px])

    def weigh(b, px, light):
        resid = seen[b][:, px].astype(f32) - light
        under = base + (resid * resid) * (1.0 / ROBUST)
        guess = pltpu.reciprocal(under, approx=True)
        weight = guess * (2.0 - under * guess)
        return weight.astype(bf16), (weight * resid).astype(bf16)

    def gather(b, px, weight, wres):
        acc_ref[:, 0:wide] += dot(weight, pair[b][:, px], NT)
        proj_ref[...] += dot(tpl[b][0:size_k, px], wres, NT)

    light = model(*steps[0])
    held = None
    for i, here in enumerate(steps):
        ahead = model(*steps[i + 1]) if i + 1 < len(steps) else None
        now = weigh(*here, light)
        if held is not None:
            gather(*steps[i - 1], *held)
        light, held = ahead, now
    gather(*steps[-1], *held)

    scales = dot(jnp.concatenate(split3(scaled), axis=0), wide_ref[...], TN)
    col = iota((1, 2 * LANES), 1) - (LANES + extra)
    is_grad = jnp.where((col >= 0) & (col < size_k), 1.0, 0.0)
    factor = scales[:, : 2 * LANES] * (scales[:, 2 * LANES :] + is_grad)
    proj = jnp.concatenate([jnp.zeros((extra, stamps), f32), proj_ref[...]], axis=0)
    proj = jnp.concatenate([proj, jnp.zeros((LANES - extra - size_k, stamps), f32)], axis=0)
    tail = acc_ref[:, LANES:] + proj.T
    terms = jnp.concatenate(
        [
            factor[:, :LANES] * acc_ref[:, :LANES],
            factor[:, LANES:] * tail + tag_ref[...],
        ],
        axis=1,
    )
    sel = sel_ref[...]
    t1, t2, t3 = split3(terms)
    rows_ref[...] = dot(sel, t1) + (dot(sel, t2) + dot(sel, t3))
    groups = half // SUB
    for d in range(n_sky):
        at = d * half
        for g in range(groups):
            line = rows_ref[at + g * SUB : at + (g + 1) * SUB, :]
            out_ref[d, :, g * LANES : (g + 1) * LANES] = line[:, :LANES]
            more = pltpu.roll(line[:, LANES:], g * GROUP, 1) if g else line[:, LANES:]
            tail = tail + more if g else more
        out_ref[d, :, groups * LANES :] = tail


def solve_kernel(
    sizes,
    recv_ref,
    other_ref,
    member_in_ref,
    full_ref,
    theta_ref,
    init_ref,
    pay_ref,
    new_ref,
    member_ref,
    rows_ref,
):
    n_sky, half, tag, learn = sizes
    size_k, obj_dev = theta_ref.shape
    total = 2 * n_sky * half
    groups = half // SUB
    group = iota((SUB, LANES), 1) // GROUP
    first = jnp.full((SUB, LANES), lax.axis_index("band")) == 0
    for d in range(n_sky):
        for g in range(groups + 1):
            span = slice(g * LANES, (g + 1) * LANES)
            mine, others = recv_ref[d, :, span], other_ref[d, :, span]
            pair = (jnp.where(first, mine, others), jnp.where(first, others, mine))
            for part, line in enumerate(pair):
                at = (part * n_sky + d) * half
                if g < groups:
                    rows_ref[at + g * SUB : at + (g + 1) * SUB, 0:LANES] = line
                else:
                    for h in range(groups):
                        rows_ref[at + h * SUB : at + (h + 1) * SUB, LANES:] = jnp.where(
                            group == h, line, 0.0
                        )
    p1, p2, p3 = split3(rows_ref[...])
    if learn:
        where_tag = jnp.where(column((8, 2 * LANES), LANES + tag), 1.0, 0.0).astype(bf16)
        ids = dot(where_tag, p1, NT) + (dot(where_tag, p2, NT) + dot(where_tag, p3, NT))
        hit = iota((obj_dev, total), 0) + 1 == ids[0:1, :].astype(jnp.int32)
        member_ref[...] = jnp.where(hit, 1.0, 0.0).astype(bf16)
        member = member_ref[...]
    else:
        member = member_in_ref[...]
    sums = dot(member, p1) + (dot(member, p2) + dot(member, p3))
    q1, q2, q3 = split3(sums)
    full = full_ref[...]
    wide = dot(full, q1, NT) + (dot(full, q2, NT) + dot(full, q3, NT))
    row = iota((size_k, obj_dev), 0)
    theta = theta_ref[...]
    target = wide[size_k * size_k :] - PRIOR * (theta - init_ref[...])
    matrix = []
    for k in range(size_k):
        line = wide[k * size_k : (k + 1) * size_k]
        matrix.append(jnp.where(row == k, line + (DAMPING * line + PRIOR), line))
    inverse = []
    for p in range(size_k):
        line = matrix[p]
        inv = 1.0 / line[p : p + 1]
        inverse.append(inv)
        if p + 1 < size_k:
            scaled = jnp.where(row > p, line * inv, 0.0)
            target = target - scaled * target[p : p + 1]
            for k in range(p + 1, size_k):
                matrix[k] = matrix[k] - scaled * line[k : k + 1]
    delta = jnp.zeros_like(target)
    for p in reversed(range(size_k)):
        value = target[p : p + 1] * inverse[p]
        delta = jnp.where(row == p, value, delta)
        if p:
            target = target - matrix[p] * value
    new = theta + STEP_LIMIT * jnp.tanh(delta / STEP_LIMIT)
    new_ref[...] = new
    if pay_ref is not None:
        half = size_k // 2
        folded = jnp.concatenate([new[:half], new[half:]], axis=1)
        for d in range(n_sky):
            pay_ref[d] = folded


def hbm(x):
    return pltpu.with_memory_space_constraint(x, pltpu.HBM)


def call(kernel, out_shape, scratch=(), spaces=None, flags=None):
    specs = {}
    if spaces:
        specs["in_specs"] = [
            pl.BlockSpec(memory_space=pltpu.HBM if s == "h" else pltpu.VMEM) for s in spaces
        ]
    return pl.pallas_call(
        kernel,
        out_shape=out_shape,
        scratch_shapes=list(scratch),
        compiler_params=pltpu.CompilerParams(vmem_limit_bytes=VMEM_LIMIT, flags=flags),
        **specs,
    )


def local(
    stamps,
    stamp_gain,
    stamp_invvar,
    stamp_dest,
    stamp_obj,
    phi_tpl,
    psi_tpl,
    theta_init,
    nb_id,
    nb_weight,
):
    n_sky = lax.axis_size("sky")
    n_band = lax.axis_size("band")
    stamp_dev, bands, pix = stamps.shape
    size_k, obj_dev = theta_init.shape
    nei = nb_id.shape[1]
    cap = 2 * stamp_dev // n_sky
    half = cap // 2
    core_dev = stamp_dev // 2
    total = n_sky * cap
    n_all = n_sky * obj_dev
    extra = size_k * (size_k + 1) // 2 - LANES
    wide = LANES + -(-extra // 16) * 16
    assert n_band == 2 and half % SUB == 0 and half // SUB <= LANES // GROUP
    assert 2 * obj_dev == LANES and size_k * size_k == 2 * LANES and extra + size_k < GROUP
    shape = jax.ShapeDtypeStruct
    chunk = max(c for c in range(LANES, 1024, LANES) if pix % c == 0)

    pixels = jnp.transpose(stamps, (1, 0, 2))
    payload, keep, ship, sel, spread, full, base, tag, gain, owner = call(
        functools.partial(ready_kernel, (n_sky, cap, obj_dev, extra, chunk)),
        (
            shape((n_sky, 16, LANES), f32),
            shape((bands, core_dev, pix), bf16),
            shape((bands, core_dev + 2 * size_k + wide, pix), bf16),
            shape((n_sky * half, core_dev), bf16),
            shape((3 * size_k, 4 * LANES), bf16),
            shape((size_k * size_k + size_k, 2 * LANES), bf16),
            shape((core_dev, LANES), f32),
            shape((core_dev, LANES), f32),
            shape((8, core_dev), f32),
            shape((8, core_dev), jnp.int32),
        ),
        [
            pltpu.VMEM((bands, stamp_dev, pix), bf16),
            pltpu.VMEM((1, stamp_dev), jnp.int32),
            pltpu.VMEM((1, stamp_dev), jnp.int32),
            pltpu.VMEM((stamp_dev,), bf16),
            pltpu.VMEM((stamp_dev,), bf16),
            pltpu.VMEM((size_k, obj_dev), f32),
            pltpu.VMEM((nei, obj_dev), jnp.int32),
            pltpu.VMEM((nei, obj_dev), f32),
            pltpu.SemaphoreType.DMA((10,)),
        ],
        "h" * 10,
    )(
        hbm(stamp_dest.T),
        hbm(stamp_obj[None, :]),
        hbm(stamp_gain),
        hbm(stamp_invvar),
        hbm(phi_tpl),
        hbm(psi_tpl),
        hbm(theta_init),
        hbm(nb_id.T),
        hbm(nb_weight.T),
        hbm(pixels),
    )
    swap = [(0, 1), (1, 0)]
    ship2 = lax.ppermute(ship, "band", swap)
    got = lax.all_to_all(payload, "sky", 0, 0, tiled=True)
    everyone, hot, blend = call(
        functools.partial(index_kernel, nei),
        (
            shape((n_sky, 8, LANES), f32),
            shape((n_all, core_dev), bf16),
            shape((n_all, 2 * core_dev), bf16),
        ),
        [pltpu.VMEM((16, n_all), f32)],
    )(got, owner)
    terms = call(
        functools.partial(terms_kernel, (n_sky, half, chunk, extra)),
        shape((n_sky, SUB, (half // SUB + 1) * LANES), f32),
        [
            pltpu.VMEM((size_k, n_all), f32),
            pltpu.VMEM((core_dev, 2 * LANES), f32),
            pltpu.VMEM((size_k, core_dev), f32),
            pltpu.VMEM((core_dev, 2 * size_k), bf16),
            pltpu.VMEM((n_sky * half, 2 * LANES), f32),
        ],
    )
    theta = theta_init
    member = None
    for sweep in range(ITERS):
        sent = terms(
            everyone,
            hot,
            blend,
            gain,
            base,
            tag,
            keep,
            ship,
            ship2,
            sel,
            spread,
        )
        recv = lax.all_to_all(sent, "sky", 0, 0, tiled=True)
        other = lax.ppermute(recv, "band", swap)
        learn, last = sweep == 0, sweep + 1 == ITERS
        sizes = (n_sky, half, extra + size_k, learn)

        def solve(*refs, learn=learn, last=last, sizes=sizes):
            refs = list(refs)
            if learn:
                refs.insert(2, None)
            if last:
                refs.insert(6, None)
            if not learn:
                refs.insert(8, None)
            solve_kernel(sizes, *refs)

        outs = [shape((n_sky, 8, LANES), f32)] * (not last)
        outs += [shape((size_k, obj_dev), f32)]
        outs += [shape((obj_dev, total), bf16)] * learn
        given = [recv, other] + [member] * (not learn) + [full, theta, theta_init]
        outs = call(solve, outs, [pltpu.VMEM((total, 2 * LANES), f32)])(*given)
        theta = outs[0 if last else 1]
        if learn:
            member = outs[-1]
        if not last:
            everyone = lax.all_to_all(outs[0], "sky", 0, 0, tiled=True)
    return theta


def solution(mesh):
    in_specs = (
        P("sky", "band", None),
        P("sky"),
        P("sky"),
        P("sky", None),
        P("sky"),
        P("band", None, None),
        P("band", None, None),
        P(None, "sky"),
        P("sky", None),
        P("sky", None),
    )
    out_specs = P(None, "sky")
    return jax.shard_map(local, mesh=mesh, in_specs=in_specs, out_specs=out_specs, check_vma=False)
```
